32 devices in a mesh: dp: 2 (over core), row: 4 (over y, x), col: 4 (over z).
Axes of the slice: x: 2, y: 2, z: 4, core: 2. Of those that a mesh axis runs over, the one named last changes fastest.
Arguments:
- x_stream: bfloat16 [512, 16384], P('col', ('dp', 'row')), may hold values from -6 to 6
- y_stream: bfloat16 [512, 16384], P('col', ('dp', 'row')), may hold values from -6 to 6
- w_qkv: bfloat16 [512, 3, 512], P('col', None, 'row'), may hold values from -0.25 to 0.25
- w_out: bfloat16 [512, 512], P('row', 'col'), may hold values from -4 to 4
- gain_attn: bfloat16 [512], P('col'), may hold values from 0.25 to 1.75
- bias_attn: bfloat16 [512], P('col'), may hold values from -3 to 3
- w_up: bfloat16 [512, 2048], P('col', 'row'), may hold values from -0.25 to 0.25
- w_down: bfloat16 [2048, 512], P('row', 'col'), may hold values from -0.1875 to 0.1875
- gain_ffn: bfloat16 [512], P('col'), may hold values from 0.25 to 1.75
- bias_ffn: bfloat16 [512], P('col'), may hold values from -3 to 3
- teach_x: bfloat16 [512, 16384], P('col', ('dp', 'row')), may hold values from -6 to 6
- teach_y: bfloat16 [512, 16384], P('col', ('dp', 'row')), may hold values from -9 to 9
- lengths: int32 [8, 9], replicated, may hold values from 1 to 1024, as said below
Outputs:
- x_out: bfloat16 [512, 16384], P('col', ('dp', 'row'))
- y_out: bfloat16 [512, 16384], P('col', ('dp', 'row'))
- grad_x: float32 [512, 16384], P('col', ('dp', 'row'))
- grad_y: float32 [512, 16384], P('col', ('dp', 'row'))
- grad_w_qkv: float32 [512, 3, 512], P('col', None, 'row')
- grad_w_out: float32 [512, 512], P('row', 'col')
- grad_gain_attn: float32 [512], P('col')
- grad_bias_attn: float32 [512], P('col')
- grad_w_up: float32 [512, 2048], P('col', 'row')
- grad_w_down: float32 [2048, 512], P('row', 'col')
- grad_gain_ffn: float32 [512], P('col')
- grad_bias_ffn: float32 [512], P('col')
- loss: float32 [], replicated
The draws below stay inside these ranges and needn't reach their ends.
Inputs may be any that keep to these rules, and one draw needn't show every extreme that they name: Prompt lengths lie in 512 to 1024 and continuation lengths in 1 to 128; group 0 has a full prompt and a full first continuation.
All inputs are finite; a program needn't handle non-finite values.
Results may differ from the reference program's by a relative error of at most 0.01115.
Values may be sent and summed in bfloat16 or wider, within the bound.
A program may use at most 256 MiB of HBM per device.

```python
import jax
import jax.numpy as jnp
from jax import lax

D = 512
HEADS = 8
FF = 2048
HD = 64
PROMPT = 1024
CONT = 128
NCONT = 8
GROUP = 2048
GROUPS = 8
TOKENS = 16384


def draw_lengths(key, part):
    first_key, second_key = jax.random.split(jax.random.fold_in(key, 17))
    prompt_len = jax.random.randint(first_key, (GROUPS, 1), PROMPT // 2, PROMPT + 1)
    cont_len = jax.random.randint(second_key, (GROUPS, NCONT), 1, CONT + 1)
    table = jnp.concatenate([prompt_len, cont_len], axis=1).astype(jnp.int32)
    return table.at[0, 0].set(PROMPT).at[0, 1].set(CONT)


def levels(stream_key, dims, cuts, least, largest):
    gain, own = 1.0, jax.random.fold_in(stream_key, 6)
    for axis_at, shards_of in cuts:
        draws = jnp.exp(jax.random.uniform(jax.random.fold_in(own, axis_at), (shards_of,), jnp.float32, least / len(cuts), largest / len(cuts)))
        gain = gain * jnp.repeat(draws, dims[axis_at] // shards_of).reshape([-1 if axis == axis_at else 1 for axis in range(len(dims))])
    return gain


def gaussian(key, dims, width, reach, shards=(), held_as=jnp.bfloat16):
    entries = width * jax.random.normal(key, dims, jnp.float32)
    if shards:
        entries = entries * levels(key, dims, shards, -0.22, 0.18)
    return jnp.clip(entries, -reach, reach).astype(held_as)


def setup_inputs(seed: int = 0) -> dict:
    splits = jax.random.split(jax.random.key(seed), 14)
    x_stream = gaussian(splits[0], (D, TOKENS), 1.0, 6.0, ((0, 4), (1, 8)))
    y_stream = gaussian(splits[1], (D, TOKENS), 1.0, 6.0, ((0, 4), (1, 8)))
    w_qkv = gaussian(splits[2], (D, 3, D), D ** -0.5, 0.25, ((0, 4), (2, 4)))
    w_out = gaussian(splits[3], (D, D), (max(D // 256, 1)) ** -0.5, 4.0, ((0, 4), (1, 4)))
    gain_attn = jnp.clip(1.0 + 0.15 * jax.random.normal(splits[4], (D,), jnp.float32), 0.25, 1.75).astype(jnp.bfloat16)
    bias_attn = gaussian(splits[5], (D,), 0.5, 3.0, ((0, 4),))
    w_up = gaussian(splits[6], (D, FF), D ** -0.5, 0.25, ((0, 4), (1, 4)))
    w_down = gaussian(splits[7], (FF, D), (FF // 2) ** -0.5, 0.1875, ((0, 4), (1, 4)))
    gain_ffn = jnp.clip(1.0 + 0.15 * jax.random.normal(splits[8], (D,), jnp.float32), 0.25, 1.75).astype(jnp.bfloat16)
    bias_ffn = gaussian(splits[9], (D,), 0.5, 3.0, ((0, 4),))
    teach_x = gaussian(splits[10], (D, TOKENS), 1.0, 6.0, ((0, 4), (1, 8)))
    teach_y = gaussian(splits[11], (D, TOKENS), 1.5, 9.0, ((0, 4), (1, 8)))
    lengths = draw_lengths(jax.random.fold_in(splits[13], 71), 0)
    return dict(x_stream=x_stream, y_stream=y_stream, w_qkv=w_qkv, w_out=w_out, gain_attn=gain_attn, bias_attn=bias_attn, w_up=w_up, w_down=w_down, gain_ffn=gain_ffn, bias_ffn=bias_ffn, teach_x=teach_x, teach_y=teach_y, lengths=lengths)


@jax.custom_vjp
def low(v):
    return lax.optimization_barrier(v.astype(jnp.bfloat16)).astype(jnp.float32)

@jax.custom_vjp
def low_back(v):
    return v

def low_keep(v):
    return (low(v), None)

def low_pass(kept, grad):
    return (grad,)

def back_keep(v):
    return (v, None)

def back_low(kept, grad):
    return (low(grad),)
low.defvjp(low_keep, low_pass)
low_back.defvjp(back_keep, back_low)
HIGHEST = lax.Precision.HIGHEST
NEG_FILL = -1000000000.0
EPS_NORM = 1e-05

def slot_mask(lengths):
    prompt_pos = jnp.arange(PROMPT, dtype=jnp.int32)
    cont_pos = jnp.arange(CONT, dtype=jnp.int32)
    prompt_live = prompt_pos[None, :] < lengths[:, 0:1]
    cont_live = cont_pos[None, None, :] < lengths[:, 1:, None]
    merged = jnp.concatenate([prompt_live, cont_live.reshape(lengths.shape[0], NCONT * CONT)], axis=1)
    return merged.astype(jnp.float32)

def pair_masks(group_len):
    prompt_pos = jnp.arange(PROMPT, dtype=jnp.int32)
    cont_pos = jnp.arange(CONT, dtype=jnp.int32)
    key_live = prompt_pos < group_len[0]
    prompt_pairs = (prompt_pos[None, :] <= prompt_pos[:, None]) & key_live[None, :]
    cont_pairs = (cont_pos[None, None, :] <= cont_pos[None, :, None]) & (cont_pos[None, None, :] < group_len[1:, None, None])
    return (key_live, prompt_pairs, cont_pairs)

def attend_group(inputs):
    query_rows, key_rows, val_rows, group_len = inputs
    factor = HD ** (-0.5)
    key_live, prompt_pairs, cont_pairs = pair_masks(group_len)
    query_p, key_p, val_p = (query_rows[:PROMPT], key_rows[:PROMPT], val_rows[:PROMPT])
    query_c = query_rows[PROMPT:].reshape(NCONT, CONT, HEADS, HD)
    key_c = key_rows[PROMPT:].reshape(NCONT, CONT, HEADS, HD)
    val_c = val_rows[PROMPT:].reshape(NCONT, CONT, HEADS, HD)
    score_pp = low_back(jnp.einsum('qhd,khd->hqk', query_p, key_p, precision=HIGHEST) * factor)
    score_cp = low_back(jnp.einsum('nthd,khd->hntk', query_c, key_p, precision=HIGHEST) * factor)
    score_cc = low_back(jnp.einsum('nthd,nuhd->hntu', query_c, key_c, precision=HIGHEST) * factor)
    score_pp = jnp.where(prompt_pairs[None], score_pp, NEG_FILL)
    score_cp = jnp.where(key_live[None, None, None, :], score_cp, NEG_FILL)
    score_cc = jnp.where(cont_pairs[None], score_cc, NEG_FILL)
    top_p = lax.optimization_barrier(jnp.max(score_pp, axis=-1, keepdims=True))
    exp_pp = jnp.exp(score_pp - top_p)
    prob_pp = low(exp_pp / lax.optimization_barrier(jnp.sum(exp_pp, axis=-1, keepdims=True)))
    top_c = jnp.maximum(lax.optimization_barrier(jnp.max(score_cp, axis=-1, keepdims=True)), lax.optimization_barrier(jnp.max(score_cc, axis=-1, keepdims=True)))
    exp_cp = jnp.exp(score_cp - top_c)
    exp_cc = jnp.exp(score_cc - top_c)
    total_c = lax.optimization_barrier(jnp.sum(exp_cp, axis=-1, keepdims=True)) + lax.optimization_barrier(jnp.sum(exp_cc, axis=-1, keepdims=True))
    prob_cp = low(exp_cp / total_c)
    prob_cc = low(exp_cc / total_c)
    out_p = jnp.einsum('hqk,khd->qhd', prob_pp, val_p, precision=HIGHEST)
    out_c = jnp.einsum('hntk,khd->nthd', prob_cp, val_p, precision=HIGHEST) + jnp.einsum('hntu,nuhd->nthd', prob_cc, val_c, precision=HIGHEST)
    return jnp.concatenate([out_p, out_c.reshape(NCONT * CONT, HEADS, HD)], axis=0)

def layer_norm(summed, gain_vec, bias_vec):
    average = lax.optimization_barrier(jnp.mean(summed, axis=-1, keepdims=True))
    squares = lax.optimization_barrier(jnp.mean(summed * summed, axis=-1, keepdims=True))
    return (summed - average) * lax.rsqrt(squares - average * average + EPS_NORM) * gain_vec + bias_vec

def forward(x_major, y_major, w_qkv, w_out, gain_attn, bias_attn, w_up, w_down, gain_ffn, bias_ffn, target_x, target_y, lengths):
    x_stream = x_major.T
    y_stream = y_major.T
    tokens_all = x_stream.shape[0]
    groups_all = tokens_all // GROUP
    projected = jnp.einsum('td,dke->tke', x_stream, w_qkv, precision=HIGHEST)
    projected = low_back(low(projected)).reshape(groups_all, GROUP, 3, HEADS, HD)
    attended = lax.map(jax.checkpoint(attend_group), (projected[:, :, 0], projected[:, :, 1], projected[:, :, 2], lengths))
    attended = low_back(low(attended.reshape(tokens_all, D)))
    branch_a = low_back(jnp.dot(attended, w_out, precision=HIGHEST))
    x_one = layer_norm(x_stream + branch_a, gain_attn, bias_attn)
    y_one = y_stream + branch_a
    pre_act = low_back(jnp.dot(low(x_one), w_up, precision=HIGHEST))
    hidden = low(jnp.maximum(pre_act, 0.0))
    branch_f = low_back(jnp.dot(hidden, w_down, precision=HIGHEST))
    x_two = layer_norm(x_one + branch_f, gain_ffn, bias_ffn)
    y_two = y_one + branch_f
    live_rows = slot_mask(lengths).reshape(tokens_all, 1)
    count_all = jnp.sum(lengths).astype(jnp.float32)
    diff_x = x_two - target_x
    diff_y = y_two - target_y
    loss_value = jnp.sum(live_rows * (diff_x * diff_x + diff_y * diff_y)) / (2.0 * count_all * D)
    return (x_two.T, y_two.T, loss_value)

def reference(x_stream, y_stream, w_qkv, w_out, gain_attn, bias_attn, w_up, w_down, gain_ffn, bias_ffn, teach_x, teach_y, lengths):
    params = tuple((array_in.astype(jnp.float32) for array_in in (x_stream, y_stream, w_qkv, w_out, gain_attn, bias_attn, w_up, w_down, gain_ffn, bias_ffn)))
    target_x = teach_x.astype(jnp.float32).T
    target_y = teach_y.astype(jnp.float32).T

    def run_layer(*values):
        return forward(*values, target_x, target_y, lengths)
    (x_two, y_two, loss_value), pullback = jax.vjp(run_layer, *params)
    seed_loss = jnp.ones_like(loss_value) * (x_two.shape[1] * D)
    gradients = pullback((jnp.zeros_like(x_two), jnp.zeros_like(y_two), seed_loss))
    return (x_two.astype(jnp.bfloat16), y_two.astype(jnp.bfloat16), gradients[0], gradients[1], gradients[2], gradients[3], gradients[4], gradients[5], gradients[6], gradients[7], gradients[8], gradients[9], loss_value)
```

```python
import functools

import jax
import jax.numpy as jnp
from jax import lax
from jax.experimental import pallas as pl
from jax.experimental.pallas import tpu as pltpu
from jax.sharding import PartitionSpec as P

HD = 64
PROMPT = 1024
CONT = 128
NCONT = 8
GROUP = 2048
BLOCK = 128

EPS_NORM = 1e-05
NEG_FILL = -1000000000.0
MESH = pl.DeviceIdType.MESH
F32 = jnp.float32
BF16 = jnp.bfloat16


def flip_low(r):
    return r + 1 - 2 * (r % 2)


def flip_high(r):
    return (r + 2) % 4


class Places:
    def __init__(self, ncol):
        self.dp = lax.axis_index("dp")
        self.row = lax.axis_index("row")
        self.col = lax.axis_index("col")
        self.ncol = ncol
        low, high = flip_low(self.row), flip_high(self.row)
        self.first = low * (1 - self.dp) + high * self.dp
        self.second = high * (1 - self.dp) + low * self.dp
        self.both = 3 - self.row
        self.sibling = (1 - self.dp, self.row, self.col)
        self.first_dev = (self.dp, self.first, self.col)
        self.second_dev = (self.dp, self.second, self.col)

    def ahead(self, k):
        return (self.col + k) % self.ncol

    def behind(self, k):
        return (self.col + self.ncol - k) % self.ncol

    def col_dev(self, c):
        return (self.dp, self.row, c)

    def meet(self):
        barrier = pltpu.get_barrier_semaphore()
        partners = [self.sibling, self.first_dev, self.second_dev]
        partners += [self.col_dev(self.ahead(k)) for k in range(1, self.ncol)]
        for partner in partners:
            pl.semaphore_signal(barrier, inc=1, device_id=partner, device_id_type=MESH)
        pl.semaphore_wait(barrier, len(partners))


def remote(src, dst, send_sem, recv_sem, device):
    return pltpu.make_async_remote_copy(
        src_ref=src,
        dst_ref=dst,
        send_sem=send_sem,
        recv_sem=recv_sem,
        device_id=device,
        device_id_type=MESH,
    )


def gather_kernel(
    ncol, parts, x_ref, td_ref, w_ref, xp_ref, xc_ref, tdo_ref, g_ref,
    act_send, act_recv, col_send, col_recv, one_send, one_recv, two_send, two_recv,
    sib_send, sib_recv, local_sem,
):
    at = Places(ncol)
    feat = x_ref.shape[0]
    half = feat // 2
    own_tokens = tdo_ref.shape[2]
    own_cont = xc_ref.shape[1]

    def rows_of(c):
        return pl.ds(pl.multiple_of(c * feat, feat), feat)

    def half_rows(c, core):
        return pl.ds(pl.multiple_of(c * feat + core * half, half), half)

    def prompt_cols(c):
        return pl.ds(pl.multiple_of(c // parts * GROUP, GROUP), PROMPT)

    def cont_cols(c):
        return pl.ds(
            pl.multiple_of(c // parts * GROUP + PROMPT + c % parts * own_cont, own_cont), own_cont
        )

    def own_cols(c):
        return pl.ds(pl.multiple_of(c * own_tokens, own_tokens), own_tokens)

    at.meet()
    my_half = w_ref.at[pl.ds(pl.multiple_of(at.dp * half, half), half)]
    pending = []

    def start(copy):
        copy.start()
        pending.append(copy)
        return copy

    mine = rows_of(at.col)
    for i, (src, dst) in enumerate(
        (
            (x_ref.at[:, prompt_cols(at.col)], xp_ref.at[mine]),
            (x_ref.at[:, cont_cols(at.col)], xc_ref.at[mine]),
            (td_ref.at[:, :, own_cols(at.col)], tdo_ref.at[:, mine]),
            (w_ref, g_ref.at[at.row, mine]),
        )
    ):
        pltpu.make_async_copy(src, dst, local_sem.at[i]).start()

    for k in range(1, ncol):
        start(
            remote(
                my_half,
                g_ref.at[at.row, half_rows(at.col, at.dp)],
                col_send.at[k],
                col_recv.at[k],
                at.col_dev(at.ahead(k)),
            )
        )
    for k in range(1, ncol):
        to = at.ahead(k)
        dev = at.col_dev(to)
        start(
            remote(
                x_ref.at[:, prompt_cols(to)], xp_ref.at[mine],
                act_send.at[0, k], act_recv.at[0, k], dev,
            )
        )
        start(
            remote(
                x_ref.at[:, cont_cols(to)], xc_ref.at[mine],
                act_send.at[1, k], act_recv.at[1, k], dev,
            )
        )
    for k in range(1, ncol):
        to = at.ahead(k)
        start(
            remote(
                td_ref.at[:, :, own_cols(to)], tdo_ref.at[:, mine],
                act_send.at[2, k], act_recv.at[2, k], at.col_dev(to),
            )
        )

    def piece(row, k, core):
        return g_ref.at[row, half_rows(at.behind(k), core)]

    def landed(dst, recv_sem):
        remote(dst, dst, recv_sem, recv_sem, at.sibling).wait_recv()

    def chunk(k):
        return my_half if k == 0 else piece(at.row, k, at.dp)

    for k in range(ncol):
        if k:
            landed(piece(at.row, k, at.dp), col_recv.at[k])
        start(remote(chunk(k), piece(at.row, k, at.dp), one_send.at[k], one_recv.at[k], at.first_dev))
        start(
            remote(chunk(k), piece(at.row, k, at.dp), two_send.at[0, k], two_recv.at[0, k], at.second_dev)
        )
        if k:
            start(
                remote(chunk(k), piece(at.row, k, at.dp), sib_send.at[0, k], sib_recv.at[0, k], at.sibling)
            )
    for k in range(ncol):
        got = piece(at.first, k, at.dp)
        landed(got, one_recv.at[k])
        start(remote(got, got, two_send.at[1, k], two_recv.at[1, k], at.second_dev))
        start(remote(got, got, sib_send.at[1, k], sib_recv.at[1, k], at.sibling))
    for k in range(ncol):
        for i, row in ((0, at.second), (1, at.both)):
            got = piece(row, k, at.dp)
            landed(got, two_recv.at[i, k])
            start(remote(got, got, sib_send.at[2 + i, k], sib_recv.at[2 + i, k], at.sibling))

    for k in range(1, ncol):
        frm = rows_of(at.behind(k))
        landed(xp_ref.at[frm], act_recv.at[0, k])
        landed(xc_ref.at[frm], act_recv.at[1, k])
        landed(tdo_ref.at[:, frm], act_recv.at[2, k])
    other = 1 - at.dp
    for k in range(ncol):
        if k:
            landed(piece(at.row, k, other), sib_recv.at[0, k])
        landed(piece(at.second, k, other), sib_recv.at[1, k])
        landed(piece(at.first, k, other), sib_recv.at[2, k])
        landed(piece(at.both, k, other), sib_recv.at[3, k])
    for copy in pending:
        copy.wait_send()
    for i, (src, dst) in enumerate(
        (
            (x_ref.at[:, prompt_cols(at.col)], xp_ref.at[mine]),
            (x_ref.at[:, cont_cols(at.col)], xc_ref.at[mine]),
            (td_ref.at[:, :, own_cols(at.col)], tdo_ref.at[:, mine]),
            (w_ref, g_ref.at[at.row, mine]),
        )
    ):
        pltpu.make_async_copy(src, dst, local_sem.at[i]).wait()


def gather_all(x_stream, teach_dy, packed, ncol, nrow, parts):
    feat = x_stream.shape[0]
    full = feat * ncol
    own_tokens = GROUP // parts
    own_cont = NCONT * CONT // parts
    dma = pltpu.SemaphoreType.DMA
    anywhere = pl.BlockSpec(memory_space=pl.ANY)
    return pl.pallas_call(
        functools.partial(gather_kernel, ncol, parts),
        out_shape=(
            jax.ShapeDtypeStruct((full, PROMPT), BF16),
            jax.ShapeDtypeStruct((full, own_cont), BF16),
            jax.ShapeDtypeStruct((2, full, own_tokens), BF16),
            jax.ShapeDtypeStruct((nrow, full, packed.shape[1]), BF16),
        ),
        in_specs=[anywhere] * 3,
        out_specs=[anywhere] * 4,
        scratch_shapes=[
            dma((3, ncol)), dma((3, ncol)), dma((ncol,)), dma((ncol,)), dma((ncol,)), dma((ncol,)),
            dma((2, ncol)), dma((2, ncol)), dma((4, ncol)), dma((4, ncol)), dma((4,)),
        ],
        compiler_params=pltpu.CompilerParams(collective_id=0, has_side_effects=True),
        name="gather_all",
    )(x_stream, teach_dy, packed)


def scatter_kernel(
    ncol, parts, xb_ref, gp_ref, gc_ref, gw_ref, sm_ref,
    xbo_ref, gpo_ref, gco_ref, gwo_ref, smo_ref,
    sib_buf, two_buf, one_buf, col_buf, sm_buf, smc_buf,
    act_send, act_recv, sib_send, sib_recv, two_send, two_recv, one_send, one_recv,
    col_send, col_recv, fin_send, fin_recv, sm_send, sm_recv, smc_send, smc_recv, local_sem,
):
    at = Places(ncol)
    feat = xbo_ref.shape[1]
    half = feat // 2
    own_tokens = xb_ref.shape[2]
    own_cont = gc_ref.shape[1]
    part = at.col % parts

    def rows_of(c):
        return pl.ds(pl.multiple_of(c * feat, feat), feat)

    def half_rows(c, core):
        return pl.ds(pl.multiple_of(c * feat + core * half, half), half)

    def prompt_cols(c):
        return pl.ds(pl.multiple_of(c // parts * PROMPT, PROMPT), PROMPT)

    def cont_cols(c):
        return pl.ds(pl.multiple_of(c * own_cont, own_cont), own_cont)

    def own_cols(c):
        return pl.ds(pl.multiple_of(c * own_tokens, own_tokens), own_tokens)

    at.meet()
    pending = []

    def start(copy):
        copy.start()
        pending.append(copy)
        return copy

    def landed(dst, recv_sem):
        remote(dst, dst, recv_sem, recv_sem, at.sibling).wait_recv()

    other = 1 - at.dp
    order = list(range(1, ncol)) + [0]
    for k in order:
        start(
            remote(
                gw_ref.at[:, half_rows(at.ahead(k), other)], sib_buf.at[k],
                sib_send.at[k], sib_recv.at[k], at.sibling,
            )
        )
    start(remote(sm_ref, sm_buf.at[0], sm_send.at[0], sm_recv.at[0], at.sibling))

    def local_copies():
        mine = rows_of(at.col)
        return [
            pltpu.make_async_copy(src, dst, local_sem.at[i])
            for i, (src, dst) in enumerate(
                (
                    (xb_ref.at[:, mine], xbo_ref.at[:, :, own_cols(at.col)]),
                    (gp_ref.at[mine], gpo_ref.at[part, :, prompt_cols(at.col)]),
                    (gc_ref.at[mine], gco_ref.at[:, cont_cols(at.col)]),
                )
            )
        ]

    for copy in local_copies():
        copy.start()
    for k in range(1, ncol):
        to = at.ahead(k)
        dev = at.col_dev(to)
        start(
            remote(
                xb_ref.at[:, rows_of(to)], xbo_ref.at[:, :, own_cols(at.col)],
                act_send.at[0, k], act_recv.at[0, k], dev,
            )
        )
        start(
            remote(
                gp_ref.at[rows_of(to)], gpo_ref.at[part, :, prompt_cols(at.col)],
                act_send.at[1, k], act_recv.at[1, k], dev,
            )
        )
        start(
            remote(
                gc_ref.at[rows_of(to)], gco_ref.at[:, cont_cols(at.col)],
                act_send.at[2, k], act_recv.at[2, k], dev,
            )
        )

    for k in order:
        landed(sib_buf.at[k], sib_recv.at[k])
        for row in range(gw_ref.shape[0]):
            here = gw_ref.at[row, half_rows(at.ahead(k), at.dp)]
            sib_buf[k, row] = (here[...].astype(F32) + sib_buf[k, row].astype(F32)).astype(BF16)
        for i, row in ((0, at.second), (1, at.both)):
            start(
                remote(
                    sib_buf.at[k, row], two_buf.at[i, k],
                    two_send.at[i, k], two_recv.at[i, k], at.second_dev,
                )
            )
    landed(sm_buf.at[0], sm_recv.at[0])
    sm_buf[3] = sm_ref[...] + sm_buf[0]
    start(remote(sm_buf.at[3], sm_buf.at[1], sm_send.at[1], sm_recv.at[1], at.second_dev))
    for k in order:
        landed(two_buf.at[1, k], two_recv.at[1, k])
        two_buf[1, k] = (sib_buf[k, at.first].astype(F32) + two_buf[1, k].astype(F32)).astype(BF16)
        start(
            remote(
                two_buf.at[1, k], one_buf.at[k], one_send.at[k], one_recv.at[k], at.first_dev
            )
        )
    landed(sm_buf.at[1], sm_recv.at[1])
    sm_buf[4] = sm_buf[3] + sm_buf[1]
    start(remote(sm_buf.at[4], sm_buf.at[2], sm_send.at[2], sm_recv.at[2], at.first_dev))
    for k in order:
        landed(two_buf.at[0, k], two_recv.at[0, k])
        landed(one_buf.at[k], one_recv.at[k])
        total = sib_buf[k, at.row].astype(F32) + two_buf[0, k].astype(F32) + one_buf[k].astype(F32)
        if k:
            two_buf[0, k] = total.astype(BF16)
            start(
                remote(
                    two_buf.at[0, k], col_buf.at[k],
                    col_send.at[k], col_recv.at[k], at.col_dev(at.ahead(k)),
                )
            )
        else:
            own_total = total
    landed(sm_buf.at[2], sm_recv.at[2])
    sm_buf[5] = sm_buf[4] + sm_buf[2]
    for k in range(1, ncol):
        to = at.ahead(k)
        start(
            remote(
                sm_buf.at[5, to], smc_buf.at[k], smc_send.at[k], smc_recv.at[k], at.col_dev(to)
            )
        )
    for k in range(1, ncol):
        landed(col_buf.at[k], col_recv.at[k])
        own_total = own_total + col_buf[k].astype(F32)
    my_rows = pl.ds(pl.multiple_of(at.dp * half, half), half)
    gwo_ref[my_rows] = own_total
    start(remote(gwo_ref.at[my_rows], gwo_ref.at[my_rows], fin_send, fin_recv, at.sibling))
    small = sm_buf[5, at.col]
    for k in range(1, ncol):
        landed(smc_buf.at[k], smc_recv.at[k])
        small = small + smc_buf[k]
    smo_ref[...] = small
    landed(gwo_ref.at[pl.ds(pl.multiple_of(other * half, half), half)], fin_recv)
    for k in range(1, ncol):
        frm = at.behind(k)
        landed(xbo_ref.at[:, :, own_cols(frm)], act_recv.at[0, k])
        landed(gpo_ref.at[frm % parts, :, prompt_cols(frm)], act_recv.at[1, k])
        landed(gco_ref.at[:, cont_cols(frm)], act_recv.at[2, k])
    for copy in pending:
        copy.wait_send()
    for copy in local_copies():
        copy.wait()


def scatter_all(xb, gp, gc, gw, small, ncol, parts):
    nrow, full, width = gw.shape
    feat = full // ncol
    half = feat // 2
    groups = ncol // parts
    own_tokens, own_cont = xb.shape[2], gc.shape[1]
    dma = pltpu.SemaphoreType.DMA
    anywhere = pl.BlockSpec(memory_space=pl.ANY)
    vmem = pl.BlockSpec(memory_space=pltpu.VMEM)
    small_shape = small.shape
    return pl.pallas_call(
        functools.partial(scatter_kernel, ncol, parts),
        out_shape=(
            jax.ShapeDtypeStruct((2, feat, ncol * own_tokens), BF16),
            jax.ShapeDtypeStruct((parts, feat, groups * PROMPT), BF16),
            jax.ShapeDtypeStruct((feat, ncol * own_cont), BF16),
            jax.ShapeDtypeStruct((feat, width), F32),
            jax.ShapeDtypeStruct(small_shape[1:], F32),
        ),
        in_specs=[anywhere, anywhere, anywhere, vmem, vmem],
        out_specs=[anywhere, anywhere, anywhere, vmem, vmem],
        scratch_shapes=[
            pltpu.VMEM((ncol, nrow, half, width), BF16),
            pltpu.VMEM((2, ncol, half, width), BF16),
            pltpu.VMEM((ncol, half, width), BF16),
            pltpu.VMEM((ncol, half, width), BF16),
            pltpu.VMEM((6,) + small_shape, F32),
            pltpu.VMEM((ncol,) + small_shape[1:], F32),
            dma((3, ncol)), dma((3, ncol)), dma((ncol,)), dma((ncol,)), dma((2, ncol)), dma((2, ncol)),
            dma((ncol,)), dma((ncol,)), dma((ncol,)), dma((ncol,)), dma(()), dma(()),
            dma((3,)), dma((3,)), dma((ncol,)), dma((ncol,)), dma((3,)),
        ],
        compiler_params=pltpu.CompilerParams(
            collective_id=1, has_side_effects=True, vmem_limit_bytes=56 << 20
        ),
        name="scatter_all",
    )(xb, gp, gc, gw, small)


def to_parts(array_in, parts):
    lead = array_in.shape[:-1]
    groups = array_in.shape[-1] // GROUP
    split = array_in.reshape(lead + (groups, GROUP))
    prompt = split[..., :PROMPT].reshape(lead + (groups, 2, parts, BLOCK))
    prompt = jnp.stack([prompt[..., 0, :, :], prompt[..., 1, ::-1, :]], axis=-2)
    prompt = prompt.reshape(lead + (groups, parts, PROMPT // parts))
    cont = split[..., PROMPT:].reshape(lead + (groups, parts, NCONT * CONT // parts))
    return jnp.concatenate([prompt, cont], axis=-1).reshape(array_in.shape)


def from_parts(array_in, parts):
    lead = array_in.shape[:-1]
    groups = array_in.shape[-1] // GROUP
    split = array_in.reshape(lead + (groups, parts, GROUP // parts))
    prompt = split[..., : PROMPT // parts].reshape(lead + (groups, parts, 2, BLOCK))
    prompt = jnp.concatenate(
        [prompt[..., :, 0, :], prompt[..., ::-1, 1, :]], axis=-2
    ).reshape(lead + (groups, PROMPT))
    cont = split[..., PROMPT // parts :].reshape(lead + (groups, NCONT * CONT))
    return jnp.concatenate([prompt, cont], axis=-1).reshape(array_in.shape)


def norm_forward(summed, gain_vec, bias_vec):
    average = jnp.mean(summed, axis=0, keepdims=True)
    squares = jnp.mean(summed * summed, axis=0, keepdims=True)
    inv_scale = lax.rsqrt(squares - average * average + EPS_NORM)
    unit_val = (summed - average) * inv_scale
    return (unit_val * gain_vec + bias_vec, unit_val, inv_scale)


def norm_backward(upstream, unit_val, inv_scale, gain_vec):
    scaled = upstream * gain_vec
    first = jnp.mean(scaled, axis=0, keepdims=True)
    second = jnp.mean(scaled * unit_val, axis=0, keepdims=True)
    d_summed = inv_scale * (scaled - first - unit_val * second)
    return (d_summed, jnp.sum(upstream * unit_val, axis=1), jnp.sum(upstream, axis=1))


def dot_tn(lhs, rhs):
    return lax.dot_general(lhs, rhs, (((0,), (0,)), ((), ())), preferred_element_type=F32)


def dot_nn(lhs, rhs):
    return lax.dot_general(lhs, rhs, (((1,), (0,)), ((), ())), preferred_element_type=F32)


def dot_nt(lhs, rhs):
    return lax.dot_general(lhs, rhs, (((1,), (1,)), ((), ())), preferred_element_type=F32)


def body(
    x_stream, y_stream, w_qkv, w_out, gain_attn, bias_attn, w_up, w_down, gain_ffn, bias_ffn,
    teach_x, teach_y, lengths,
):
    ncol, nrow = lax.axis_size("col"), lax.axis_size("row")
    feat, tokens = x_stream.shape
    full = feat * ncol
    groups_here = tokens // GROUP
    parts = ncol // groups_here
    assert parts * 2 * BLOCK == PROMPT and nrow == 4
    heads = full // HD
    block = w_qkv.shape[2]
    ff_block = w_up.shape[1]
    col = lax.axis_index("col")
    part = col % parts
    own_cont = NCONT * CONT // parts
    conts = NCONT // parts
    own = GROUP // parts
    half_own = PROMPT // parts

    y_f32 = y_stream.astype(F32)
    dy = y_f32 - teach_y.astype(F32)
    teach_dy = to_parts(jnp.stack([teach_x, dy.astype(BF16)]), parts)
    packed = jnp.concatenate([w_qkv.reshape(feat, 3 * block), w_out.T, w_up, w_down.T], axis=1)
    small_vecs = jnp.stack([gain_attn, bias_attn, gain_ffn, bias_ffn])
    vecs = lax.all_gather(small_vecs, "col", axis=1, tiled=True).astype(F32)
    gain_a, bias_a, gain_f, bias_f = (vecs[i][:, None] for i in range(4))

    x_prompt, x_cont, tdo, weights = gather_all(x_stream, teach_dy, packed, ncol, nrow, parts)

    first = (lax.axis_index("dp") * nrow + lax.axis_index("row")) * groups_here
    lens = lax.dynamic_slice_in_dim(lengths, first + col // parts, 1, 0)[0]
    lens_cont = lax.dynamic_slice_in_dim(lens, 1 + part * conts, conts, 0)
    count_all = jnp.sum(lengths).astype(F32)
    total_tokens = lengths.shape[0] * GROUP

    def wide(first_col, width):
        return weights[:, :, first_col : first_col + width].transpose(1, 0, 2).reshape(full, -1)

    w_q, w_k, w_v = (wide(i * block, block) for i in range(3))
    w_o = wide(3 * block, block)
    w_u = wide(4 * block, ff_block)
    w_d = wide(4 * block + ff_block, ff_block)

    lo = lax.dynamic_slice_in_dim(x_prompt, part * BLOCK, BLOCK, 1)
    hi = lax.dynamic_slice_in_dim(x_prompt, (2 * parts - 1 - part) * BLOCK, BLOCK, 1)
    x_own = jnp.concatenate([lo, hi, x_cont], axis=1)
    x_keys = jnp.concatenate([x_prompt, x_cont], axis=1)
    query = dot_tn(w_q, x_own).astype(BF16).reshape(heads, HD, own)
    key = dot_tn(w_k, x_keys).astype(BF16).reshape(heads, HD, PROMPT + own_cont)
    val = dot_tn(w_v, x_keys).astype(BF16).reshape(heads, HD, PROMPT + own_cont)
    key_p, val_p = key[:, :, :PROMPT], val[:, :, :PROMPT]
    key_c = key[:, :, PROMPT:].reshape(heads, HD, conts, CONT)
    val_c = val[:, :, PROMPT:].reshape(heads, HD, conts, CONT)
    slots = jnp.arange(BLOCK, dtype=jnp.int32)
    positions = jnp.concatenate(
        [part * BLOCK + slots, (2 * parts - 1 - part) * BLOCK + slots, jnp.full((own_cont,), PROMPT)]
    )
    key_pos = jnp.arange(PROMPT, dtype=jnp.int32)
    allowed = (key_pos[None, :] <= positions[:, None]) & (key_pos < lens[0])[None, :]
    cont_pos = jnp.arange(CONT, dtype=jnp.int32)
    allowed_c = (cont_pos[None, None, :] <= cont_pos[None, :, None]) & (
        cont_pos[None, None, :] < lens_cont[:, None, None]
    )
    factor = HD ** (-0.5)
    score_p = jnp.einsum("hdq,hdk->hqk", query, key_p, preferred_element_type=F32) * factor
    query_c = query[:, :, half_own:].reshape(heads, HD, conts, CONT)
    score_c = jnp.einsum("hdnt,hdnu->hntu", query_c, key_c, preferred_element_type=F32) * factor
    score_p = jnp.where(allowed[None], score_p, NEG_FILL)
    score_c = jnp.where(allowed_c[None], score_c, NEG_FILL)

    def join(cont_rows):
        cont_rows = cont_rows.reshape(heads, own_cont)
        return jnp.concatenate([jnp.full((heads, half_own), NEG_FILL, F32), cont_rows], axis=1)

    def join_zero(cont_rows):
        cont_rows = cont_rows.reshape(heads, own_cont)
        return jnp.concatenate([jnp.zeros((heads, half_own), F32), cont_rows], axis=1)

    top = jnp.maximum(jnp.max(score_p, axis=-1), join(jnp.max(score_c, axis=-1)))
    top_c = top[:, half_own:].reshape(heads, conts, CONT)
    exp_p = jnp.exp(score_p - top[..., None])
    exp_c = jnp.exp(score_c - top_c[..., None])
    denom = jnp.sum(exp_p, axis=-1) + join_zero(jnp.sum(exp_c, axis=-1))
    denom_c = denom[:, half_own:].reshape(heads, conts, CONT)
    prob_p = exp_p / denom[..., None]
    prob_c = exp_c / denom_c[..., None]
    low_p, low_c = prob_p.astype(BF16), prob_c.astype(BF16)
    att_p = jnp.einsum("hdk,hqk->hdq", val_p, low_p, preferred_element_type=F32)
    att_c = jnp.einsum("hdnu,hntu->hdnt", val_c, low_c, preferred_element_type=F32)
    att_c = att_c.reshape(heads, HD, own_cont)
    attended = jnp.concatenate([att_p[:, :, :half_own], att_p[:, :, half_own:] + att_c], axis=2)
    attended = attended.astype(BF16).reshape(full, own)

    branch_a = dot_nn(w_o, attended)
    x_one, unit_a, inv_a = norm_forward(x_own.astype(F32) + branch_a, gain_a, bias_a)
    x_low = x_one.astype(BF16)
    pre_act = dot_tn(w_u, x_low)
    hidden = jnp.maximum(pre_act, 0.0).astype(BF16)
    branch_f = dot_nn(w_d, hidden)
    x_two, unit_f, inv_f = norm_forward(x_one + branch_f, gain_f, bias_f)
    branch_sum = branch_a + branch_f

    live_own = jnp.concatenate(
        [
            positions[:half_own] < lens[0],
            (cont_pos[None, :] < lens_cont[:, None]).reshape(own_cont),
        ]
    ).astype(F32)[None, :]
    diff_x = x_two - tdo[0].astype(F32)
    diff_y = branch_sum + tdo[1].astype(F32)
    loss_part = jnp.sum(live_own * (diff_x * diff_x + diff_y * diff_y))
    weight = live_own * (total_tokens / count_all)
    grad_two = diff_x * weight
    grad_y = diff_y * weight
    d_sum_f, gain_grad_f, bias_grad_f = norm_backward(grad_two, unit_f, inv_f, gain_f)
    d_branch_f = (d_sum_f + grad_y).astype(BF16)
    grad_down = dot_nt(d_branch_f, hidden)
    d_pre = jnp.where(pre_act > 0, dot_tn(w_d, d_branch_f), 0.0).astype(BF16)
    grad_up = dot_nt(x_low, d_pre)
    d_x_one = d_sum_f + dot_nn(w_u, d_pre)
    d_sum_a, gain_grad_a, bias_grad_a = norm_backward(d_x_one, unit_a, inv_a, gain_a)
    d_branch_a = (d_sum_a + grad_y).astype(BF16)
    grad_out = dot_nt(d_branch_a, attended)
    d_att = dot_tn(w_o, d_branch_a).astype(BF16).reshape(heads, HD, own)

    dprob_p = jnp.einsum("hdq,hdk->hqk", d_att, val_p, preferred_element_type=F32)
    d_att_c = d_att[:, :, half_own:].reshape(heads, HD, conts, CONT)
    dprob_c = jnp.einsum("hdnt,hdnu->hntu", d_att_c, val_c, preferred_element_type=F32)
    delta = jnp.sum(prob_p * dprob_p, axis=-1) + join_zero(jnp.sum(prob_c * dprob_c, axis=-1))
    delta_c = delta[:, half_own:].reshape(heads, conts, CONT)
    ds_p = (prob_p * (dprob_p - delta[..., None])).astype(BF16)
    ds_c = (prob_c * (dprob_c - delta_c[..., None])).astype(BF16)
    d_q = jnp.einsum("hqk,hdk->hdq", ds_p, key_p, preferred_element_type=F32)
    d_q_c = jnp.einsum("hntu,hdnu->hdnt", ds_c, key_c, preferred_element_type=F32)
    d_q_c = d_q_c.reshape(heads, HD, own_cont)
    d_q = jnp.concatenate([d_q[:, :, :half_own], d_q[:, :, half_own:] + d_q_c], axis=2)
    d_q = (d_q * factor).astype(BF16).reshape(full, own)
    d_k_p = jnp.einsum("hqk,hdq->hdk", ds_p, query, preferred_element_type=F32) * factor
    d_k_c = jnp.einsum("hntu,hdnt->hdnu", ds_c, query_c, preferred_element_type=F32) * factor
    d_v_p = jnp.einsum("hqk,hdq->hdk", low_p, d_att, preferred_element_type=F32)
    d_v_c = jnp.einsum("hntu,hdnt->hdnu", low_c, d_att_c, preferred_element_type=F32)
    d_k = jnp.concatenate([d_k_p, d_k_c.reshape(heads, HD, own_cont)], axis=2)
    d_v = jnp.concatenate([d_v_p, d_v_c.reshape(heads, HD, own_cont)], axis=2)
    d_k = d_k.astype(BF16).reshape(full, PROMPT + own_cont)
    d_v = d_v.astype(BF16).reshape(full, PROMPT + own_cont)

    grad_q = dot_nt(x_own, d_q)
    grad_k = dot_nt(x_keys, d_k)
    grad_v = dot_nt(x_keys, d_v)
    dx_keys = dot_nn(w_k, d_k) + dot_nn(w_v, d_v)
    dx_own = dot_nn(w_q, d_q) + d_sum_a
    dx_prompt = dx_keys[:, :PROMPT]
    for first_col, piece in (
        (part * BLOCK, dx_own[:, :BLOCK]),
        ((2 * parts - 1 - part) * BLOCK, dx_own[:, BLOCK:half_own]),
    ):
        now = lax.dynamic_slice_in_dim(dx_prompt, first_col, BLOCK, 1)
        dx_prompt = lax.dynamic_update_slice_in_dim(dx_prompt, now + piece, first_col, 1)
    dx_cont = dx_keys[:, PROMPT:] + dx_own[:, half_own:]

    def by_row(grad, width):
        return grad.reshape(full, nrow, width).transpose(1, 0, 2)

    grads = jnp.concatenate(
        [by_row(g, block) for g in (grad_q, grad_k, grad_v, grad_out)]
        + [by_row(grad_up, ff_block), by_row(grad_down, ff_block)],
        axis=2,
    ).astype(BF16)
    small = jnp.stack(
        [gain_grad_a, bias_grad_a, gain_grad_f, bias_grad_f, jnp.full((full,), loss_part)]
        + [jnp.zeros((full,), F32)] * 3
    )
    lanes = max(feat, 128)
    small = small.reshape(8, ncol, feat).transpose(1, 0, 2)
    small = jnp.pad(small, ((0, 0), (0, 0), (0, lanes - feat)))
    xb, gp, gc, gw, sums = scatter_all(
        jnp.stack([x_two.astype(BF16), branch_sum.astype(BF16)]),
        dx_prompt.astype(BF16), dx_cont.astype(BF16), grads, small, ncol, parts,
    )

    xb = from_parts(xb, parts)
    branch = xb[1].astype(F32)
    live_all = live_slots(
        lax.dynamic_slice_in_dim(lengths, first, groups_here, 0)
    ).reshape(1, tokens)
    y_out = (y_f32 + branch).astype(BF16)
    grad_y_out = (dy + branch) * (live_all * (total_tokens / count_all))
    gp = jnp.sum(gp.astype(F32), axis=0).reshape(feat, groups_here, PROMPT)
    gc = gc.astype(F32).reshape(feat, groups_here, NCONT * CONT)
    grad_x = jnp.concatenate([gp, gc], axis=2).reshape(feat, tokens)
    loss = sums[4, 0] / (2.0 * count_all * full)
    first_up = 4 * block
    return (
        xb[0],
        y_out,
        grad_x,
        grad_y_out,
        gw[:, : 3 * block].reshape(feat, 3, block),
        gw[:, 3 * block : 4 * block].T,
        sums[0, :feat],
        sums[1, :feat],
        gw[:, first_up : first_up + ff_block],
        gw[:, first_up + ff_block :].T,
        sums[2, :feat],
        sums[3, :feat],
        loss,
    )


def live_slots(lens):
    prompt = jnp.arange(PROMPT, dtype=jnp.int32)[None, :] < lens[:, 0:1]
    cont = jnp.arange(CONT, dtype=jnp.int32)[None, None, :] < lens[:, 1:, None]
    cont = cont.reshape(lens.shape[0], NCONT * CONT)
    return jnp.concatenate([prompt, cont], axis=1).astype(F32)


def solution(mesh):
    stream = P("col", ("dp", "row"))
    up, down = P("col", "row"), P("row", "col")
    qkv, vec = P("col", None, "row"), P("col")
    return jax.shard_map(
        body,
        mesh=mesh,
        in_specs=(
            stream, stream, qkv, down, vec, vec, up, down, vec, vec, stream, stream, P(),
        ),
        out_specs=(
            stream, stream, stream, stream, qkv, down, vec, vec, up, down, vec, vec, P(),
        ),
        check_vma=False,
    )
```

```python
import functools

import jax
import jax.numpy as jnp
from jax import lax
from jax.experimental import pallas as pl
from jax.experimental.pallas import tpu as pltpu
from jax.sharding import PartitionSpec as P

HD = 64
PROMPT = 1024
CONT = 128
NCONT = 8
GROUP = 2048
BLOCK = 128

EPS_NORM = 1e-05
NEG_FILL = -1000000000.0
MESH = pl.DeviceIdType.MESH
F32 = jnp.float32
BF16 = jnp.bfloat16


def flip_low(r):
    return r + 1 - 2 * (r % 2)


def flip_high(r):
    return (r + 2) % 4


class Places:
    def __init__(self, ncol):
        self.dp = lax.axis_index("dp")
        self.row = lax.axis_index("row")
        self.col = lax.axis_index("col")
        self.ncol = ncol
        low, high = flip_low(self.row), flip_high(self.row)
        self.first = low * (1 - self.dp) + high * self.dp
        self.second = high * (1 - self.dp) + low * self.dp
        self.both = 3 - self.row
        self.sibling = (1 - self.dp, self.row, self.col)
        self.first_dev = (self.dp, self.first, self.col)
        self.second_dev = (self.dp, self.second, self.col)

    def ahead(self, k):
        return (self.col + k) % self.ncol

    def behind(self, k):
        return (self.col + self.ncol - k) % self.ncol

    def col_dev(self, c):
        return (self.dp, self.row, c)

    def meet(self):
        barrier = pltpu.get_barrier_semaphore()
        partners = [self.sibling, self.first_dev, self.second_dev]
        partners += [self.col_dev(self.ahead(k)) for k in range(1, self.ncol)]
        for partner in partners:
            pl.semaphore_signal(barrier, inc=1, device_id=partner, device_id_type=MESH)
        pl.semaphore_wait(barrier, len(partners))


def remote(src, dst, send_sem, recv_sem, device):
    return pltpu.make_async_remote_copy(
        src_ref=src,
        dst_ref=dst,
        send_sem=send_sem,
        recv_sem=recv_sem,
        device_id=device,
        device_id_type=MESH,
    )


def gather_kernel(
    ncol, parts, x_ref, td_ref, w_ref, xp_ref, xc_ref, tdo_ref, g_ref,
    act_send, act_recv, col_send, col_recv, one_send, one_recv, two_send, two_recv,
    sib_send, sib_recv, local_sem,
):
    at = Places(ncol)
    feat = x_ref.shape[0]
    half = feat // 2
    own_tokens = tdo_ref.shape[2]
    own_cont = xc_ref.shape[1]

    def rows_of(c):
        return pl.ds(pl.multiple_of(c * feat, feat), feat)

    def half_rows(c, core):
        return pl.ds(pl.multiple_of(c * feat + core * half, half), half)

    def prompt_cols(c):
        return pl.ds(pl.multiple_of(c // parts * GROUP, GROUP), PROMPT)

    def cont_cols(c):
        return pl.ds(
            pl.multiple_of(c // parts * GROUP + PROMPT + c % parts * own_cont, own_cont), own_cont
        )

    def own_cols(c):
        return pl.ds(pl.multiple_of(c * own_tokens, own_tokens), own_tokens)

    at.meet()
    my_half = w_ref.at[pl.ds(pl.multiple_of(at.dp * half, half), half)]
    pending = []

    def start(copy):
        copy.start()
        pending.append(copy)
        return copy

    mine = rows_of(at.col)
    for i, (src, dst) in enumerate(
        (
            (x_ref.at[:, prompt_cols(at.col)], xp_ref.at[mine]),
            (x_ref.at[:, cont_cols(at.col)], xc_ref.at[mine]),
            (td_ref.at[:, :, own_cols(at.col)], tdo_ref.at[:, mine]),
            (w_ref, g_ref.at[at.row, mine]),
        )
    ):
        pltpu.make_async_copy(src, dst, local_sem.at[i]).start()

    for k in range(1, ncol):
        start(
            remote(
                my_half,
                g_ref.at[at.row, half_rows(at.col, at.dp)],
                col_send.at[k],
                col_recv.at[k],
                at.col_dev(at.ahead(k)),
            )
        )
    for k in range(1, ncol):
        to = at.ahead(k)
        dev = at.col_dev(to)
        start(
            remote(
                x_ref.at[:, prompt_cols(to)], xp_ref.at[mine],
                act_send.at[0, k], act_recv.at[0, k], dev,
            )
        )
        start(
            remote(
                x_ref.at[:, cont_cols(to)], xc_ref.at[mine],
                act_send.at[1, k], act_recv.at[1, k], dev,
            )
        )
    for k in range(1, ncol):
        to = at.ahead(k)
        start(
            remote(
                td_ref.at[:, :, own_cols(to)], tdo_ref.at[:, mine],
                act_send.at[2, k], act_recv.at[2, k], at.col_dev(to),
            )
        )

    def piece(row, k, core):
        return g_ref.at[row, half_rows(at.behind(k), core)]

    def landed(dst, recv_sem):
        remote(dst, dst, recv_sem, recv_sem, at.sibling).wait_recv()

    def chunk(k):
        return my_half if k == 0 else piece(at.row, k, at.dp)

    for k in range(ncol):
        if k:
            landed(piece(at.row, k, at.dp), col_recv.at[k])
        start(remote(chunk(k), piece(at.row, k, at.dp), one_send.at[k], one_recv.at[k], at.first_dev))
        start(
            remote(chunk(k), piece(at.row, k, at.dp), two_send.at[0, k], two_recv.at[0, k], at.second_dev)
        )
        if k:
            start(
                remote(chunk(k), piece(at.row, k, at.dp), sib_send.at[0, k], sib_recv.at[0, k], at.sibling)
            )
    for k in range(ncol):
        got = piece(at.first, k, at.dp)
        landed(got, one_recv.at[k])
        start(remote(got, got, two_send.at[1, k], two_recv.at[1, k], at.second_dev))
        start(remote(got, got, sib_send.at[1, k], sib_recv.at[1, k], at.sibling))
    for k in range(ncol):
        for i, row in ((0, at.second), (1, at.both)):
            got = piece(row, k, at.dp)
            landed(got, two_recv.at[i, k])
            start(remote(got, got, sib_send.at[2 + i, k], sib_recv.at[2 + i, k], at.sibling))

    for k in range(1, ncol):
        frm = rows_of(at.behind(k))
        landed(xp_ref.at[frm], act_recv.at[0, k])
        landed(xc_ref.at[frm], act_recv.at[1, k])
        landed(tdo_ref.at[:, frm], act_recv.at[2, k])
    other = 1 - at.dp
    for k in range(ncol):
        if k:
            landed(piece(at.row, k, other), sib_recv.at[0, k])
        landed(piece(at.second, k, other), sib_recv.at[1, k])
        landed(piece(at.first, k, other), sib_recv.at[2, k])
        landed(piece(at.both, k, other), sib_recv.at[3, k])
    for copy in pending:
        copy.wait_send()
    for i, (src, dst) in enumerate(
        (
            (x_ref.at[:, prompt_cols(at.col)], xp_ref.at[mine]),
            (x_ref.at[:, cont_cols(at.col)], xc_ref.at[mine]),
            (td_ref.at[:, :, own_cols(at.col)], tdo_ref.at[:, mine]),
            (w_ref, g_ref.at[at.row, mine]),
        )
    ):
        pltpu.make_async_copy(src, dst, local_sem.at[i]).wait()


def gather_all(x_stream, teach_dy, packed, ncol, nrow, parts):
    feat = x_stream.shape[0]
    full = feat * ncol
    own_tokens = GROUP // parts
    own_cont = NCONT * CONT // parts
    dma = pltpu.SemaphoreType.DMA
    anywhere = pl.BlockSpec(memory_space=pl.ANY)
    return pl.pallas_call(
        functools.partial(gather_kernel, ncol, parts),
        out_shape=(
            jax.ShapeDtypeStruct((full, PROMPT), BF16),
            jax.ShapeDtypeStruct((full, own_cont), BF16),
            jax.ShapeDtypeStruct((2, full, own_tokens), BF16),
            jax.ShapeDtypeStruct((nrow, full, packed.shape[1]), BF16),
        ),
        in_specs=[anywhere] * 3,
        out_specs=[anywhere] * 4,
        scratch_shapes=[
            dma((3, ncol)), dma((3, ncol)), dma((ncol,)), dma((ncol,)), dma((ncol,)), dma((ncol,)),
            dma((2, ncol)), dma((2, ncol)), dma((4, ncol)), dma((4, ncol)), dma((4,)),
        ],
        compiler_params=pltpu.CompilerParams(collective_id=0, has_side_effects=True),
        name="gather_all",
    )(x_stream, teach_dy, packed)


def scatter_kernel(
    ncol, parts, xb_ref, gp_ref, gc_ref, gw_ref, sm_ref,
    xbo_ref, gpo_ref, gco_ref, gwo_ref, smo_ref,
    sib_buf, two_buf, one_buf, col_buf, sm_buf, smc_buf,
    act_send, act_recv, sib_send, sib_recv, two_send, two_recv, one_send, one_recv,
    col_send, col_recv, fin_send, fin_recv, sm_send, sm_recv, smc_send, smc_recv, local_sem,
):
    at = Places(ncol)
    feat = xbo_ref.shape[1]
    half = feat // 2
    own_tokens = xb_ref.shape[2]
    own_cont = gc_ref.shape[1]
    part = at.col % parts

    def rows_of(c):
        return pl.ds(pl.multiple_of(c * feat, feat), feat)

    def half_rows(c, core):
        return pl.ds(pl.multiple_of(c * feat + core * half, half), half)

    def prompt_cols(c):
        return pl.ds(pl.multiple_of(c // parts * PROMPT, PROMPT), PROMPT)

    def cont_cols(c):
        return pl.ds(pl.multiple_of(c * own_cont, own_cont), own_cont)

    def own_cols(c):
        return pl.ds(pl.multiple_of(c * own_tokens, own_tokens), own_tokens)

    at.meet()
    pending = []

    def start(copy):
        copy.start()
        pending.append(copy)
        return copy

    def landed(dst, recv_sem):
        remote(dst, dst, recv_sem, recv_sem, at.sibling).wait_recv()

    other = 1 - at.dp
    order = list(range(1, ncol)) + [0]
    for k in order:
        start(
            remote(
                gw_ref.at[:, half_rows(at.ahead(k), other)], sib_buf.at[k],
                sib_send.at[k], sib_recv.at[k], at.sibling,
            )
        )
    start(remote(sm_ref, sm_buf.at[0], sm_send.at[0], sm_recv.at[0], at.sibling))

    def local_copies():
        mine = rows_of(at.col)
        return [
            pltpu.make_async_copy(src, dst, local_sem.at[i])
            for i, (src, dst) in enumerate(
                (
                    (xb_ref.at[:, mine], xbo_ref.at[:, :, own_cols(at.col)]),
                    (gp_ref.at[mine], gpo_ref.at[part, :, prompt_cols(at.col)]),
                    (gc_ref.at[mine], gco_ref.at[:, cont_cols(at.col)]),
                )
            )
        ]

    for copy in local_copies():
        copy.start()
    for k in range(1, ncol):
        to = at.ahead(k)
        dev = at.col_dev(to)
        start(
            remote(
                xb_ref.at[:, rows_of(to)], xbo_ref.at[:, :, own_cols(at.col)],
                act_send.at[0, k], act_recv.at[0, k], dev,
            )
        )
        start(
            remote(
                gp_ref.at[rows_of(to)], gpo_ref.at[part, :, prompt_cols(at.col)],
                act_send.at[1, k], act_recv.at[1, k], dev,
            )
        )
        start(
            remote(
                gc_ref.at[rows_of(to)], gco_ref.at[:, cont_cols(at.col)],
                act_send.at[2, k], act_recv.at[2, k], dev,
            )
        )

    for k in order:
        landed(sib_buf.at[k], sib_recv.at[k])
        for row in range(gw_ref.shape[0]):
            here = gw_ref.at[row, half_rows(at.ahead(k), at.dp)]
            sib_buf[k, row] = (here[...].astype(F32) + sib_buf[k, row].astype(F32)).astype(BF16)
        for i, row in ((0, at.second), (1, at.both)):
            start(
                remote(
                    sib_buf.at[k, row], two_buf.at[i, k],
                    two_send.at[i, k], two_recv.at[i, k], at.second_dev,
                )
            )
    landed(sm_buf.at[0], sm_recv.at[0])
    sm_buf[3] = sm_ref[...] + sm_buf[0]
    start(remote(sm_buf.at[3], sm_buf.at[1], sm_send.at[1], sm_recv.at[1], at.second_dev))
    for k in order:
        landed(two_buf.at[1, k], two_recv.at[1, k])
        two_buf[1, k] = (sib_buf[k, at.first].astype(F32) + two_buf[1, k].astype(F32)).astype(BF16)
        start(
            remote(
                two_buf.at[1, k], one_buf.at[k], one_send.at[k], one_recv.at[k], at.first_dev
            )
        )
    landed(sm_buf.at[1], sm_recv.at[1])
    sm_buf[4] = sm_buf[3] + sm_buf[1]
    start(remote(sm_buf.at[4], sm_buf.at[2], sm_send.at[2], sm_recv.at[2], at.first_dev))
    for k in order:
        landed(two_buf.at[0, k], two_recv.at[0, k])
        landed(one_buf.at[k], one_recv.at[k])
        total = sib_buf[k, at.row].astype(F32) + two_buf[0, k].astype(F32) + one_buf[k].astype(F32)
        if k:
            two_buf[0, k] = total.astype(BF16)
            start(
                remote(
                    two_buf.at[0, k], col_buf.at[k],
                    col_send.at[k], col_recv.at[k], at.col_dev(at.ahead(k)),
                )
            )
        else:
            own_total = total
    landed(sm_buf.at[2], sm_recv.at[2])
    sm_buf[5] = sm_buf[4] + sm_buf[2]
    for k in range(1, ncol):
        to = at.ahead(k)
        start(
            remote(
                sm_buf.at[5, to], smc_buf.at[k], smc_send.at[k], smc_recv.at[k], at.col_dev(to)
            )
        )
    for k in range(1, ncol):
        landed(col_buf.at[k], col_recv.at[k])
        own_total = own_total + col_buf[k].astype(F32)
    my_rows = pl.ds(pl.multiple_of(at.dp * half, half), half)
    gwo_ref[my_rows] = own_total
    start(remote(gwo_ref.at[my_rows], gwo_ref.at[my_rows], fin_send, fin_recv, at.sibling))
    small = sm_buf[5, at.col]
    for k in range(1, ncol):
        landed(smc_buf.at[k], smc_recv.at[k])
        small = small + smc_buf[k]
    smo_ref[...] = small
    landed(gwo_ref.at[pl.ds(pl.multiple_of(other * half, half), half)], fin_recv)
    for k in range(1, ncol):
        frm = at.behind(k)
        landed(xbo_ref.at[:, :, own_cols(frm)], act_recv.at[0, k])
        landed(gpo_ref.at[frm % parts, :, prompt_cols(frm)], act_recv.at[1, k])
        landed(gco_ref.at[:, cont_cols(frm)], act_recv.at[2, k])
    for copy in pending:
        copy.wait_send()
    for copy in local_copies():
        copy.wait()


def scatter_all(xb, gp, gc, gw, small, ncol, parts):
    nrow, full, width = gw.shape
    feat = full // ncol
    half = feat // 2
    groups = ncol // parts
    own_tokens, own_cont = xb.shape[2], gc.shape[1]
    dma = pltpu.SemaphoreType.DMA
    anywhere = pl.BlockSpec(memory_space=pl.ANY)
    vmem = pl.BlockSpec(memory_space=pltpu.VMEM)
    small_shape = small.shape
    return pl.pallas_call(
        functools.partial(scatter_kernel, ncol, parts),
        out_shape=(
            jax.ShapeDtypeStruct((2, feat, ncol * own_tokens), BF16),
            jax.ShapeDtypeStruct((parts, feat, groups * PROMPT), BF16),
            jax.ShapeDtypeStruct((feat, ncol * own_cont), BF16),
            jax.ShapeDtypeStruct((feat, width), F32),
            jax.ShapeDtypeStruct(small_shape[1:], F32),
        ),
        in_specs=[anywhere, anywhere, anywhere, vmem, vmem],
        out_specs=[anywhere, anywhere, anywhere, vmem, vmem],
        scratch_shapes=[
            pltpu.VMEM((ncol, nrow, half, width), BF16),
            pltpu.VMEM((2, ncol, half, width), BF16),
            pltpu.VMEM((ncol, half, width), BF16),
            pltpu.VMEM((ncol, half, width), BF16),
            pltpu.VMEM((6,) + small_shape, F32),
            pltpu.VMEM((ncol,) + small_shape[1:], F32),
            dma((3, ncol)), dma((3, ncol)), dma((ncol,)), dma((ncol,)), dma((2, ncol)), dma((2, ncol)),
            dma((ncol,)), dma((ncol,)), dma((ncol,)), dma((ncol,)), dma(()), dma(()),
            dma((3,)), dma((3,)), dma((ncol,)), dma((ncol,)), dma((3,)),
        ],
        compiler_params=pltpu.CompilerParams(
            collective_id=1, has_side_effects=True, vmem_limit_bytes=56 << 20
        ),
        name="scatter_all",
    )(xb, gp, gc, gw, small)


def to_parts(array_in, parts):
    lead = array_in.shape[:-1]
    groups = array_in.shape[-1] // GROUP
    split = array_in.reshape(lead + (groups, GROUP))
    prompt = split[..., :PROMPT].reshape(lead + (groups, 2, parts, BLOCK))
    prompt = jnp.stack([prompt[..., 0, :, :], prompt[..., 1, ::-1, :]], axis=-2)
    prompt = prompt.reshape(lead + (groups, parts, PROMPT // parts))
    cont = split[..., PROMPT:].reshape(lead + (groups, parts, NCONT * CONT // parts))
    return jnp.concatenate([prompt, cont], axis=-1).reshape(array_in.shape)


def from_parts(array_in, parts):
    lead = array_in.shape[:-1]
    groups = array_in.shape[-1] // GROUP
    split = array_in.reshape(lead + (groups, parts, GROUP // parts))
    prompt = split[..., : PROMPT // parts].reshape(lead + (groups, parts, 2, BLOCK))
    prompt = jnp.concatenate(
        [prompt[..., :, 0, :], prompt[..., ::-1, 1, :]], axis=-2
    ).reshape(lead + (groups, PROMPT))
    cont = split[..., PROMPT // parts :].reshape(lead + (groups, NCONT * CONT))
    return jnp.concatenate([prompt, cont], axis=-1).reshape(array_in.shape)


def norm_forward(summed, gain_vec, bias_vec):
    average = jnp.mean(summed, axis=0, keepdims=True)
    squares = jnp.mean(summed * summed, axis=0, keepdims=True)
    inv_scale = lax.rsqrt(squares - average * average + EPS_NORM)
    unit_val = (summed - average) * inv_scale
    return (unit_val * gain_vec + bias_vec, unit_val, inv_scale)


def norm_backward(upstream, unit_val, inv_scale, gain_vec):
    scaled = upstream * gain_vec
    first = jnp.mean(scaled, axis=0, keepdims=True)
    second = jnp.mean(scaled * unit_val, axis=0, keepdims=True)
    d_summed = inv_scale * (scaled - first - unit_val * second)
    sums = [jnp.sum(v, axis=1, keepdims=True) for v in (upstream * unit_val, upstream)]
    return (d_summed, *sums)


def dot_tn(lhs, rhs):
    return lax.dot_general(lhs, rhs, (((0,), (0,)), ((), ())), preferred_element_type=F32)


def dot_nn(lhs, rhs):
    return lax.dot_general(lhs, rhs, (((1,), (0,)), ((), ())), preferred_element_type=F32)


def dot_nt(lhs, rhs):
    return lax.dot_general(lhs, rhs, (((1,), (1,)), ((), ())), preferred_element_type=F32)


def iota(shape, axis):
    return lax.broadcasted_iota(jnp.int32, shape, axis)


def fold(array_in, op):
    return op(array_in.reshape(array_in.shape[0] // 8, 8, array_in.shape[1]), axis=0)


KEYS = 256
PAIR = 2 * BLOCK


class Layer:
    def __init__(self, part, parts, lens, total_tokens, count):
        self.part, self.parts = part, parts
        self.lens = lens
        self.total_tokens, self.count = total_tokens, count
        slot = iota((1, BLOCK), 1)
        low, high = part * BLOCK + slot, (2 * parts - 1 - part) * BLOCK + slot
        last = lens[0] - 1
        self.bound = jnp.concatenate(
            [jnp.minimum(low, last), jnp.minimum(high, last), jnp.full((1, PAIR), last, jnp.int32)],
            axis=1,
        )
        live = [low < lens[0], high < lens[0]] + [slot < n for n in lens[1:]]
        self.live = jnp.concatenate([m.astype(F32) for m in live], axis=1)

    def own_columns(self):
        low = pl.ds(pl.multiple_of(self.part * BLOCK, BLOCK), BLOCK)
        high = pl.ds(pl.multiple_of((2 * self.parts - 1 - self.part) * BLOCK, BLOCK), BLOCK)
        return low, high

    def project(self, xp, xc, w, xo, xt, kv, kvt, qt):
        low, high = self.own_columns()
        xo[:, :BLOCK] = xp[:, low]
        xo[:, BLOCK:PAIR] = xp[:, high]
        xo[:, PAIR:] = xc[...]
        xt[:PROMPT] = xp[...].T
        xt[PROMPT:] = xc[...].T

        def step(r, carry):
            wq, wkv = w[r, :, :BLOCK], w[r, :, BLOCK : 3 * BLOCK]
            cols = pl.ds(pl.multiple_of(r * PAIR, PAIR), PAIR)
            kv[:, cols] = dot_nn(xt[...], wkv).astype(BF16)
            kvt[r, :, :PROMPT] = dot_tn(wkv, xp[...]).astype(BF16)
            kvt[r, :, PROMPT:] = dot_tn(wkv, xc[...]).astype(BF16)
            rows = pl.ds(pl.multiple_of(r * BLOCK, BLOCK), BLOCK)
            qt[rows] = (dot_tn(wq, xo[...]).astype(BF16).astype(F32) * HD ** (-0.5)).astype(BF16)
            return carry

        lax.fori_loop(0, w.shape[0], step, 0)

    def one_head(self, array_in, head):
        zeros = jnp.zeros((HD, array_in.shape[1]), array_in.dtype)
        mine = array_in[head * HD : (head + 1) * HD]
        return jnp.concatenate([mine, zeros] if head == 0 else [zeros, mine], axis=0)

    def masked(self, score, first_key, columns):
        keys = iota(score.shape, 0) + first_key
        return jnp.where(keys <= self.bound[:, columns], score, NEG_FILL)

    def masked_own(self, score, n):
        keys = iota(score.shape, 0)
        return jnp.where(
            (keys <= iota(score.shape, 1)) & (keys < self.lens[1 + n]), score, NEG_FILL
        )

    def attend(self, kv, kvt, qt, att, lse, s_scr, p_scr):
        def step(r, carry):
            k_cols = pl.ds(pl.multiple_of(r * PAIR, PAIR), BLOCK)
            q_pair = qt[pl.ds(pl.multiple_of(r * BLOCK, BLOCK), BLOCK)]
            for head in range(2):
                query = self.one_head(q_pair, head)
                v_rows = slice(BLOCK + head * HD, BLOCK + (head + 1) * HD)
                for b in range(2):
                    columns = slice(b * PAIR, (b + 1) * PAIR)
                    q_here = query[:, columns]
                    top = jnp.full((8, PAIR), NEG_FILL, F32)
                    for first in range(0, PROMPT, KEYS):
                        score = dot_nn(kv[first : first + KEYS, k_cols], q_here)
                        score = self.masked(score, first, columns)
                        s_scr[head, first : first + KEYS] = score
                        top = jnp.maximum(top, fold(score, jnp.max))
                    own_scores = []
                    if b == 1:
                        for n in range(2):
                            keys = slice(PROMPT + n * BLOCK, PROMPT + (n + 1) * BLOCK)
                            score = dot_nn(kv[keys, k_cols], q_here[:, n * BLOCK : (n + 1) * BLOCK])
                            own_scores.append(self.masked_own(score, n))
                        own_top = [fold(score, jnp.max) for score in own_scores]
                        top = jnp.maximum(top, jnp.concatenate(own_top, axis=1))
                    top = jnp.max(top, axis=0, keepdims=True)
                    total = jnp.zeros((8, PAIR), F32)
                    for first in range(0, PROMPT, KEYS):
                        prob = jnp.exp(s_scr[head, first : first + KEYS] - top)
                        total = total + fold(prob, jnp.sum)
                        p_scr[head, first : first + KEYS] = prob.astype(BF16)
                    out = dot_nn(kvt[r, v_rows, :PROMPT], p_scr[head])
                    if b == 1:
                        own_out, own_total = [], []
                        for n in range(2):
                            lanes = slice(n * BLOCK, (n + 1) * BLOCK)
                            prob = jnp.exp(own_scores[n] - top[:, lanes])
                            own_total.append(fold(prob, jnp.sum))
                            keys = slice(PROMPT + n * BLOCK, PROMPT + (n + 1) * BLOCK)
                            own_out.append(dot_nn(kvt[r, v_rows, keys], prob.astype(BF16)))
                        total = total + jnp.concatenate(own_total, axis=1)
                        out = out + jnp.concatenate(own_out, axis=1)
                    total = jnp.sum(total, axis=0, keepdims=True)
                    rows = pl.ds(pl.multiple_of(r * BLOCK + head * HD, HD), HD)
                    att[rows, columns] = (out / total).astype(BF16)
                    lse[pl.ds(2 * r + head, 1), columns] = top + jnp.log(total)
            return carry

        lax.fori_loop(0, kvt.shape[0], step, 0)

    def attend_back(self, kv, kvt, qt, lse, delta, d_att, dkvt, dqt, p_scr, ds_scr):
        def step(r, carry):
            k_cols = pl.ds(pl.multiple_of(r * PAIR, PAIR), BLOCK)
            v_cols = pl.ds(pl.multiple_of(r * PAIR + BLOCK, BLOCK), BLOCK)
            pair = pl.ds(pl.multiple_of(r * BLOCK, BLOCK), BLOCK)
            q_pair, d_pair = qt[pair], d_att[pair]
            for head in range(2):
                query, d_out = self.one_head(q_pair, head), self.one_head(d_pair, head)
                q_mine = q_pair[head * HD : (head + 1) * HD]
                d_mine = d_pair[head * HD : (head + 1) * HD]
                k_rows = slice(head * HD, (head + 1) * HD)
                v_rows = slice(BLOCK + head * HD, BLOCK + (head + 1) * HD)
                norm = lse[pl.ds(2 * r + head, 1)]
                dlt = delta[pl.ds(2 * r + head, 1)]
                for b in range(2):
                    columns = slice(b * PAIR, (b + 1) * PAIR)
                    for first in range(0, PROMPT, KEYS):
                        keys = slice(first, first + KEYS)
                        score = dot_nn(kv[keys, k_cols], query[:, columns])
                        score = self.masked(score, first, columns)
                        prob = jnp.exp(score - norm[:, columns])
                        dprob = dot_nn(kv[keys, v_cols], d_out[:, columns])
                        p_scr[head, keys, columns] = prob.astype(BF16)
                        ds_scr[head, keys, columns] = (prob * (dprob - dlt[:, columns])).astype(BF16)
                d_query = dot_nn(kvt[r, k_rows, :PROMPT], ds_scr[head])
                own_dq = [jnp.zeros((HD, PAIR), F32)]
                for n in range(2):
                    keys = slice(PROMPT + n * BLOCK, PROMPT + (n + 1) * BLOCK)
                    lanes = slice(PAIR + n * BLOCK, PAIR + (n + 1) * BLOCK)
                    score = self.masked_own(dot_nn(kv[keys, k_cols], query[:, lanes]), n)
                    prob = jnp.exp(score - norm[:, lanes])
                    dprob = dot_nn(kv[keys, v_cols], d_out[:, lanes])
                    d_score = (prob * (dprob - dlt[:, lanes])).astype(BF16)
                    own_dq.append(dot_nn(kvt[r, k_rows, keys], d_score))
                    dkvt[r, k_rows, keys] = dot_nt(q_mine[:, lanes], d_score).astype(BF16)
                    dkvt[r, v_rows, keys] = dot_nt(d_mine[:, lanes], prob.astype(BF16)).astype(BF16)
                d_query = (d_query + jnp.concatenate(own_dq, axis=1)) * HD ** (-0.5)
                rows = pl.ds(pl.multiple_of(r * BLOCK + head * HD, HD), HD)
                dqt[rows] = d_query.astype(BF16)
                dkvt[r, k_rows, :PROMPT] = dot_nt(q_mine, ds_scr[head]).astype(BF16)
                dkvt[r, v_rows, :PROMPT] = dot_nt(d_mine, p_scr[head]).astype(BF16)
            return carry

        lax.fori_loop(0, kvt.shape[0], step, 0)

    def input_grads(self, xp, xc, xo, w, dkvt, dqt, dsa, gp, gc, gw, dx, dxo):
        for r in range(w.shape[0]):
            wq, wkv = w[r, :, :BLOCK], w[r, :, BLOCK : 3 * BLOCK]
            part = dot_nn(wkv, dkvt[r])
            rows = slice(r * BLOCK, (r + 1) * BLOCK)
            own = dot_nn(wq, dqt[rows])
            if r == 0:
                dx[...] = part
                dxo[...] = dsa[...] + own
            else:
                dx[...] += part
                dxo[...] += own
            gw[r, :, :BLOCK] = dot_nt(xo[...], dqt[rows]).astype(BF16)
            gw[r, :, BLOCK : 3 * BLOCK] = (
                dot_nt(xp[...], dkvt[r, :, :PROMPT]) + dot_nt(xc[...], dkvt[r, :, PROMPT:])
            ).astype(BF16)
        low, high = self.own_columns()
        dx[:, low] += dxo[:, :BLOCK]
        dx[:, high] += dxo[:, BLOCK:PAIR]
        gp[...] = dx[:, :PROMPT].astype(BF16)
        gc[...] = (dx[:, PROMPT:] + dxo[:, PAIR:]).astype(BF16)

    def middle(self, xo, tdo, w, vec, att, xb, gw, sm, d_att, delta, dsa, hid, acc, ba):
        nrow, full = w.shape[0], w.shape[1]
        ff = (w.shape[2] - 4 * BLOCK) // 2
        up, down = slice(4 * BLOCK, 4 * BLOCK + ff), slice(4 * BLOCK + ff, 4 * BLOCK + 2 * ff)
        gain_a, bias_a, gain_f, bias_f = (vec[:, i : i + 1].astype(F32) for i in range(4))
        w_o = jnp.concatenate([w[r, :, 3 * BLOCK : 4 * BLOCK] for r in range(nrow)], axis=1)
        ba[...] = dot_nn(w_o, att[...])
        x_one, unit_a, inv_a = norm_forward(xo[...].astype(F32) + ba[...], gain_a, bias_a)
        x_low = x_one.astype(BF16)
        x_low_t = x_low.T
        acc[...] = jnp.zeros_like(acc)

        def up_down(r, carry):
            pre = dot_nn(x_low_t, w[r, :, up])
            hidden = jnp.maximum(pre, 0.0).astype(BF16)
            hid[r] = hidden
            acc[...] += dot_nt(w[r, :, down], hidden)
            return carry

        lax.fori_loop(0, nrow, up_down, 0)
        branch_f = acc[...]
        x_two, unit_f, inv_f = norm_forward(x_one + branch_f, gain_f, bias_f)
        branch = ba[...] + branch_f
        xb[0] = x_two.astype(BF16)
        xb[1] = branch.astype(BF16)
        diff_x = x_two - tdo[0].astype(F32)
        diff_y = branch + tdo[1].astype(F32)
        loss = jnp.sum(self.live * (diff_x * diff_x + diff_y * diff_y))
        weight = self.live * (self.total_tokens / self.count)
        grad_y = diff_y * weight
        d_sum_f, gain_grad_f, bias_grad_f = norm_backward(diff_x * weight, unit_f, inv_f, gain_f)
        d_branch_f = (d_sum_f + grad_y).astype(BF16)
        d_branch_t = d_branch_f.T
        acc[...] = d_sum_f

        def back(r, carry):
            hidden = hid[r]
            d_hidden = dot_nn(d_branch_t, w[r, :, down])
            d_pre = jnp.where(hidden.astype(F32) > 0, d_hidden, 0.0).astype(BF16)
            gw[r, :, up] = dot_nn(x_low, d_pre).astype(BF16)
            gw[r, :, down] = dot_nn(d_branch_f, hidden).astype(BF16)
            acc[...] += dot_nt(w[r, :, up], d_pre)
            return carry

        lax.fori_loop(0, nrow, back, 0)
        d_sum_a, gain_grad_a, bias_grad_a = norm_backward(acc[...], unit_a, inv_a, gain_a)
        dsa[...] = d_sum_a
        d_branch_a = (d_sum_a + grad_y).astype(BF16)
        for r in range(nrow):
            rows = slice(r * BLOCK, (r + 1) * BLOCK)
            attended = att[rows]
            gw[r, :, 3 * BLOCK : 4 * BLOCK] = dot_nt(d_branch_a, attended).astype(BF16)
            d_here = dot_tn(w[r, :, 3 * BLOCK : 4 * BLOCK], d_branch_a).astype(BF16)
            d_att[rows] = d_here
            product = attended.astype(F32) * d_here.astype(F32)
            for head in range(2):
                delta[2 * r + head : 2 * r + head + 1] = jnp.sum(
                    product[head * HD : (head + 1) * HD], axis=0, keepdims=True
                )
        lane = iota((full, 128), 1)
        sums = jnp.zeros((full, 128), F32)
        for i, vector in enumerate((gain_grad_a, bias_grad_a, gain_grad_f, bias_grad_f)):
            sums = jnp.where(lane == i, vector, sums)
        sums = jnp.where(lane == 4, loss, sums)
        sm[...] = sums.T[:8]


def layer_kernel(
    parts, lens_ref, len_table, xp, xc, tdo, w, vec, xb, gp, gc, gw, sm,
    xo, xt, kv, kvt, qt, att, lse, delta, d_att, dkvt, dqt, s_scr, pf_scr, p_scr, ds_scr,
    dsa, hid, acc, ba, dx,
):
    col = lax.axis_index("col")
    groups = lax.axis_size("col") // parts
    chip = lax.axis_index("dp") * lax.axis_size("row") + lax.axis_index("row")
    group = chip * groups + col // parts
    part = col % parts
    lens = [lens_ref[group, 0]] + [lens_ref[group, 1 + 2 * part + n] for n in range(2)]
    count = jnp.sum(len_table[...].astype(F32))
    layer = Layer(part, parts, lens, lens_ref.shape[0] * GROUP, count)
    layer.project(xp, xc, w, xo, xt, kv, kvt, qt)
    layer.attend(kv, kvt, qt, att, lse, s_scr, pf_scr)
    layer.middle(xo, tdo, w, vec, att, xb, gw, sm, d_att, delta, dsa, hid, acc, ba)
    layer.attend_back(kv, kvt, qt, lse, delta, d_att, dkvt, dqt, p_scr, ds_scr)
    layer.input_grads(xp, xc, xo, w, dkvt, dqt, dsa, gp, gc, gw, dx, acc)


def run_layer(lengths, xp, xc, tdo, weights, vec, parts):
    nrow, full, width = weights.shape
    own, keys = tdo.shape[2], xp.shape[1] + xc.shape[1]
    heads = full // HD
    vmem = pl.BlockSpec(memory_space=pltpu.VMEM)
    return pl.pallas_call(
        functools.partial(layer_kernel, parts),
        out_shape=(
            jax.ShapeDtypeStruct((2, full, own), BF16),
            jax.ShapeDtypeStruct(xp.shape, BF16),
            jax.ShapeDtypeStruct(xc.shape, BF16),
            jax.ShapeDtypeStruct(weights.shape, BF16),
            jax.ShapeDtypeStruct((8, full), F32),
        ),
        in_specs=[pl.BlockSpec(memory_space=pltpu.SMEM)] + [vmem] * 6,
        out_specs=[vmem] * 5,
        scratch_shapes=[
            pltpu.VMEM((full, own), BF16),
            pltpu.VMEM((keys, full), BF16),
            pltpu.VMEM((keys, nrow * PAIR), BF16),
            pltpu.VMEM((nrow, PAIR, keys), BF16),
            pltpu.VMEM((full, own), BF16),
            pltpu.VMEM((full, own), BF16),
            pltpu.VMEM((heads, own), F32),
            pltpu.VMEM((heads, own), F32),
            pltpu.VMEM((full, own), BF16),
            pltpu.VMEM((nrow, PAIR, keys), BF16),
            pltpu.VMEM((full, own), BF16),
            pltpu.VMEM((2, PROMPT, PAIR), F32),
            pltpu.VMEM((2, PROMPT, PAIR), BF16),
            pltpu.VMEM((2, PROMPT, own), BF16),
            pltpu.VMEM((2, PROMPT, own), BF16),
            pltpu.VMEM((full, own), F32),
            pltpu.VMEM((nrow, own, (width - 4 * BLOCK) // 2), BF16),
            pltpu.VMEM((full, own), F32),
            pltpu.VMEM((full, own), F32),
            pltpu.VMEM((full, keys), F32),
        ],
        compiler_params=pltpu.CompilerParams(vmem_limit_bytes=60 << 20),
        name="layer",
    )(lengths, lengths, xp, xc, tdo, weights, vec)


def body(
    x_stream, y_stream, w_qkv, w_out, gain_attn, bias_attn, w_up, w_down, gain_ffn, bias_ffn,
    teach_x, teach_y, lengths,
):
    ncol, nrow = lax.axis_size("col"), lax.axis_size("row")
    feat, tokens = x_stream.shape
    full = feat * ncol
    groups_here = tokens // GROUP
    parts = ncol // groups_here
    assert parts * 2 * BLOCK == PROMPT and nrow == 4
    block = w_qkv.shape[2]
    ff_block = w_up.shape[1]

    y_f32 = y_stream.astype(F32)
    dy = y_f32 - teach_y.astype(F32)
    teach_dy = to_parts(jnp.stack([teach_x, dy.astype(BF16)]), parts)
    packed = jnp.concatenate([w_qkv.reshape(feat, 3 * block), w_out.T, w_up, w_down.T], axis=1)
    small_vecs = jnp.stack([gain_attn, bias_attn, gain_ffn, bias_ffn])
    vecs = lax.all_gather(small_vecs, "col", axis=1, tiled=True)

    x_prompt, x_cont, tdo, weights = gather_all(x_stream, teach_dy, packed, ncol, nrow, parts)

    first = (lax.axis_index("dp") * nrow + lax.axis_index("row")) * groups_here
    count_all = jnp.sum(lengths).astype(F32)
    total_tokens = lengths.shape[0] * GROUP
    vec = jnp.pad(vecs.T, ((0, 0), (0, 124)))
    xb, gp, gc, gw, small = run_layer(lengths, x_prompt, x_cont, tdo, weights, vec, parts)
    lanes = max(feat, 128)
    small = small.reshape(8, ncol, feat).transpose(1, 0, 2)
    small = jnp.pad(small, ((0, 0), (0, 0), (0, lanes - feat)))
    xb, gp, gc, gw, sums = scatter_all(xb, gp, gc, gw, small, ncol, parts)

    xb = from_parts(xb, parts)
    branch = xb[1].astype(F32)
    live_all = live_slots(
        lax.dynamic_slice_in_dim(lengths, first, groups_here, 0)
    ).reshape(1, tokens)
    y_out = (y_f32 + branch).astype(BF16)
    grad_y_out = (dy + branch) * (live_all * (total_tokens / count_all))
    gp = jnp.sum(gp.astype(F32), axis=0).reshape(feat, groups_here, PROMPT)
    gc = gc.astype(F32).reshape(feat, groups_here, NCONT * CONT)
    grad_x = jnp.concatenate([gp, gc], axis=2).reshape(feat, tokens)
    loss = sums[4, 0] / (2.0 * count_all * full)
    first_up = 4 * block
    return (
        xb[0],
        y_out,
        grad_x,
        grad_y_out,
        gw[:, : 3 * block].reshape(feat, 3, block),
        gw[:, 3 * block : 4 * block].T,
        sums[0, :feat],
        sums[1, :feat],
        gw[:, first_up : first_up + ff_block],
        gw[:, first_up + ff_block :].T,
        sums[2, :feat],
        sums[3, :feat],
        loss,
    )


def live_slots(lens):
    prompt = jnp.arange(PROMPT, dtype=jnp.int32)[None, :] < lens[:, 0:1]
    cont = jnp.arange(CONT, dtype=jnp.int32)[None, None, :] < lens[:, 1:, None]
    cont = cont.reshape(lens.shape[0], NCONT * CONT)
    return jnp.concatenate([prompt, cont], axis=1).astype(F32)


def solution(mesh):
    stream = P("col", ("dp", "row"))
    up, down = P("col", "row"), P("row", "col")
    qkv, vec = P("col", None, "row"), P("col")
    return jax.shard_map(
        body,
        mesh=mesh,
        in_specs=(
            stream, stream, qkv, down, vec, vec, up, down, vec, vec, stream, stream, P(),
        ),
        out_specs=(
            stream, stream, stream, stream, qkv, down, vec, vec, up, down, vec, vec, P(),
        ),
        check_vma=False,
    )
```

```python
import functools

import jax
import jax.numpy as jnp
from jax import lax
from jax.experimental import pallas as pl
from jax.experimental.pallas import tpu as pltpu
from jax.sharding import PartitionSpec as P

HD = 64
PROMPT = 1024
CONT = 128
NCONT = 8
GROUP = 2048
BLOCK = 128

EPS_NORM = 1e-05
NEG_FILL = -1000000000.0
MESH = pl.DeviceIdType.MESH
F32 = jnp.float32
BF16 = jnp.bfloat16


def flip_low(r):
    return r + 1 - 2 * (r % 2)


def flip_high(r):
    return (r + 2) % 4


class Places:
    def __init__(self, ncol):
        self.dp = lax.axis_index("dp")
        self.row = lax.axis_index("row")
        self.col = lax.axis_index("col")
        self.ncol = ncol
        low, high = flip_low(self.row), flip_high(self.row)
        self.first = low * (1 - self.dp) + high * self.dp
        self.second = high * (1 - self.dp) + low * self.dp
        self.both = 3 - self.row
        self.sibling = (1 - self.dp, self.row, self.col)
        self.first_dev = (self.dp, self.first, self.col)
        self.second_dev = (self.dp, self.second, self.col)
        self.aheads = [(self.col + k) % ncol for k in range(ncol)]
        self.behinds = [(self.col + ncol - k) % ncol for k in range(ncol)]

    def ahead(self, k):
        return self.aheads[k]

    def behind(self, k):
        return self.behinds[k]

    def col_dev(self, c):
        return (self.dp, self.row, c)

    def meet(self):
        barrier = pltpu.get_barrier_semaphore()
        partners = [self.sibling, self.first_dev, self.second_dev]
        partners += [self.col_dev(self.ahead(k)) for k in range(1, self.ncol)]
        for partner in partners:
            pl.semaphore_signal(barrier, inc=1, device_id=partner, device_id_type=MESH)
        pl.semaphore_wait(barrier, len(partners))


def remote(src, dst, send_sem, recv_sem, device):
    return pltpu.make_async_remote_copy(
        src_ref=src,
        dst_ref=dst,
        send_sem=send_sem,
        recv_sem=recv_sem,
        device_id=device,
        device_id_type=MESH,
    )


def gather_kernel(
    ncol, parts, x_ref, td_ref, w_ref, xp_ref, xc_ref, tdo_ref, g_ref,
    act_send, act_recv, col_send, col_recv, one_send, one_recv, two_send, two_recv,
    sib_send, sib_recv, local_sem,
):
    at = Places(ncol)
    feat = x_ref.shape[0]
    half = feat // 2
    own_tokens = tdo_ref.shape[2]
    own_cont = xc_ref.shape[1]

    def rows_of(c):
        return pl.ds(pl.multiple_of(c * feat, feat), feat)

    def half_rows(c, core):
        return pl.ds(pl.multiple_of(c * feat + core * half, half), half)

    def prompt_cols(c):
        return pl.ds(pl.multiple_of(c // parts * GROUP, GROUP), PROMPT)

    def cont_cols(c):
        return pl.ds(
            pl.multiple_of(c // parts * GROUP + PROMPT + c % parts * own_cont, own_cont), own_cont
        )

    def own_cols(c):
        return pl.ds(pl.multiple_of(c * own_tokens, own_tokens), own_tokens)

    at.meet()
    my_half = w_ref.at[pl.ds(pl.multiple_of(at.dp * half, half), half)]
    pending = []

    def start(copy):
        copy.start()
        pending.append(copy)
        return copy

    mine = rows_of(at.col)
    for i, (src, dst) in enumerate(
        (
            (x_ref.at[:, prompt_cols(at.col)], xp_ref.at[mine]),
            (x_ref.at[:, cont_cols(at.col)], xc_ref.at[mine]),
            (td_ref.at[:, :, own_cols(at.col)], tdo_ref.at[:, mine]),
            (w_ref, g_ref.at[at.row, mine]),
        )
    ):
        pltpu.make_async_copy(src, dst, local_sem.at[i]).start()

    for k in range(1, ncol):
        start(
            remote(
                my_half,
                g_ref.at[at.row, half_rows(at.col, at.dp)],
                col_send.at[k],
                col_recv.at[k],
                at.col_dev(at.ahead(k)),
            )
        )
    for k in range(1, ncol):
        to = at.ahead(k)
        dev = at.col_dev(to)
        start(
            remote(
                x_ref.at[:, prompt_cols(to)], xp_ref.at[mine],
                act_send.at[0, k], act_recv.at[0, k], dev,
            )
        )
        start(
            remote(
                x_ref.at[:, cont_cols(to)], xc_ref.at[mine],
                act_send.at[1, k], act_recv.at[1, k], dev,
            )
        )
    for k in range(1, ncol):
        to = at.ahead(k)
        start(
            remote(
                td_ref.at[:, :, own_cols(to)], tdo_ref.at[:, mine],
                act_send.at[2, k], act_recv.at[2, k], at.col_dev(to),
            )
        )

    def piece(row, k, core):
        return g_ref.at[row, half_rows(at.behind(k), core)]

    def landed(dst, recv_sem):
        remote(dst, dst, recv_sem, recv_sem, at.sibling).wait_recv()

    def chunk(k):
        return my_half if k == 0 else piece(at.row, k, at.dp)

    for k in range(ncol):
        if k:
            landed(piece(at.row, k, at.dp), col_recv.at[k])
        start(remote(chunk(k), piece(at.row, k, at.dp), one_send.at[k], one_recv.at[k], at.first_dev))
        start(
            remote(chunk(k), piece(at.row, k, at.dp), two_send.at[0, k], two_recv.at[0, k], at.second_dev)
        )
        if k:
            start(
                remote(chunk(k), piece(at.row, k, at.dp), sib_send.at[0, k], sib_recv.at[0, k], at.sibling)
            )
    for k in range(ncol):
        got = piece(at.first, k, at.dp)
        landed(got, one_recv.at[k])
        start(remote(got, got, two_send.at[1, k], two_recv.at[1, k], at.second_dev))
        start(remote(got, got, sib_send.at[1, k], sib_recv.at[1, k], at.sibling))
    for k in range(ncol):
        for i, row in ((0, at.second), (1, at.both)):
            got = piece(row, k, at.dp)
            landed(got, two_recv.at[i, k])
            start(remote(got, got, sib_send.at[2 + i, k], sib_recv.at[2 + i, k], at.sibling))

    for k in range(1, ncol):
        frm = rows_of(at.behind(k))
        landed(xp_ref.at[frm], act_recv.at[0, k])
        landed(xc_ref.at[frm], act_recv.at[1, k])
        landed(tdo_ref.at[:, frm], act_recv.at[2, k])
    other = 1 - at.dp
    for k in range(ncol):
        if k:
            landed(piece(at.row, k, other), sib_recv.at[0, k])
        landed(piece(at.second, k, other), sib_recv.at[1, k])
        landed(piece(at.first, k, other), sib_recv.at[2, k])
        landed(piece(at.both, k, other), sib_recv.at[3, k])
    for copy in pending:
        copy.wait_send()
    for i, (src, dst) in enumerate(
        (
            (x_ref.at[:, prompt_cols(at.col)], xp_ref.at[mine]),
            (x_ref.at[:, cont_cols(at.col)], xc_ref.at[mine]),
            (td_ref.at[:, :, own_cols(at.col)], tdo_ref.at[:, mine]),
            (w_ref, g_ref.at[at.row, mine]),
        )
    ):
        pltpu.make_async_copy(src, dst, local_sem.at[i]).wait()


def gather_all(x_stream, teach_dy, packed, ncol, nrow, parts):
    feat = x_stream.shape[0]
    full = feat * ncol
    own_tokens = GROUP // parts
    own_cont = NCONT * CONT // parts
    dma = pltpu.SemaphoreType.DMA
    anywhere = pl.BlockSpec(memory_space=pl.ANY)
    return pl.pallas_call(
        functools.partial(gather_kernel, ncol, parts),
        out_shape=(
            jax.ShapeDtypeStruct((full, PROMPT), BF16),
            jax.ShapeDtypeStruct((full, own_cont), BF16),
            jax.ShapeDtypeStruct((2, full, own_tokens), BF16),
            jax.ShapeDtypeStruct((nrow, full, packed.shape[1]), BF16),
        ),
        in_specs=[anywhere] * 3,
        out_specs=[anywhere] * 4,
        scratch_shapes=[
            dma((3, ncol)), dma((3, ncol)), dma((ncol,)), dma((ncol,)), dma((ncol,)), dma((ncol,)),
            dma((2, ncol)), dma((2, ncol)), dma((4, ncol)), dma((4, ncol)), dma((4,)),
        ],
        compiler_params=pltpu.CompilerParams(collective_id=0, has_side_effects=True),
        name="gather_all",
    )(x_stream, teach_dy, packed)


def scatter_kernel(
    ncol, parts, xb_ref, gp_ref, gc_ref, gw_ref, sm_ref,
    xbo_ref, gpo_ref, gco_ref, gwo_ref, smo_ref,
    sib_buf, two_buf, one_buf, col_buf, sm_buf, smc_buf,
    act_send, act_recv, sib_send, sib_recv, two_send, two_recv, one_send, one_recv,
    col_send, col_recv, fin_send, fin_recv, sm_send, sm_recv, smc_send, smc_recv, local_sem,
):
    at = Places(ncol)
    feat = xbo_ref.shape[1]
    half = feat // 2
    own_tokens = xb_ref.shape[2]
    own_cont = gc_ref.shape[1]
    part = at.col % parts

    def rows_of(c):
        return pl.ds(pl.multiple_of(c * feat, feat), feat)

    def half_rows(c, core):
        return pl.ds(pl.multiple_of(c * feat + core * half, half), half)

    def prompt_cols(c):
        return pl.ds(pl.multiple_of(c // parts * PROMPT, PROMPT), PROMPT)

    def cont_cols(c):
        return pl.ds(pl.multiple_of(c * own_cont, own_cont), own_cont)

    def own_cols(c):
        return pl.ds(pl.multiple_of(c * own_tokens, own_tokens), own_tokens)

    at.meet()
    pending = []

    def start(copy):
        copy.start()
        pending.append(copy)
        return copy

    def landed(dst, recv_sem):
        remote(dst, dst, recv_sem, recv_sem, at.sibling).wait_recv()

    other = 1 - at.dp
    order = list(range(1, ncol)) + [0]
    for k in order:
        start(
            remote(
                gw_ref.at[:, half_rows(at.ahead(k), other)], sib_buf.at[k],
                sib_send.at[k], sib_recv.at[k], at.sibling,
            )
        )
    start(remote(sm_ref, sm_buf.at[0], sm_send.at[0], sm_recv.at[0], at.sibling))

    def local_copies():
        mine = rows_of(at.col)
        return [
            pltpu.make_async_copy(src, dst, local_sem.at[i])
            for i, (src, dst) in enumerate(
                (
                    (xb_ref.at[:, mine], xbo_ref.at[:, :, own_cols(at.col)]),
                    (gp_ref.at[mine], gpo_ref.at[part, :, prompt_cols(at.col)]),
                    (gc_ref.at[mine], gco_ref.at[:, cont_cols(at.col)]),
                )
            )
        ]

    for copy in local_copies():
        copy.start()
    for k in range(1, ncol):
        to = at.ahead(k)
        dev = at.col_dev(to)
        start(
            remote(
                xb_ref.at[:, rows_of(to)], xbo_ref.at[:, :, own_cols(at.col)],
                act_send.at[0, k], act_recv.at[0, k], dev,
            )
        )
        start(
            remote(
                gp_ref.at[rows_of(to)], gpo_ref.at[part, :, prompt_cols(at.col)],
                act_send.at[1, k], act_recv.at[1, k], dev,
            )
        )
        start(
            remote(
                gc_ref.at[rows_of(to)], gco_ref.at[:, cont_cols(at.col)],
                act_send.at[2, k], act_recv.at[2, k], dev,
            )
        )

    for k in order:
        landed(sib_buf.at[k], sib_recv.at[k])
        for row in range(gw_ref.shape[0]):
            here = gw_ref.at[row, half_rows(at.ahead(k), at.dp)]
            sib_buf[k, row] = (here[...].astype(F32) + sib_buf[k, row].astype(F32)).astype(BF16)
        for i, row in ((0, at.second), (1, at.both)):
            start(
                remote(
                    sib_buf.at[k, row], two_buf.at[i, k],
                    two_send.at[i, k], two_recv.at[i, k], at.second_dev,
                )
            )
    landed(sm_buf.at[0], sm_recv.at[0])
    sm_buf[3] = sm_ref[...] + sm_buf[0]
    start(remote(sm_buf.at[3], sm_buf.at[1], sm_send.at[1], sm_recv.at[1], at.second_dev))
    for k in order:
        landed(two_buf.at[1, k], two_recv.at[1, k])
        two_buf[1, k] = (sib_buf[k, at.first].astype(F32) + two_buf[1, k].astype(F32)).astype(BF16)
        start(
            remote(
                two_buf.at[1, k], one_buf.at[k], one_send.at[k], one_recv.at[k], at.first_dev
            )
        )
    landed(sm_buf.at[1], sm_recv.at[1])
    sm_buf[4] = sm_buf[3] + sm_buf[1]
    start(remote(sm_buf.at[4], sm_buf.at[2], sm_send.at[2], sm_recv.at[2], at.first_dev))
    for k in order:
        landed(two_buf.at[0, k], two_recv.at[0, k])
        landed(one_buf.at[k], one_recv.at[k])
        total = sib_buf[k, at.row].astype(F32) + two_buf[0, k].astype(F32) + one_buf[k].astype(F32)
        if k:
            two_buf[0, k] = total.astype(BF16)
            start(
                remote(
                    two_buf.at[0, k], col_buf.at[k],
                    col_send.at[k], col_recv.at[k], at.col_dev(at.ahead(k)),
                )
            )
        else:
            own_total = total
    landed(sm_buf.at[2], sm_recv.at[2])
    sm_buf[5] = sm_buf[4] + sm_buf[2]
    for k in range(1, ncol):
        to = at.ahead(k)
        start(
            remote(
                sm_buf.at[5, to], smc_buf.at[k], smc_send.at[k], smc_recv.at[k], at.col_dev(to)
            )
        )
    for k in range(1, ncol):
        landed(col_buf.at[k], col_recv.at[k])
        own_total = own_total + col_buf[k].astype(F32)
    my_rows = pl.ds(pl.multiple_of(at.dp * half, half), half)
    gwo_ref[my_rows] = own_total
    start(remote(gwo_ref.at[my_rows], gwo_ref.at[my_rows], fin_send, fin_recv, at.sibling))
    small = sm_buf[5, at.col]
    for k in range(1, ncol):
        landed(smc_buf.at[k], smc_recv.at[k])
        small = small + smc_buf[k]
    smo_ref[...] = small
    landed(gwo_ref.at[pl.ds(pl.multiple_of(other * half, half), half)], fin_recv)
    for k in range(1, ncol):
        frm = at.behind(k)
        landed(xbo_ref.at[:, :, own_cols(frm)], act_recv.at[0, k])
        landed(gpo_ref.at[frm % parts, :, prompt_cols(frm)], act_recv.at[1, k])
        landed(gco_ref.at[:, cont_cols(frm)], act_recv.at[2, k])
    for copy in pending:
        copy.wait_send()
    for copy in local_copies():
        copy.wait()


def scatter_all(xb, gp, gc, gw, small, ncol, parts):
    nrow, full, width = gw.shape
    feat = full // ncol
    half = feat // 2
    groups = ncol // parts
    own_tokens, own_cont = xb.shape[2], gc.shape[1]
    dma = pltpu.SemaphoreType.DMA
    anywhere = pl.BlockSpec(memory_space=pl.ANY)
    vmem = pl.BlockSpec(memory_space=pltpu.VMEM)
    small_shape = small.shape
    return pl.pallas_call(
        functools.partial(scatter_kernel, ncol, parts),
        out_shape=(
            jax.ShapeDtypeStruct((2, feat, ncol * own_tokens), BF16),
            jax.ShapeDtypeStruct((parts, feat, groups * PROMPT), BF16),
            jax.ShapeDtypeStruct((feat, ncol * own_cont), BF16),
            jax.ShapeDtypeStruct((feat, width), F32),
            jax.ShapeDtypeStruct(small_shape[1:], F32),
        ),
        in_specs=[anywhere, anywhere, anywhere, vmem, vmem],
        out_specs=[anywhere, anywhere, anywhere, vmem, vmem],
        scratch_shapes=[
            pltpu.VMEM((ncol, nrow, half, width), BF16),
            pltpu.VMEM((2, ncol, half, width), BF16),
            pltpu.VMEM((ncol, half, width), BF16),
            pltpu.VMEM((ncol, half, width), BF16),
            pltpu.VMEM((6,) + small_shape, F32),
            pltpu.VMEM((ncol,) + small_shape[1:], F32),
            dma((3, ncol)), dma((3, ncol)), dma((ncol,)), dma((ncol,)), dma((2, ncol)), dma((2, ncol)),
            dma((ncol,)), dma((ncol,)), dma((ncol,)), dma((ncol,)), dma(()), dma(()),
            dma((3,)), dma((3,)), dma((ncol,)), dma((ncol,)), dma((3,)),
        ],
        compiler_params=pltpu.CompilerParams(
            collective_id=1, has_side_effects=True, vmem_limit_bytes=56 << 20
        ),
        name="scatter_all",
    )(xb, gp, gc, gw, small)


def to_parts(array_in, parts):
    lead = array_in.shape[:-1]
    groups = array_in.shape[-1] // GROUP
    split = array_in.reshape(lead + (groups, GROUP))
    prompt = split[..., :PROMPT].reshape(lead + (groups, 2, parts, BLOCK))
    prompt = jnp.stack([prompt[..., 0, :, :], prompt[..., 1, ::-1, :]], axis=-2)
    prompt = prompt.reshape(lead + (groups, parts, PROMPT // parts))
    cont = split[..., PROMPT:].reshape(lead + (groups, parts, NCONT * CONT // parts))
    return jnp.concatenate([prompt, cont], axis=-1).reshape(array_in.shape)


def from_parts(array_in, parts):
    lead = array_in.shape[:-1]
    groups = array_in.shape[-1] // GROUP
    split = array_in.reshape(lead + (groups, parts, GROUP // parts))
    prompt = split[..., : PROMPT // parts].reshape(lead + (groups, parts, 2, BLOCK))
    prompt = jnp.concatenate(
        [prompt[..., :, 0, :], prompt[..., ::-1, 1, :]], axis=-2
    ).reshape(lead + (groups, PROMPT))
    cont = split[..., PROMPT // parts :].reshape(lead + (groups, NCONT * CONT))
    return jnp.concatenate([prompt, cont], axis=-1).reshape(array_in.shape)


def norm_forward(summed, gain_vec, bias_vec):
    average = jnp.mean(summed, axis=0, keepdims=True)
    squares = jnp.mean(summed * summed, axis=0, keepdims=True)
    inv_scale = lax.rsqrt(squares - average * average + EPS_NORM)
    unit_val = (summed - average) * inv_scale
    return (unit_val * gain_vec + bias_vec, unit_val, inv_scale)


def norm_backward(upstream, unit_val, inv_scale, gain_vec):
    scaled = upstream * gain_vec
    first = jnp.mean(scaled, axis=0, keepdims=True)
    second = jnp.mean(scaled * unit_val, axis=0, keepdims=True)
    d_summed = inv_scale * (scaled - first - unit_val * second)
    sums = [jnp.sum(v, axis=1, keepdims=True) for v in (upstream * unit_val, upstream)]
    return (d_summed, *sums)


def dot_tn(lhs, rhs):
    return lax.dot_general(lhs, rhs, (((0,), (0,)), ((), ())), preferred_element_type=F32)


def dot_nn(lhs, rhs):
    return lax.dot_general(lhs, rhs, (((1,), (0,)), ((), ())), preferred_element_type=F32)


def dot_nt(lhs, rhs):
    return lax.dot_general(lhs, rhs, (((1,), (1,)), ((), ())), preferred_element_type=F32)


def iota(shape, axis):
    return lax.broadcasted_iota(jnp.int32, shape, axis)


def fold(array_in, op):
    return op(array_in.reshape(array_in.shape[0] // 8, 8, array_in.shape[1]), axis=0)


KEYS = 256
PAIR = 2 * BLOCK


class Layer:
    def __init__(self, part, parts, lens, total_tokens, count):
        self.part, self.parts = part, parts
        self.lens = lens
        self.total_tokens, self.count = total_tokens, count
        slot = iota((1, BLOCK), 1)
        low, high = part * BLOCK + slot, (2 * parts - 1 - part) * BLOCK + slot
        last = lens[0] - 1
        self.bound = jnp.concatenate(
            [jnp.minimum(low, last), jnp.minimum(high, last), jnp.full((1, PAIR), last, jnp.int32)],
            axis=1,
        )
        live = [low < lens[0], high < lens[0]] + [slot < n for n in lens[1:]]
        self.live = jnp.concatenate([m.astype(F32) for m in live], axis=1)

    def own_columns(self):
        low = pl.ds(pl.multiple_of(self.part * BLOCK, BLOCK), BLOCK)
        high = pl.ds(pl.multiple_of((2 * self.parts - 1 - self.part) * BLOCK, BLOCK), BLOCK)
        return low, high

    def project(self, xp, xc, w, xo, xt, kv, kvt, qt):
        low, high = self.own_columns()
        xo[:, :BLOCK] = xp[:, low]
        xo[:, BLOCK:PAIR] = xp[:, high]
        xo[:, PAIR:] = xc[...]
        xt[:PROMPT] = xp[...].T
        xt[PROMPT:] = xc[...].T

        def step(r, carry):
            wq, wkv = w[r, :, :BLOCK], w[r, :, BLOCK : 3 * BLOCK]
            cols = pl.ds(pl.multiple_of(r * PAIR, PAIR), PAIR)
            kv[:, cols] = dot_nn(xt[...], wkv).astype(BF16)
            kvt[r, :, :PROMPT] = dot_tn(wkv, xp[...]).astype(BF16)
            kvt[r, :, PROMPT:] = dot_tn(wkv, xc[...]).astype(BF16)
            rows = pl.ds(pl.multiple_of(r * BLOCK, BLOCK), BLOCK)
            qt[rows] = (dot_tn(wq, xo[...]).astype(BF16).astype(F32) * HD ** (-0.5)).astype(BF16)
            return carry

        lax.fori_loop(0, w.shape[0], step, 0)

    def one_head(self, array_in, head):
        zeros = jnp.zeros((HD, array_in.shape[1]), array_in.dtype)
        mine = array_in[head * HD : (head + 1) * HD]
        return jnp.concatenate([mine, zeros] if head == 0 else [zeros, mine], axis=0)

    def masked(self, score, first_key, columns):
        keys = iota(score.shape, 0) + first_key
        return jnp.where(keys <= self.bound[:, columns], score, NEG_FILL)

    def masked_own(self, score, n):
        keys = iota(score.shape, 0)
        return jnp.where(
            (keys <= iota(score.shape, 1)) & (keys < self.lens[1 + n]), score, NEG_FILL
        )

    def attend(self, kv, kvt, qt, att, lse, s_scr, p_scr, between=None):
        def step(r, carry):
            k_cols = pl.ds(pl.multiple_of(r * PAIR, PAIR), BLOCK)
            q_pair = qt[pl.ds(pl.multiple_of(r * BLOCK, BLOCK), BLOCK)]
            for head in range(2):
                query = self.one_head(q_pair, head)
                v_rows = slice(BLOCK + head * HD, BLOCK + (head + 1) * HD)
                for b in range(2):
                    columns = slice(b * PAIR, (b + 1) * PAIR)
                    q_here = query[:, columns]
                    top = jnp.full((8, PAIR), NEG_FILL, F32)
                    for first in range(0, PROMPT, KEYS):
                        score = dot_nn(kv[first : first + KEYS, k_cols], q_here)
                        score = self.masked(score, first, columns)
                        s_scr[head, first : first + KEYS] = score
                        top = jnp.maximum(top, fold(score, jnp.max))
                    own_scores = []
                    if b == 1:
                        for n in range(2):
                            keys = slice(PROMPT + n * BLOCK, PROMPT + (n + 1) * BLOCK)
                            score = dot_nn(kv[keys, k_cols], q_here[:, n * BLOCK : (n + 1) * BLOCK])
                            own_scores.append(self.masked_own(score, n))
                        own_top = [fold(score, jnp.max) for score in own_scores]
                        top = jnp.maximum(top, jnp.concatenate(own_top, axis=1))
                    top = jnp.max(top, axis=0, keepdims=True)
                    total = jnp.zeros((8, PAIR), F32)
                    for first in range(0, PROMPT, KEYS):
                        prob = jnp.exp(s_scr[head, first : first + KEYS] - top)
                        total = total + fold(prob, jnp.sum)
                        p_scr[head, first : first + KEYS] = prob.astype(BF16)
                    out = dot_nn(kvt[r, v_rows, :PROMPT], p_scr[head])
                    if b == 1:
                        own_out, own_total = [], []
                        for n in range(2):
                            lanes = slice(n * BLOCK, (n + 1) * BLOCK)
                            prob = jnp.exp(own_scores[n] - top[:, lanes])
                            own_total.append(fold(prob, jnp.sum))
                            keys = slice(PROMPT + n * BLOCK, PROMPT + (n + 1) * BLOCK)
                            own_out.append(dot_nn(kvt[r, v_rows, keys], prob.astype(BF16)))
                        total = total + jnp.concatenate(own_total, axis=1)
                        out = out + jnp.concatenate(own_out, axis=1)
                    total = jnp.sum(total, axis=0, keepdims=True)
                    rows = pl.ds(pl.multiple_of(r * BLOCK + head * HD, HD), HD)
                    att[rows, columns] = (out / total).astype(BF16)
                    lse[pl.ds(2 * r + head, 1), columns] = top + jnp.log(total)
            if between is not None:
                between(r)
            return carry

        lax.fori_loop(0, kvt.shape[0], step, 0)

    def attend_back(
        self, kv, kvt, qt, lse, delta, d_att, dkvt, dqt, p_scr, ds_scr, between=None, grads=None
    ):
        def step(r, carry):
            k_cols = pl.ds(pl.multiple_of(r * PAIR, PAIR), BLOCK)
            v_cols = pl.ds(pl.multiple_of(r * PAIR + BLOCK, BLOCK), BLOCK)
            pair = pl.ds(pl.multiple_of(r * BLOCK, BLOCK), BLOCK)
            q_pair, d_pair = qt[pair], d_att[pair]
            for head in range(2):
                query, d_out = self.one_head(q_pair, head), self.one_head(d_pair, head)
                q_mine = q_pair[head * HD : (head + 1) * HD]
                d_mine = d_pair[head * HD : (head + 1) * HD]
                k_rows = slice(head * HD, (head + 1) * HD)
                v_rows = slice(BLOCK + head * HD, BLOCK + (head + 1) * HD)
                norm = lse[pl.ds(2 * r + head, 1)]
                dlt = delta[pl.ds(2 * r + head, 1)]
                for b in range(2):
                    columns = slice(b * PAIR, (b + 1) * PAIR)
                    for first in range(0, PROMPT, KEYS):
                        keys = slice(first, first + KEYS)
                        score = dot_nn(kv[keys, k_cols], query[:, columns])
                        score = self.masked(score, first, columns)
                        prob = jnp.exp(score - norm[:, columns])
                        dprob = dot_nn(kv[keys, v_cols], d_out[:, columns])
                        p_scr[head, keys, columns] = prob.astype(BF16)
                        ds_scr[head, keys, columns] = (prob * (dprob - dlt[:, columns])).astype(BF16)
                d_query = dot_nn(kvt[r, k_rows, :PROMPT], ds_scr[head])
                own_dq = [jnp.zeros((HD, PAIR), F32)]
                for n in range(2):
                    keys = slice(PROMPT + n * BLOCK, PROMPT + (n + 1) * BLOCK)
                    lanes = slice(PAIR + n * BLOCK, PAIR + (n + 1) * BLOCK)
                    score = self.masked_own(dot_nn(kv[keys, k_cols], query[:, lanes]), n)
                    prob = jnp.exp(score - norm[:, lanes])
                    dprob = dot_nn(kv[keys, v_cols], d_out[:, lanes])
                    d_score = (prob * (dprob - dlt[:, lanes])).astype(BF16)
                    own_dq.append(dot_nn(kvt[r, k_rows, keys], d_score))
                    dkvt[r, k_rows, keys] = dot_nt(q_mine[:, lanes], d_score).astype(BF16)
                    dkvt[r, v_rows, keys] = dot_nt(d_mine[:, lanes], prob.astype(BF16)).astype(BF16)
                d_query = (d_query + jnp.concatenate(own_dq, axis=1)) * HD ** (-0.5)
                rows = pl.ds(pl.multiple_of(r * BLOCK + head * HD, HD), HD)
                dqt[rows] = d_query.astype(BF16)
                dkvt[r, k_rows, :PROMPT] = dot_nt(q_mine, ds_scr[head]).astype(BF16)
                dkvt[r, v_rows, :PROMPT] = dot_nt(d_mine, p_scr[head]).astype(BF16)
            if grads is not None:
                self.projection_grads(r, pair, *grads, dkvt, dqt)
            if between is not None:
                between(r)
            return carry

        lax.fori_loop(0, kvt.shape[0], step, 0)

    def projection_grads(self, r, rows, xp, xc, xo, gw, dkvt, dqt):
        gw[r, :, :BLOCK] = dot_nt(xo[...], dqt[rows]).astype(BF16)
        gw[r, :, BLOCK : 3 * BLOCK] = (
            dot_nt(xp[...], dkvt[r, :, :PROMPT]) + dot_nt(xc[...], dkvt[r, :, PROMPT:])
        ).astype(BF16)

    def input_grads(self, xp, xc, xo, w, dkvt, dqt, dsa, gp, gc, gw, dx, dxo):
        for r in range(w.shape[0]):
            wq, wkv = w[r, :, :BLOCK], w[r, :, BLOCK : 3 * BLOCK]
            part = dot_nn(wkv, dkvt[r])
            rows = slice(r * BLOCK, (r + 1) * BLOCK)
            own = dot_nn(wq, dqt[rows])
            if r == 0:
                dx[...] = part
                dxo[...] = dsa[...] + own
            else:
                dx[...] += part
                dxo[...] += own
            self.projection_grads(r, rows, xp, xc, xo, gw, dkvt, dqt)
        low, high = self.own_columns()
        dx[:, low] += dxo[:, :BLOCK]
        dx[:, high] += dxo[:, BLOCK:PAIR]
        gp[...] = dx[:, :PROMPT].astype(BF16)
        gc[...] = (dx[:, PROMPT:] + dxo[:, PAIR:]).astype(BF16)

    def middle(
        self, xo, tdo, w, vec, att, xb, gw, sm, d_att, delta, dsa, hid, acc, ba,
        tokens_ready=None, outputs_ready=None,
    ):
        nrow, full = w.shape[0], w.shape[1]
        ff = (w.shape[2] - 4 * BLOCK) // 2
        up, down = slice(4 * BLOCK, 4 * BLOCK + ff), slice(4 * BLOCK + ff, 4 * BLOCK + 2 * ff)
        gain_a, bias_a, gain_f, bias_f = (vec[:, i : i + 1].astype(F32) for i in range(4))
        w_o = jnp.concatenate([w[r, :, 3 * BLOCK : 4 * BLOCK] for r in range(nrow)], axis=1)
        ba[...] = dot_nn(w_o, att[...])
        x_one, unit_a, inv_a = norm_forward(xo[...].astype(F32) + ba[...], gain_a, bias_a)
        x_low = x_one.astype(BF16)
        x_low_t = x_low.T
        acc[...] = jnp.zeros_like(acc)

        def up_down(r, carry):
            pre = dot_nn(x_low_t, w[r, :, up])
            hidden = jnp.maximum(pre, 0.0).astype(BF16)
            hid[r] = hidden
            acc[...] += dot_nt(w[r, :, down], hidden)
            return carry

        lax.fori_loop(0, nrow, up_down, 0)
        branch_f = acc[...]
        x_two, unit_f, inv_f = norm_forward(x_one + branch_f, gain_f, bias_f)
        branch = ba[...] + branch_f
        xb[0] = x_two.astype(BF16)
        xb[1] = branch.astype(BF16)
        if outputs_ready is not None:
            outputs_ready()
            tokens_ready()
        diff_x = x_two - tdo[0].astype(F32)
        diff_y = branch + tdo[1].astype(F32)
        loss = jnp.sum(self.live * (diff_x * diff_x + diff_y * diff_y))
        weight = self.live * (self.total_tokens / self.count)
        grad_y = diff_y * weight
        d_sum_f, gain_grad_f, bias_grad_f = norm_backward(diff_x * weight, unit_f, inv_f, gain_f)
        d_branch_f = (d_sum_f + grad_y).astype(BF16)
        d_branch_t = d_branch_f.T
        acc[...] = d_sum_f

        def back(r, carry):
            hidden = hid[r]
            d_hidden = dot_nn(d_branch_t, w[r, :, down])
            d_pre = jnp.where(hidden.astype(F32) > 0, d_hidden, 0.0).astype(BF16)
            gw[r, :, up] = dot_nn(x_low, d_pre).astype(BF16)
            gw[r, :, down] = dot_nn(d_branch_f, hidden).astype(BF16)
            acc[...] += dot_nt(w[r, :, up], d_pre)
            return carry

        lax.fori_loop(0, nrow, back, 0)
        d_sum_a, gain_grad_a, bias_grad_a = norm_backward(acc[...], unit_a, inv_a, gain_a)
        dsa[...] = d_sum_a
        d_branch_a = (d_sum_a + grad_y).astype(BF16)
        for r in range(nrow):
            rows = slice(r * BLOCK, (r + 1) * BLOCK)
            attended = att[rows]
            gw[r, :, 3 * BLOCK : 4 * BLOCK] = dot_nt(d_branch_a, attended).astype(BF16)
            d_here = dot_tn(w[r, :, 3 * BLOCK : 4 * BLOCK], d_branch_a).astype(BF16)
            d_att[rows] = d_here
            product = attended.astype(F32) * d_here.astype(F32)
            for head in range(2):
                delta[2 * r + head : 2 * r + head + 1] = jnp.sum(
                    product[head * HD : (head + 1) * HD], axis=0, keepdims=True
                )
        lane = iota((full, 128), 1)
        sums = jnp.zeros((full, 128), F32)
        for i, vector in enumerate((gain_grad_a, bias_grad_a, gain_grad_f, bias_grad_f)):
            sums = jnp.where(lane == i, vector, sums)
        sums = jnp.where(lane == 4, loss, sums)
        sums = sums.T[:8]
        for s in range(sm.shape[0]):
            sm[s] = sums[:, s * sm.shape[2] : (s + 1) * sm.shape[2]]


def layer_kernel(
    parts, lens_ref, len_table, xp, xc, tdo, w, vec, xb, gp, gc, gw, sm,
    xo, xt, kv, kvt, qt, att, lse, delta, d_att, dkvt, dqt, s_scr, pf_scr, p_scr, ds_scr,
    dsa, hid, acc, ba, dx,
):
    col = lax.axis_index("col")
    groups = lax.axis_size("col") // parts
    chip = lax.axis_index("dp") * lax.axis_size("row") + lax.axis_index("row")
    group = chip * groups + col // parts
    part = col % parts
    lens = [lens_ref[group, 0]] + [lens_ref[group, 1 + 2 * part + n] for n in range(2)]
    count = jnp.sum(len_table[...].astype(F32))
    layer = Layer(part, parts, lens, lens_ref.shape[0] * GROUP, count)
    layer.project(xp, xc, w, xo, xt, kv, kvt, qt)
    layer.attend(kv, kvt, qt, att, lse, s_scr, pf_scr)
    layer.middle(xo, tdo, w, vec, att, xb, gw, sm, d_att, delta, dsa, hid, acc, ba)
    layer.attend_back(kv, kvt, qt, lse, delta, d_att, dkvt, dqt, p_scr, ds_scr)
    layer.input_grads(xp, xc, xo, w, dkvt, dqt, dsa, gp, gc, gw, dx, acc)


def run_layer(lengths, xp, xc, tdo, weights, vec, parts):
    nrow, full, width = weights.shape
    own, keys = tdo.shape[2], xp.shape[1] + xc.shape[1]
    heads = full // HD
    vmem = pl.BlockSpec(memory_space=pltpu.VMEM)
    return pl.pallas_call(
        functools.partial(layer_kernel, parts),
        out_shape=(
            jax.ShapeDtypeStruct((2, full, own), BF16),
            jax.ShapeDtypeStruct(xp.shape, BF16),
            jax.ShapeDtypeStruct(xc.shape, BF16),
            jax.ShapeDtypeStruct(weights.shape, BF16),
            jax.ShapeDtypeStruct((1, 8, full), F32),
        ),
        in_specs=[pl.BlockSpec(memory_space=pltpu.SMEM)] + [vmem] * 6,
        out_specs=[vmem] * 5,
        scratch_shapes=[
            pltpu.VMEM((full, own), BF16),
            pltpu.VMEM((keys, full), BF16),
            pltpu.VMEM((keys, nrow * PAIR), BF16),
            pltpu.VMEM((nrow, PAIR, keys), BF16),
            pltpu.VMEM((full, own), BF16),
            pltpu.VMEM((full, own), BF16),
            pltpu.VMEM((heads, own), F32),
            pltpu.VMEM((heads, own), F32),
            pltpu.VMEM((full, own), BF16),
            pltpu.VMEM((nrow, PAIR, keys), BF16),
            pltpu.VMEM((full, own), BF16),
            pltpu.VMEM((2, PROMPT, PAIR), F32),
            pltpu.VMEM((2, PROMPT, PAIR), BF16),
            pltpu.VMEM((2, PROMPT, own), BF16),
            pltpu.VMEM((2, PROMPT, own), BF16),
            pltpu.VMEM((full, own), F32),
            pltpu.VMEM((nrow, own, (width - 4 * BLOCK) // 2), BF16),
            pltpu.VMEM((full, own), F32),
            pltpu.VMEM((full, own), F32),
            pltpu.VMEM((full, keys), F32),
        ],
        compiler_params=pltpu.CompilerParams(vmem_limit_bytes=60 << 20),
        name="layer",
    )(lengths, lengths, xp, xc, tdo, weights, vec)


class Line:
    def __init__(self, c):
        self.c = c
        self.mid = c * (3 - c) // 2 == 1
        self.end = c * (3 - c) // 2 == 0
        inner = c * (3 - c) // 2
        far = 3 * (1 - c // 2)
        one = c - 1 + 2 * ((4 - c) // 4)
        self.near = [c, one, 6 - c - one - far, far]
        self.pass_to = [None, c + 1, c - 1, 3 * (c - 1)]
        last = 1 + c % 2
        second = 6 - c - far - last
        self.far = [far, second, last, c]
        self.sum_to = [last, last + inner * (second - last), last]
        self.slot = [far, second + 4 * inner * (2 - c), last + c // 2 * (4 - last)]


class Traffic:
    def __init__(self, at):
        self.at = at
        self.pending = {}

    def start(self, key, make, cond=None):
        if cond is None:
            make().start()
        else:
            pl.when(cond)(lambda: make().start())
        self.pending[key] = (make, cond)

    def send(self, key, src, dst, send_sem, recv_sem, device, cond=None):
        self.start(key, lambda: remote(src(), dst(), send_sem(), recv_sem(), device), cond)

    def landed(self, dst, recv_sem):
        remote(dst, dst, recv_sem, recv_sem, self.at.sibling).wait_recv()

    def drain(self):
        for make, cond in self.pending.values():
            if cond is None:
                make().wait_send()
            else:
                pl.when(cond)(lambda make=make: make().wait_send())


def at_index(ref, *index):
    return ref.at[index]


class WeightGather:
    def __init__(self, tag, traffic, line, w, cols, feat, sems):
        self.tag, self.t, self.at, self.line = tag, traffic, traffic.at, line
        self.w, self.cols, self.feat = w, cols, feat
        self.col_s, self.col_r, self.one_s, self.one_r, self.two_s, self.two_r, self.sib_s, self.sib_r = sems

    def piece(self, row, c, core):
        half = self.feat // 2
        rows = pl.ds(pl.multiple_of(c * self.feat + core * half, half), half)
        return self.w.at[row, rows, self.cols]

    def move(self, key, row, c, send_sem, recv_sem, device, cond=None):
        here = functools.partial(self.piece, row, c, self.at.dp)
        self.t.send(
            (self.tag,) + key, here, here,
            lambda: at_index(*send_sem), lambda: at_index(*recv_sem), device, cond,
        )

    def own(self):
        at, line = self.at, self.line
        c = line.c
        for i in range(2):
            self.move(
                ("own", i), at.row, c, (self.col_s, i), (self.col_r, c),
                at.col_dev(line.near[1 + i]), line.mid if i else None,
            )
        self.rows(0)

    def rows(self, j):
        at, c = self.at, self.line.near[j]
        self.move(("one", j), at.row, c, (self.one_s, j), (self.one_r, j), at.first_dev)
        self.move(("two", j), at.row, c, (self.two_s, 0, j), (self.two_r, 0, j), at.second_dev)
        if j:
            self.move(("sib", j), at.row, c, (self.sib_s, 0, j), (self.sib_r, 0, j), at.sibling)

    def arrive(self, j):
        at, c = self.at, self.line.near[j]
        self.t.landed(self.piece(at.row, c, at.dp), self.col_r.at[c])
        self.move(
            ("pass", j), at.row, c, (self.col_s, 1 + j), (self.col_r, c),
            at.col_dev(self.line.pass_to[j]), self.line.mid,
        )
        self.rows(j)

    def first(self, j):
        at, c = self.at, self.line.near[j]
        self.t.landed(self.piece(at.first, c, at.dp), self.one_r.at[j])
        self.move(("far", j), at.first, c, (self.two_s, 1, j), (self.two_r, 1, j), at.second_dev)
        self.move(("sib1", j), at.first, c, (self.sib_s, 1, j), (self.sib_r, 1, j), at.sibling)

    def second(self, j):
        at, c = self.at, self.line.near[j]
        for i, row in ((0, at.second), (1, at.both)):
            self.t.landed(self.piece(row, c, at.dp), self.two_r.at[i, j])
            self.move(
                ("sib2", i, j), row, c, (self.sib_s, 2 + i, j), (self.sib_r, 2 + i, j), at.sibling
            )

    def finish(self):
        at = self.at
        for j in range(4):
            c, core = self.line.near[j], 1 - at.dp
            if j:
                self.t.landed(self.piece(at.row, c, core), self.sib_r.at[0, j])
            self.t.landed(self.piece(at.second, c, core), self.sib_r.at[1, j])
            self.t.landed(self.piece(at.first, c, core), self.sib_r.at[2, j])
            self.t.landed(self.piece(at.both, c, core), self.sib_r.at[3, j])


class WeightScatter:
    def __init__(self, tag, traffic, line, gw, cols, feat, sib, two, one, zb, out, sems):
        self.tag, self.t, self.at, self.line = tag, traffic, traffic.at, line
        self.gw, self.cols, self.feat = gw, cols, feat
        self.sib, self.two, self.one, self.zb, self.out = sib, two, one, zb, out
        self.sib_s, self.sib_r, self.two_s, self.two_r, self.one_s, self.one_r = sems[:6]
        self.col_s, self.col_r, self.fin_s, self.fin_r = sems[6:]

    def rows(self, i, core):
        half = self.feat // 2
        return pl.ds(pl.multiple_of(self.line.far[i] * self.feat + core * half, half), half)

    def begin(self, i):
        self.t.send(
            (self.tag, "sib", i),
            lambda: self.gw.at[:, self.rows(i, 1 - self.at.dp), self.cols],
            lambda: self.sib.at[i],
            lambda: self.sib_s.at[i], lambda: self.sib_r.at[i], self.at.sibling,
        )

    def step1(self, i):
        at = self.at
        self.t.landed(self.sib.at[i], self.sib_r.at[i])
        for row in range(4):
            here = self.gw[row, self.rows(i, at.dp), self.cols]
            self.sib[i, row] = (here.astype(F32) + self.sib[i, row].astype(F32)).astype(BF16)
        for n, row in ((1, at.both), (0, at.second)):
            self.t.send(
                (self.tag, "two", n, i),
                lambda row=row: self.sib.at[i, row],
                lambda n=n: self.two.at[n, i],
                lambda n=n: self.two_s.at[n, i], lambda n=n: self.two_r.at[n, i], at.second_dev,
            )

    def step2(self, i):
        at = self.at
        self.t.landed(self.two.at[1, i], self.two_r.at[1, i])
        total = self.sib[i, at.first].astype(F32) + self.two[1, i].astype(F32)
        self.two[1, i] = total.astype(BF16)
        self.t.send(
            (self.tag, "one", i),
            lambda: self.two.at[1, i], lambda: self.one.at[i],
            lambda: self.one_s.at[i], lambda: self.one_r.at[i], at.first_dev,
        )

    def total(self, i):
        near = self.sib[i, self.at.row].astype(F32) + self.two[0, i].astype(F32)
        return near + self.one[i].astype(F32)

    def step3(self, i):
        line = self.line
        self.t.landed(self.two.at[0, i], self.two_r.at[0, i])
        self.t.landed(self.one.at[i], self.one_r.at[i])
        if i < 3:

            @pl.when(line.mid)
            def _():
                self.t.landed(self.zb.at[line.far[i]], self.col_r.at[line.far[i]])
                total = self.total(i) + self.zb[line.far[i]].astype(F32)
                self.two[0, i] = total.astype(BF16)

            @pl.when(line.end)
            def _():
                self.two[0, i] = self.total(i).astype(BF16)

            self.t.send(
                (self.tag, "col", i),
                lambda: self.two.at[0, i], lambda: self.zb.at[line.slot[i]],
                lambda: self.col_s.at[i], lambda: self.col_r.at[line.slot[i]],
                self.at.col_dev(line.sum_to[i]),
            )
            return
        half = self.feat // 2
        mine = pl.ds(pl.multiple_of(self.at.dp * half, half), half)
        self.out[mine] = self.total(i)
        for slot, cond in ((line.c, line.c > 0), (4, line.c < 3)):

            @pl.when(cond)
            def _(slot=slot):
                self.t.landed(self.zb.at[slot], self.col_r.at[slot])
                self.out[mine] += self.zb[slot].astype(F32)

        self.t.send(
            (self.tag, "fin"),
            lambda: self.out.at[mine], lambda: self.out.at[mine],
            lambda: self.fin_s, lambda: self.fin_r, self.at.sibling,
        )

    def finish(self):
        half = self.feat // 2
        other = pl.ds(pl.multiple_of((1 - self.at.dp) * half, half), half)
        self.t.landed(self.out.at[other], self.fin_r)


def step_kernel(
    parts, lens_ref, len_table, x_ref, y_ref, tx_ref, ty_ref, wq_ref, wo_ref, wu_ref, wd_ref, vec_ref,
    xout_ref, yout_ref, gx_ref, gy_ref, gq_ref, go_ref, gu_ref, gd_ref, gv_ref,
    w, gw, xp, xc, xo, xt, kv, kvt, qt, att, lse, delta, d_att, s_scr, pf_scr, p_scr, ds_scr,
    dsa, hid, acc, ba, dx, dxo, tdp, tdo, xb, xbo, vrow, gpb, gxz, gcb, gco, sm, smb, smz,
    sib1, two1, one1, zb1, out1, sib2, two2, one2, zb2, out2,
    xs, xr, cs, cr, ts, tr, vs, vr, bs, br, gs, gr, ks, kr, ss, sr, zs, zr, *wsems,
):
    ncol = 4
    at = Places(ncol)
    t = Traffic(at)
    c = at.col
    line = Line(c)
    feat = x_ref.shape[0]
    own = xo.shape[1]
    cont = xc.shape[1]
    qkv, rest = slice(0, 3 * BLOCK), slice(3 * BLOCK, w.shape[2])

    def rows_of(s):
        return pl.ds(pl.multiple_of(s * feat, feat), feat)

    def own_cols(s):
        return pl.ds(pl.multiple_of(s * own, own), own)

    def cont_cols(s, first=0):
        return pl.ds(pl.multiple_of(first + s * cont, cont), cont)

    mine = rows_of(c)
    at.meet()
    gather1 = WeightGather("w1", t, line, w, qkv, feat, wsems[0:8])
    gather2 = WeightGather("w2", t, line, w, rest, feat, wsems[8:16])

    w[at.row, mine, qkv] = wq_ref[...]
    gather1.own()
    for i in range(2):
        t.send(
            ("x", i),
            lambda: x_ref.at[:, :PROMPT], lambda: xp.at[mine],
            lambda i=i: xs.at[i], lambda: xr.at[c],
            at.col_dev(line.near[1 + i]), line.mid if i else None,
        )
    for k in range(1, ncol):
        to = at.ahead(k)
        t.send(
            ("xc", k),
            lambda to=to: x_ref.at[:, cont_cols(to, PROMPT)], lambda: xc.at[mine],
            lambda k=k: cs.at[k], lambda k=k: cr.at[k], at.col_dev(to),
        )
    local = [
        lambda: pltpu.make_async_copy(x_ref.at[:, :PROMPT], xp.at[mine], cs.at[0]),
        lambda: pltpu.make_async_copy(x_ref.at[:, cont_cols(c, PROMPT)], xc.at[mine], cr.at[0]),
    ]
    for make in local:
        make().start()
    vrow[c] = vec_ref[...]
    for k in range(1, ncol):
        to = at.ahead(k)
        t.send(
            ("v", k),
            lambda: vrow.at[c], lambda: vrow.at[c],
            lambda k=k: vs.at[k], lambda k=k: vr.at[k], at.col_dev(to),
        )
    w[at.row, mine, 3 * BLOCK : 4 * BLOCK] = wo_ref[...].T
    ff = wu_ref.shape[1]
    w[at.row, mine, 4 * BLOCK : 4 * BLOCK + ff] = wu_ref[...]
    w[at.row, mine, 4 * BLOCK + ff :] = wd_ref[...].T
    gather2.own()

    pieces = []
    for p in range(parts):
        pieces.append((p * own, p * BLOCK, BLOCK))
        pieces.append((p * own + BLOCK, (2 * parts - 1 - p) * BLOCK, BLOCK))
        pieces.append((p * own + PAIR, PROMPT + p * cont, cont))
    for to, frm, width in pieces:
        tdp[0, :, to : to + width] = tx_ref[:, frm : frm + width]
        y_here = y_ref[:, frm : frm + width].astype(F32)
        tdp[1, :, to : to + width] = (y_here - ty_ref[:, frm : frm + width].astype(F32)).astype(BF16)

    def x_arrive(j):
        s = line.near[j]
        t.landed(xp.at[rows_of(s)], xr.at[s])
        t.send(
            ("xpass", j),
            lambda: xp.at[rows_of(s)], lambda: xp.at[rows_of(s)],
            lambda: xs.at[1 + j], lambda: xr.at[s],
            at.col_dev(line.pass_to[j]), line.mid,
        )

    gather1.arrive(1)
    gather1.arrive(2)
    gather1.first(0)
    gather1.arrive(3)
    x_arrive(1)
    x_arrive(2)
    for j in range(1, 4):
        gather1.first(j)
    for j in range(4):
        gather1.second(j)
    gather2.arrive(1)
    gather2.arrive(2)
    gather2.first(0)
    x_arrive(3)
    for k in range(1, ncol):
        t.landed(xc.at[rows_of(at.behind(k))], cr.at[k])
    for make in local:
        make().wait()
    gather1.finish()

    group = at.dp * lax.axis_size("row") + at.row
    lens = [lens_ref[group, 0]] + [lens_ref[group, 1 + 2 * c + n] for n in range(2)]
    count = jnp.sum(len_table[...].astype(F32))
    total_tokens = lens_ref.shape[0] * GROUP
    layer = Layer(c, parts, lens, total_tokens, count)
    layer.project(xp, xc, w, xo, xt, kv, kvt, qt)

    gather2.arrive(3)
    for k in range(1, ncol):
        to = at.ahead(k)
        t.send(
            ("td", k),
            lambda to=to: tdp.at[:, :, own_cols(to)], lambda: tdo.at[:, mine],
            lambda k=k: ts.at[k], lambda k=k: tr.at[k], at.col_dev(to),
        )
    tdo[:, mine] = tdp[:, :, own_cols(c)]

    def forward_steps(r):
        @pl.when(r == 0)
        def _():
            gather2.first(1)
            gather2.first(2)

        @pl.when(r == 1)
        def _():
            gather2.second(0)
            gather2.second(1)

        @pl.when(r == 2)
        def _():
            gather2.first(3)
            gather2.second(2)

        @pl.when(r == 3)
        def _():
            gather2.second(3)

    layer.attend(kv, kvt, qt, att, lse, s_scr, pf_scr, forward_steps)
    for k in range(1, ncol):
        t.landed(vrow.at[at.behind(k)], vr.at[k])
    gather2.finish()
    vec = jnp.concatenate([vrow[s].T for s in range(ncol)], axis=0)

    def tokens_ready():
        for k in range(1, ncol):
            t.landed(tdo.at[:, rows_of(at.behind(k))], tr.at[k])

    def outputs_ready():
        for k in range(1, ncol):
            to = at.ahead(k)
            t.send(
                ("xb", k),
                lambda to=to: xb.at[:, rows_of(to)], lambda: xbo.at[:, :, own_cols(c)],
                lambda k=k: bs.at[k], lambda k=k: br.at[k], at.col_dev(to),
            )
        xbo[:, :, own_cols(c)] = xb[:, mine]

    layer.middle(
        xo, tdo, w, vec, att, xb, gw, sm, d_att, delta, dsa, hid, acc, ba, tokens_ready, outputs_ready
    )

    scatter1 = WeightScatter(
        "g1", t, line, gw, qkv, feat, sib1, two1, one1, zb1, out1, wsems[16:26]
    )
    scatter2 = WeightScatter(
        "g2", t, line, gw, rest, feat, sib2, two2, one2, zb2, out2, wsems[26:36]
    )
    for i in range(4):
        scatter2.begin(i)

    def small_send(i, src, device):
        t.send(
            ("sm", i), src, lambda: smb.at[i], lambda: ss.at[i], lambda: sr.at[i], device
        )

    small_send(0, lambda: sm, at.sibling)

    def back_steps(r):
        @pl.when(r == 0)
        def _():
            scatter2.step1(0)
            scatter2.step1(1)
            t.landed(smb.at[0], sr.at[0])
            smb[3] = sm[...] + smb[0]
            small_send(1, lambda: smb.at[3], at.second_dev)

        @pl.when(r == 1)
        def _():
            scatter2.step1(2)
            scatter2.step1(3)
            t.landed(smb.at[1], sr.at[1])
            smb[4] = smb[3] + smb[1]
            small_send(2, lambda: smb.at[4], at.first_dev)

        @pl.when(r == 2)
        def _():
            scatter2.step2(0)
            t.landed(smb.at[2], sr.at[2])
            smb[5] = smb[4] + smb[2]
            for k in range(1, ncol):
                to = at.ahead(k)
                t.send(
                    ("smz", k),
                    lambda to=to: smb.at[5, to], lambda k=k: smz.at[k],
                    lambda k=k: zs.at[k], lambda k=k: zr.at[k], at.col_dev(to),
                )

        @pl.when(r == 3)
        def _():
            scatter2.step2(1)

    layer.attend_back(
        kv, kvt, qt, lse, delta, d_att, kvt, qt, p_scr, ds_scr, back_steps, (xp, xc, xo, gw)
    )
    for i in range(4):
        scatter1.begin(i)

    def grad_block(s):
        rows = rows_of(s)
        for r in range(w.shape[0]):
            part = dot_nn(w[r, rows, BLOCK : 3 * BLOCK], kvt[r])
            mine_part = dot_nn(w[r, rows, :BLOCK], qt[r * BLOCK : (r + 1) * BLOCK])
            if r == 0:
                dx[...] = part
                dxo[...] = dsa[rows] + mine_part
            else:
                dx[...] += part
                dxo[...] += mine_part
        low, high = layer.own_columns()
        dx[:, low] += dxo[:, :BLOCK]
        dx[:, high] += dxo[:, BLOCK:PAIR]
        dx[:, PROMPT:] += dxo[:, PAIR:]

    def grad_send(i):
        s = line.far[i]
        grad_block(s)

        @pl.when(line.mid)
        def _():
            t.landed(gxz.at[s], gr.at[s])
            gpb[i] = (dx[:, :PROMPT] + gxz[s].astype(F32)).astype(BF16)

        @pl.when(line.end)
        def _():
            gpb[i] = dx[:, :PROMPT].astype(BF16)

        t.send(
            ("gx", i),
            lambda: gpb.at[i], lambda: gxz.at[line.slot[i]],
            lambda: gs.at[i], lambda: gr.at[line.slot[i]], at.col_dev(line.sum_to[i]),
        )
        gcb[i] = dx[:, PROMPT:].astype(BF16)
        t.send(
            ("gc", i),
            lambda: gcb.at[i], lambda: gco.at[c],
            lambda: ks.at[i], lambda: kr.at[c], at.col_dev(s),
        )

    grad_send(0)
    scatter2.step2(2)
    for i in range(4):
        scatter1.step1(i)
    grad_send(1)
    scatter2.step2(3)
    for i in range(4):
        scatter1.step2(i)
    grad_send(2)
    scatter2.step3(0)
    scatter2.step3(1)
    grad_block(c)
    gx_ref[:, :PROMPT] = dx[:, :PROMPT]
    gx_ref[:, cont_cols(c, PROMPT)] = dx[:, PROMPT:]
    scatter1.step3(0)
    scatter1.step3(1)
    scatter2.step3(2)
    scatter1.step3(2)

    for k in range(1, ncol):
        t.landed(xbo.at[:, :, own_cols(at.behind(k))], br.at[k])
    slot = iota((1, CONT), 1)
    weight = jnp.concatenate(
        [(iota((1, PROMPT), 1) < lens[0]).astype(F32)]
        + [(slot < lens_ref[group, 1 + n]).astype(F32) for n in range(NCONT)],
        axis=1,
    ) * (total_tokens / count)
    for frm, to, width in pieces:
        cols = slice(to, to + width)
        xout_ref[:, cols] = xbo[0, :, frm : frm + width]
        branch = xbo[1, :, frm : frm + width].astype(F32)
        y_here = y_ref[:, cols].astype(F32)
        yout_ref[:, cols] = (y_here + branch).astype(BF16)
        gy_ref[:, cols] = (y_here - ty_ref[:, cols].astype(F32) + branch) * weight[:, cols]

    scatter2.step3(3)
    scatter1.step3(3)
    small = smb[5, c]
    for k in range(1, ncol):
        t.landed(smz.at[k], zr.at[k])
        small = small + smz[k]
    gv_ref[...] = small
    for k in range(1, ncol):
        s = at.behind(k)
        t.landed(gco.at[s], kr.at[s])
        gx_ref[:, cont_cols(s, PROMPT)] = gco[s].astype(F32)
    for slot_at, cond in ((c, c > 0), (4, c < 3)):

        @pl.when(cond)
        def _(slot_at=slot_at):
            t.landed(gxz.at[slot_at], gr.at[slot_at])
            gx_ref[:, :PROMPT] += gxz[slot_at].astype(F32)

    scatter2.finish()
    scatter1.finish()
    for i in range(3):
        gq_ref[i] = out1[:, i * BLOCK : (i + 1) * BLOCK]
    go_ref[...] = out2[:, :BLOCK].T
    gu_ref[...] = out2[:, BLOCK : BLOCK + ff]
    gd_ref[...] = out2[:, BLOCK + ff :].T
    t.drain()


def run_step(lengths, x, y, tx, ty, wq, wo, wu, wd, vec):
    feat, tokens = x.shape
    full = 4 * feat
    ff = wu.shape[1]
    width = 4 * BLOCK + 2 * ff
    rest = BLOCK + 2 * ff
    half = feat // 2
    own, cont = tokens // 4, NCONT * CONT // 4
    keys = PROMPT + cont
    heads = full // HD
    vmem = pl.BlockSpec(memory_space=pltpu.VMEM)
    dma = pltpu.SemaphoreType.DMA

    def bf(*shape):
        return pltpu.VMEM(shape, BF16)

    def f32(*shape):
        return pltpu.VMEM(shape, F32)

    def reduce_buffers(cols):
        return [
            bf(4, 4, half, cols), bf(2, 4, half, cols), bf(4, half, cols), bf(5, half, cols), f32(feat, cols),
        ]

    gather_sems = [
        dma((5,)), dma((4,)), dma((4,)), dma((4,)), dma((2, 4)), dma((2, 4)), dma((4, 4)), dma((4, 4)),
    ]
    scatter_sems = [
        dma((4,)), dma((4,)), dma((2, 4)), dma((2, 4)), dma((4,)), dma((4,)), dma((3,)), dma((5,)),
        dma(()), dma(()),
    ]
    sums = (4, 8, feat)
    return pl.pallas_call(
        functools.partial(step_kernel, 4),
        out_shape=(
            jax.ShapeDtypeStruct((feat, tokens), BF16),
            jax.ShapeDtypeStruct((feat, tokens), BF16),
            jax.ShapeDtypeStruct((feat, tokens), F32),
            jax.ShapeDtypeStruct((feat, tokens), F32),
            jax.ShapeDtypeStruct((3, feat, BLOCK), F32),
            jax.ShapeDtypeStruct(wo.shape, F32),
            jax.ShapeDtypeStruct(wu.shape, F32),
            jax.ShapeDtypeStruct(wd.shape, F32),
            jax.ShapeDtypeStruct((8, feat), F32),
        ),
        in_specs=[pl.BlockSpec(memory_space=pltpu.SMEM), vmem, pl.BlockSpec(memory_space=pl.ANY)]
        + [vmem] * 8,
        out_specs=[vmem] * 9,
        scratch_shapes=[
            bf(4, full, width), bf(4, full, width), bf(full, PROMPT), bf(full, cont), bf(full, own),
            bf(keys, full), bf(keys, 4 * PAIR), bf(4, PAIR, keys), bf(full, own), bf(full, own),
            f32(heads, own), f32(heads, own), bf(full, own), f32(2, PROMPT, PAIR), bf(2, PROMPT, PAIR),
            bf(2, PROMPT, own), bf(2, PROMPT, own), f32(full, own), bf(4, own, ff), f32(full, own),
            f32(full, own), f32(feat, keys), f32(feat, own), bf(2, feat, tokens), bf(2, full, own),
            bf(2, full, own), bf(2, feat, tokens), f32(4, 8, feat), bf(3, feat, PROMPT),
            bf(5, feat, PROMPT), bf(3, feat, cont), bf(4, feat, cont),
            f32(*sums), f32(6, *sums), f32(*sums),
        ]
        + reduce_buffers(3 * BLOCK)
        + reduce_buffers(rest)
        + [
            dma((5,)), dma((4,)), dma((4,)), dma((4,)), dma((4,)), dma((4,)), dma((4,)), dma((4,)),
            dma((4,)), dma((4,)), dma((3,)), dma((5,)), dma((3,)), dma((4,)), dma((3,)), dma((3,)),
            dma((4,)), dma((4,)),
        ]
        + gather_sems * 2
        + scatter_sems * 2,
        compiler_params=pltpu.CompilerParams(
            collective_id=2, has_side_effects=True, vmem_limit_bytes=61 << 20
        ),
        name="layer_step",
    )(lengths, lengths, x, y, tx, ty, wq, wo, wu, wd, vec)


def body(
    x_stream, y_stream, w_qkv, w_out, gain_attn, bias_attn, w_up, w_down, gain_ffn, bias_ffn,
    teach_x, teach_y, lengths,
):
    ncol, nrow = lax.axis_size("col"), lax.axis_size("row")
    feat, tokens = x_stream.shape
    full = feat * ncol
    groups_here = tokens // GROUP
    parts = ncol // groups_here
    assert parts * 2 * BLOCK == PROMPT and nrow == 4
    block = w_qkv.shape[2]
    ff_block = w_up.shape[1]

    if ncol == parts:
        small_vecs = jnp.stack([gain_attn, bias_attn, gain_ffn, bias_ffn] * 2).astype(F32)
        x_out, y_out, grad_x, grad_y, g_q, g_o, g_u, g_d, sums = run_step(
            lengths, x_stream, y_stream, teach_x, teach_y, w_qkv.reshape(feat, 3 * block),
            w_out, w_up, w_down, small_vecs,
        )
        loss = sums[4, 0] / (2.0 * jnp.sum(lengths).astype(F32) * full)
        return (
            x_out, y_out, grad_x, grad_y, g_q.transpose(1, 0, 2), g_o, sums[0], sums[1], g_u, g_d,
            sums[2], sums[3], loss,
        )

    y_f32 = y_stream.astype(F32)
    dy = y_f32 - teach_y.astype(F32)
    teach_dy = to_parts(jnp.stack([teach_x, dy.astype(BF16)]), parts)
    packed = jnp.concatenate([w_qkv.reshape(feat, 3 * block), w_out.T, w_up, w_down.T], axis=1)
    small_vecs = jnp.stack([gain_attn, bias_attn, gain_ffn, bias_ffn])
    vecs = lax.all_gather(small_vecs, "col", axis=1, tiled=True)

    x_prompt, x_cont, tdo, weights = gather_all(x_stream, teach_dy, packed, ncol, nrow, parts)

    first = (lax.axis_index("dp") * nrow + lax.axis_index("row")) * groups_here
    count_all = jnp.sum(lengths).astype(F32)
    total_tokens = lengths.shape[0] * GROUP
    vec = jnp.pad(vecs.T, ((0, 0), (0, 124)))
    xb, gp, gc, gw, small = run_layer(lengths, x_prompt, x_cont, tdo, weights, vec, parts)
    lanes = max(feat, 128)
    small = small[0].reshape(8, ncol, feat).transpose(1, 0, 2)
    small = jnp.pad(small, ((0, 0), (0, 0), (0, lanes - feat)))
    xb, gp, gc, gw, sums = scatter_all(xb, gp, gc, gw, small, ncol, parts)

    xb = from_parts(xb, parts)
    branch = xb[1].astype(F32)
    live_all = live_slots(
        lax.dynamic_slice_in_dim(lengths, first, groups_here, 0)
    ).reshape(1, tokens)
    y_out = (y_f32 + branch).astype(BF16)
    grad_y_out = (dy + branch) * (live_all * (total_tokens / count_all))
    gp = jnp.sum(gp.astype(F32), axis=0).reshape(feat, groups_here, PROMPT)
    gc = gc.astype(F32).reshape(feat, groups_here, NCONT * CONT)
    grad_x = jnp.concatenate([gp, gc], axis=2).reshape(feat, tokens)
    loss = sums[4, 0] / (2.0 * count_all * full)
    first_up = 4 * block
    return (
        xb[0],
        y_out,
        grad_x,
        grad_y_out,
        gw[:, : 3 * block].reshape(feat, 3, block),
        gw[:, 3 * block : 4 * block].T,
        sums[0, :feat],
        sums[1, :feat],
        gw[:, first_up : first_up + ff_block],
        gw[:, first_up + ff_block :].T,
        sums[2, :feat],
        sums[3, :feat],
        loss,
    )


def live_slots(lens):
    prompt = jnp.arange(PROMPT, dtype=jnp.int32)[None, :] < lens[:, 0:1]
    cont = jnp.arange(CONT, dtype=jnp.int32)[None, None, :] < lens[:, 1:, None]
    cont = cont.reshape(lens.shape[0], NCONT * CONT)
    return jnp.concatenate([prompt, cont], axis=1).astype(F32)


def solution(mesh):
    stream = P("col", ("dp", "row"))
    up, down = P("col", "row"), P("row", "col")
    qkv, vec = P("col", None, "row"), P("col")
    return jax.shard_map(
        body,
        mesh=mesh,
        in_specs=(
            stream, stream, qkv, down, vec, vec, up, down, vec, vec, stream, stream, P(),
        ),
        out_specs=(
            stream, stream, stream, stream, qkv, down, vec, vec, up, down, vec, vec, P(),
        ),
        check_vma=False,
    )
```

```python
import functools

import jax
import jax.numpy as jnp
from jax import lax
from jax.experimental import pallas as pl
from jax.experimental.pallas import tpu as pltpu
from jax.sharding import PartitionSpec as P

HD = 64
PROMPT = 1024
CONT = 128
NCONT = 8
GROUP = 2048
BLOCK = 128

EPS_NORM = 1e-05
NEG_FILL = -1000000000.0
MESH = pl.DeviceIdType.MESH
F32 = jnp.float32
BF16 = jnp.bfloat16


def flip_low(r):
    return r + 1 - 2 * (r % 2)


def flip_high(r):
    return (r + 2) % 4


class Places:
    def __init__(self, ncol):
        self.dp = lax.axis_index("dp")
        self.row = lax.axis_index("row")
        self.col = lax.axis_index("col")
        self.ncol = ncol
        low, high = flip_low(self.row), flip_high(self.row)
        self.first = low * (1 - self.dp) + high * self.dp
        self.second = high * (1 - self.dp) + low * self.dp
        self.both = 3 - self.row
        self.sibling = (1 - self.dp, self.row, self.col)
        self.first_dev = (self.dp, self.first, self.col)
        self.second_dev = (self.dp, self.second, self.col)
        self.aheads = [(self.col + k) % ncol for k in range(ncol)]
        self.behinds = [(self.col + ncol - k) % ncol for k in range(ncol)]

    def ahead(self, k):
        return self.aheads[k]

    def behind(self, k):
        return self.behinds[k]

    def col_dev(self, c):
        return (self.dp, self.row, c)

    def meet(self):
        barrier = pltpu.get_barrier_semaphore()
        partners = [self.sibling, self.first_dev, self.second_dev]
        partners += [self.col_dev(self.ahead(k)) for k in range(1, self.ncol)]
        for partner in partners:
            pl.semaphore_signal(barrier, inc=1, device_id=partner, device_id_type=MESH)
        pl.semaphore_wait(barrier, len(partners))


def remote(src, dst, send_sem, recv_sem, device):
    return pltpu.make_async_remote_copy(
        src_ref=src,
        dst_ref=dst,
        send_sem=send_sem,
        recv_sem=recv_sem,
        device_id=device,
        device_id_type=MESH,
    )


def gather_kernel(
    ncol, parts, x_ref, td_ref, w_ref, xp_ref, xc_ref, tdo_ref, g_ref,
    act_send, act_recv, col_send, col_recv, one_send, one_recv, two_send, two_recv,
    sib_send, sib_recv, local_sem,
):
    at = Places(ncol)
    feat = x_ref.shape[0]
    half = feat // 2
    own_tokens = tdo_ref.shape[2]
    own_cont = xc_ref.shape[1]

    def rows_of(c):
        return pl.ds(pl.multiple_of(c * feat, feat), feat)

    def half_rows(c, core):
        return pl.ds(pl.multiple_of(c * feat + core * half, half), half)

    def prompt_cols(c):
        return pl.ds(pl.multiple_of(c // parts * GROUP, GROUP), PROMPT)

    def cont_cols(c):
        return pl.ds(
            pl.multiple_of(c // parts * GROUP + PROMPT + c % parts * own_cont, own_cont), own_cont
        )

    def own_cols(c):
        return pl.ds(pl.multiple_of(c * own_tokens, own_tokens), own_tokens)

    at.meet()
    my_half = w_ref.at[pl.ds(pl.multiple_of(at.dp * half, half), half)]
    pending = []

    def start(copy):
        copy.start()
        pending.append(copy)
        return copy

    mine = rows_of(at.col)
    for i, (src, dst) in enumerate(
        (
            (x_ref.at[:, prompt_cols(at.col)], xp_ref.at[mine]),
            (x_ref.at[:, cont_cols(at.col)], xc_ref.at[mine]),
            (td_ref.at[:, :, own_cols(at.col)], tdo_ref.at[:, mine]),
            (w_ref, g_ref.at[at.row, mine]),
        )
    ):
        pltpu.make_async_copy(src, dst, local_sem.at[i]).start()

    for k in range(1, ncol):
        start(
            remote(
                my_half,
                g_ref.at[at.row, half_rows(at.col, at.dp)],
                col_send.at[k],
                col_recv.at[k],
                at.col_dev(at.ahead(k)),
            )
        )
    for k in range(1, ncol):
        to = at.ahead(k)
        dev = at.col_dev(to)
        start(
            remote(
                x_ref.at[:, prompt_cols(to)], xp_ref.at[mine],
                act_send.at[0, k], act_recv.at[0, k], dev,
            )
        )
        start(
            remote(
                x_ref.at[:, cont_cols(to)], xc_ref.at[mine],
                act_send.at[1, k], act_recv.at[1, k], dev,
            )
        )
    for k in range(1, ncol):
        to = at.ahead(k)
        start(
            remote(
                td_ref.at[:, :, own_cols(to)], tdo_ref.at[:, mine],
                act_send.at[2, k], act_recv.at[2, k], at.col_dev(to),
            )
        )

    def piece(row, k, core):
        return g_ref.at[row, half_rows(at.behind(k), core)]

    def landed(dst, recv_sem):
        remote(dst, dst, recv_sem, recv_sem, at.sibling).wait_recv()

    def chunk(k):
        return my_half if k == 0 else piece(at.row, k, at.dp)

    for k in range(ncol):
        if k:
            landed(piece(at.row, k, at.dp), col_recv.at[k])
        start(remote(chunk(k), piece(at.row, k, at.dp), one_send.at[k], one_recv.at[k], at.first_dev))
        start(
            remote(chunk(k), piece(at.row, k, at.dp), two_send.at[0, k], two_recv.at[0, k], at.second_dev)
        )
        if k:
            start(
                remote(chunk(k), piece(at.row, k, at.dp), sib_send.at[0, k], sib_recv.at[0, k], at.sibling)
            )
    for k in range(ncol):
        got = piece(at.first, k, at.dp)
        landed(got, one_recv.at[k])
        start(remote(got, got, two_send.at[1, k], two_recv.at[1, k], at.second_dev))
        start(remote(got, got, sib_send.at[1, k], sib_recv.at[1, k], at.sibling))
    for k in range(ncol):
        for i, row in ((0, at.second), (1, at.both)):
            got = piece(row, k, at.dp)
            landed(got, two_recv.at[i, k])
            start(remote(got, got, sib_send.at[2 + i, k], sib_recv.at[2 + i, k], at.sibling))

    for k in range(1, ncol):
        frm = rows_of(at.behind(k))
        landed(xp_ref.at[frm], act_recv.at[0, k])
        landed(xc_ref.at[frm], act_recv.at[1, k])
        landed(tdo_ref.at[:, frm], act_recv.at[2, k])
    other = 1 - at.dp
    for k in range(ncol):
        if k:
            landed(piece(at.row, k, other), sib_recv.at[0, k])
        landed(piece(at.second, k, other), sib_recv.at[1, k])
        landed(piece(at.first, k, other), sib_recv.at[2, k])
        landed(piece(at.both, k, other), sib_recv.at[3, k])
    for copy in pending:
        copy.wait_send()
    for i, (src, dst) in enumerate(
        (
            (x_ref.at[:, prompt_cols(at.col)], xp_ref.at[mine]),
            (x_ref.at[:, cont_cols(at.col)], xc_ref.at[mine]),
            (td_ref.at[:, :, own_cols(at.col)], tdo_ref.at[:, mine]),
            (w_ref, g_ref.at[at.row, mine]),
        )
    ):
        pltpu.make_async_copy(src, dst, local_sem.at[i]).wait()


def gather_all(x_stream, teach_dy, packed, ncol, nrow, parts):
    feat = x_stream.shape[0]
    full = feat * ncol
    own_tokens = GROUP // parts
    own_cont = NCONT * CONT // parts
    dma = pltpu.SemaphoreType.DMA
    anywhere = pl.BlockSpec(memory_space=pl.ANY)
    return pl.pallas_call(
        functools.partial(gather_kernel, ncol, parts),
        out_shape=(
            jax.ShapeDtypeStruct((full, PROMPT), BF16),
            jax.ShapeDtypeStruct((full, own_cont), BF16),
            jax.ShapeDtypeStruct((2, full, own_tokens), BF16),
            jax.ShapeDtypeStruct((nrow, full, packed.shape[1]), BF16),
        ),
        in_specs=[anywhere] * 3,
        out_specs=[anywhere] * 4,
        scratch_shapes=[
            dma((3, ncol)), dma((3, ncol)), dma((ncol,)), dma((ncol,)), dma((ncol,)), dma((ncol,)),
            dma((2, ncol)), dma((2, ncol)), dma((4, ncol)), dma((4, ncol)), dma((4,)),
        ],
        compiler_params=pltpu.CompilerParams(collective_id=0, has_side_effects=True),
        name="gather_all",
    )(x_stream, teach_dy, packed)


def scatter_kernel(
    ncol, parts, xb_ref, gp_ref, gc_ref, gw_ref, sm_ref,
    xbo_ref, gpo_ref, gco_ref, gwo_ref, smo_ref,
    sib_buf, two_buf, one_buf, col_buf, sm_buf, smc_buf,
    act_send, act_recv, sib_send, sib_recv, two_send, two_recv, one_send, one_recv,
    col_send, col_recv, fin_send, fin_recv, sm_send, sm_recv, smc_send, smc_recv, local_sem,
):
    at = Places(ncol)
    feat = xbo_ref.shape[1]
    half = feat // 2
    own_tokens = xb_ref.shape[2]
    own_cont = gc_ref.shape[1]
    part = at.col % parts

    def rows_of(c):
        return pl.ds(pl.multiple_of(c * feat, feat), feat)

    def half_rows(c, core):
        return pl.ds(pl.multiple_of(c * feat + core * half, half), half)

    def prompt_cols(c):
        return pl.ds(pl.multiple_of(c // parts * PROMPT, PROMPT), PROMPT)

    def cont_cols(c):
        return pl.ds(pl.multiple_of(c * own_cont, own_cont), own_cont)

    def own_cols(c):
        return pl.ds(pl.multiple_of(c * own_tokens, own_tokens), own_tokens)

    at.meet()
    pending = []

    def start(copy):
        copy.start()
        pending.append(copy)
        return copy

    def landed(dst, recv_sem):
        remote(dst, dst, recv_sem, recv_sem, at.sibling).wait_recv()

    other = 1 - at.dp
    order = list(range(1, ncol)) + [0]
    for k in order:
        start(
            remote(
                gw_ref.at[:, half_rows(at.ahead(k), other)], sib_buf.at[k],
                sib_send.at[k], sib_recv.at[k], at.sibling,
            )
        )
    start(remote(sm_ref, sm_buf.at[0], sm_send.at[0], sm_recv.at[0], at.sibling))

    def local_copies():
        mine = rows_of(at.col)
        return [
            pltpu.make_async_copy(src, dst, local_sem.at[i])
            for i, (src, dst) in enumerate(
                (
                    (xb_ref.at[:, mine], xbo_ref.at[:, :, own_cols(at.col)]),
                    (gp_ref.at[mine], gpo_ref.at[part, :, prompt_cols(at.col)]),
                    (gc_ref.at[mine], gco_ref.at[:, cont_cols(at.col)]),
                )
            )
        ]

    for copy in local_copies():
        copy.start()
    for k in range(1, ncol):
        to = at.ahead(k)
        dev = at.col_dev(to)
        start(
            remote(
                xb_ref.at[:, rows_of(to)], xbo_ref.at[:, :, own_cols(at.col)],
                act_send.at[0, k], act_recv.at[0, k], dev,
            )
        )
        start(
            remote(
                gp_ref.at[rows_of(to)], gpo_ref.at[part, :, prompt_cols(at.col)],
                act_send.at[1, k], act_recv.at[1, k], dev,
            )
        )
        start(
            remote(
                gc_ref.at[rows_of(to)], gco_ref.at[:, cont_cols(at.col)],
                act_send.at[2, k], act_recv.at[2, k], dev,
            )
        )

    for k in order:
        landed(sib_buf.at[k], sib_recv.at[k])
        for row in range(gw_ref.shape[0]):
            here = gw_ref.at[row, half_rows(at.ahead(k), at.dp)]
            sib_buf[k, row] = (here[...].astype(F32) + sib_buf[k, row].astype(F32)).astype(BF16)
        for i, row in ((0, at.second), (1, at.both)):
            start(
                remote(
                    sib_buf.at[k, row], two_buf.at[i, k],
                    two_send.at[i, k], two_recv.at[i, k], at.second_dev,
                )
            )
    landed(sm_buf.at[0], sm_recv.at[0])
    sm_buf[3] = sm_ref[...] + sm_buf[0]
    start(remote(sm_buf.at[3], sm_buf.at[1], sm_send.at[1], sm_recv.at[1], at.second_dev))
    for k in order:
        landed(two_buf.at[1, k], two_recv.at[1, k])
        two_buf[1, k] = (sib_buf[k, at.first].astype(F32) + two_buf[1, k].astype(F32)).astype(BF16)
        start(
            remote(
                two_buf.at[1, k], one_buf.at[k], one_send.at[k], one_recv.at[k], at.first_dev
            )
        )
    landed(sm_buf.at[1], sm_recv.at[1])
    sm_buf[4] = sm_buf[3] + sm_buf[1]
    start(remote(sm_buf.at[4], sm_buf.at[2], sm_send.at[2], sm_recv.at[2], at.first_dev))
    for k in order:
        landed(two_buf.at[0, k], two_recv.at[0, k])
        landed(one_buf.at[k], one_recv.at[k])
        total = sib_buf[k, at.row].astype(F32) + two_buf[0, k].astype(F32) + one_buf[k].astype(F32)
        if k:
            two_buf[0, k] = total.astype(BF16)
            start(
                remote(
                    two_buf.at[0, k], col_buf.at[k],
                    col_send.at[k], col_recv.at[k], at.col_dev(at.ahead(k)),
                )
            )
        else:
            own_total = total
    landed(sm_buf.at[2], sm_recv.at[2])
    sm_buf[5] = sm_buf[4] + sm_buf[2]
    for k in range(1, ncol):
        to = at.ahead(k)
        start(
            remote(
                sm_buf.at[5, to], smc_buf.at[k], smc_send.at[k], smc_recv.at[k], at.col_dev(to)
            )
        )
    for k in range(1, ncol):
        landed(col_buf.at[k], col_recv.at[k])
        own_total = own_total + col_buf[k].astype(F32)
    my_rows = pl.ds(pl.multiple_of(at.dp * half, half), half)
    gwo_ref[my_rows] = own_total
    start(remote(gwo_ref.at[my_rows], gwo_ref.at[my_rows], fin_send, fin_recv, at.sibling))
    small = sm_buf[5, at.col]
    for k in range(1, ncol):
        landed(smc_buf.at[k], smc_recv.at[k])
        small = small + smc_buf[k]
    smo_ref[...] = small
    landed(gwo_ref.at[pl.ds(pl.multiple_of(other * half, half), half)], fin_recv)
    for k in range(1, ncol):
        frm = at.behind(k)
        landed(xbo_ref.at[:, :, own_cols(frm)], act_recv.at[0, k])
        landed(gpo_ref.at[frm % parts, :, prompt_cols(frm)], act_recv.at[1, k])
        landed(gco_ref.at[:, cont_cols(frm)], act_recv.at[2, k])
    for copy in pending:
        copy.wait_send()
    for copy in local_copies():
        copy.wait()


def scatter_all(xb, gp, gc, gw, small, ncol, parts):
    nrow, full, width = gw.shape
    feat = full // ncol
    half = feat // 2
    groups = ncol // parts
    own_tokens, own_cont = xb.shape[2], gc.shape[1]
    dma = pltpu.SemaphoreType.DMA
    anywhere = pl.BlockSpec(memory_space=pl.ANY)
    vmem = pl.BlockSpec(memory_space=pltpu.VMEM)
    small_shape = small.shape
    return pl.pallas_call(
        functools.partial(scatter_kernel, ncol, parts),
        out_shape=(
            jax.ShapeDtypeStruct((2, feat, ncol * own_tokens), BF16),
            jax.ShapeDtypeStruct((parts, feat, groups * PROMPT), BF16),
            jax.ShapeDtypeStruct((feat, ncol * own_cont), BF16),
            jax.ShapeDtypeStruct((feat, width), F32),
            jax.ShapeDtypeStruct(small_shape[1:], F32),
        ),
        in_specs=[anywhere, anywhere, anywhere, vmem, vmem],
        out_specs=[anywhere, anywhere, anywhere, vmem, vmem],
        scratch_shapes=[
            pltpu.VMEM((ncol, nrow, half, width), BF16),
            pltpu.VMEM((2, ncol, half, width), BF16),
            pltpu.VMEM((ncol, half, width), BF16),
            pltpu.VMEM((ncol, half, width), BF16),
            pltpu.VMEM((6,) + small_shape, F32),
            pltpu.VMEM((ncol,) + small_shape[1:], F32),
            dma((3, ncol)), dma((3, ncol)), dma((ncol,)), dma((ncol,)), dma((2, ncol)), dma((2, ncol)),
            dma((ncol,)), dma((ncol,)), dma((ncol,)), dma((ncol,)), dma(()), dma(()),
            dma((3,)), dma((3,)), dma((ncol,)), dma((ncol,)), dma((3,)),
        ],
        compiler_params=pltpu.CompilerParams(
            collective_id=1, has_side_effects=True, vmem_limit_bytes=56 << 20
        ),
        name="scatter_all",
    )(xb, gp, gc, gw, small)


def to_parts(array_in, parts):
    lead = array_in.shape[:-1]
    groups = array_in.shape[-1] // GROUP
    split = array_in.reshape(lead + (groups, GROUP))
    prompt = split[..., :PROMPT].reshape(lead + (groups, 2, parts, BLOCK))
    prompt = jnp.stack([prompt[..., 0, :, :], prompt[..., 1, ::-1, :]], axis=-2)
    prompt = prompt.reshape(lead + (groups, parts, PROMPT // parts))
    cont = split[..., PROMPT:].reshape(lead + (groups, parts, NCONT * CONT // parts))
    return jnp.concatenate([prompt, cont], axis=-1).reshape(array_in.shape)


def from_parts(array_in, parts):
    lead = array_in.shape[:-1]
    groups = array_in.shape[-1] // GROUP
    split = array_in.reshape(lead + (groups, parts, GROUP // parts))
    prompt = split[..., : PROMPT // parts].reshape(lead + (groups, parts, 2, BLOCK))
    prompt = jnp.concatenate(
        [prompt[..., :, 0, :], prompt[..., ::-1, 1, :]], axis=-2
    ).reshape(lead + (groups, PROMPT))
    cont = split[..., PROMPT // parts :].reshape(lead + (groups, NCONT * CONT))
    return jnp.concatenate([prompt, cont], axis=-1).reshape(array_in.shape)


def norm_forward(summed, gain_vec, bias_vec):
    average = jnp.mean(summed, axis=0, keepdims=True)
    squares = jnp.mean(summed * summed, axis=0, keepdims=True)
    inv_scale = lax.rsqrt(squares - average * average + EPS_NORM)
    unit_val = (summed - average) * inv_scale
    return (unit_val * gain_vec + bias_vec, unit_val, inv_scale)


def norm_backward(upstream, unit_val, inv_scale, gain_vec):
    scaled = upstream * gain_vec
    first = jnp.mean(scaled, axis=0, keepdims=True)
    second = jnp.mean(scaled * unit_val, axis=0, keepdims=True)
    d_summed = inv_scale * (scaled - first - unit_val * second)
    sums = [jnp.sum(v, axis=1, keepdims=True) for v in (upstream * unit_val, upstream)]
    return (d_summed, *sums)


def dot_tn(lhs, rhs):
    return lax.dot_general(lhs, rhs, (((0,), (0,)), ((), ())), preferred_element_type=F32)


def dot_nn(lhs, rhs):
    return lax.dot_general(lhs, rhs, (((1,), (0,)), ((), ())), preferred_element_type=F32)


def dot_nt(lhs, rhs):
    return lax.dot_general(lhs, rhs, (((1,), (1,)), ((), ())), preferred_element_type=F32)


def iota(shape, axis):
    return lax.broadcasted_iota(jnp.int32, shape, axis)


def fold(array_in, op):
    return op(array_in.reshape(array_in.shape[0] // 8, 8, array_in.shape[1]), axis=0)


KEYS = 256
PAIR = 2 * BLOCK


def put(ref, r, cols, value):
    lead = ref.shape[1:-1]
    index = (r,) + (slice(None),) * len(lead) + (cols,)
    ref[index] = value.astype(BF16).reshape(lead + (value.shape[1],))


class Layer:
    def __init__(self, part, parts, lens, total_tokens, count, order=lambda n: n):
        self.part, self.parts = part, parts
        self.order = order
        self.lens = lens
        self.total_tokens, self.count = total_tokens, count
        slot = iota((1, BLOCK), 1)
        low, high = part * BLOCK + slot, (2 * parts - 1 - part) * BLOCK + slot
        last = lens[0] - 1
        self.bound = jnp.concatenate(
            [jnp.minimum(low, last), jnp.minimum(high, last), jnp.full((1, PAIR), last, jnp.int32)],
            axis=1,
        )
        live = [low < lens[0], high < lens[0]] + [slot < n for n in lens[1:]]
        self.live = jnp.concatenate([m.astype(F32) for m in live], axis=1)

    def own_columns(self):
        low = pl.ds(pl.multiple_of(self.part * BLOCK, BLOCK), BLOCK)
        high = pl.ds(pl.multiple_of((2 * self.parts - 1 - self.part) * BLOCK, BLOCK), BLOCK)
        return low, high

    def project(self, xp, xc, w, xo, xt, kv, kvt, qt):
        low, high = self.own_columns()
        xo[:, :BLOCK] = xp[:, low]
        xo[:, BLOCK:PAIR] = xp[:, high]
        xo[:, PAIR:] = xc[...]
        xt[:PROMPT] = xp[...].T
        xt[PROMPT:] = xc[...].T

        def step(r, carry):
            wq, wkv = w[r, :, :BLOCK], w[r, :, BLOCK : 3 * BLOCK]
            cols = pl.ds(pl.multiple_of(r * PAIR, PAIR), PAIR)
            kv[:, cols] = dot_nn(xt[...], wkv).astype(BF16)
            kvt[r, :, :PROMPT] = dot_tn(wkv, xp[...]).astype(BF16)
            kvt[r, :, PROMPT:] = dot_tn(wkv, xc[...]).astype(BF16)
            rows = pl.ds(pl.multiple_of(r * BLOCK, BLOCK), BLOCK)
            qt[rows] = (dot_tn(wq, xo[...]).astype(BF16).astype(F32) * HD ** (-0.5)).astype(BF16)
            return carry

        lax.fori_loop(0, w.shape[0], step, 0)

    def one_head(self, array_in, head):
        zeros = jnp.zeros((HD, array_in.shape[1]), array_in.dtype)
        mine = array_in[head * HD : (head + 1) * HD]
        return jnp.concatenate([mine, zeros] if head == 0 else [zeros, mine], axis=0)

    def masked(self, score, first_key, columns):
        keys = iota(score.shape, 0) + first_key
        return jnp.where(keys <= self.bound[:, columns], score, NEG_FILL)

    def masked_own(self, score, n):
        keys = iota(score.shape, 0)
        return jnp.where(
            (keys <= iota(score.shape, 1)) & (keys < self.lens[1 + n]), score, NEG_FILL
        )

    def attend(self, kv, kvt, qt, att, lse, s_scr, p_scr, between=None):
        def step(r, carry):
            k_cols = pl.ds(pl.multiple_of(r * PAIR, PAIR), BLOCK)
            q_pair = qt[pl.ds(pl.multiple_of(r * BLOCK, BLOCK), BLOCK)]
            for head in range(2):
                query = self.one_head(q_pair, head)
                v_rows = slice(BLOCK + head * HD, BLOCK + (head + 1) * HD)
                for b in range(2):
                    columns = slice(b * PAIR, (b + 1) * PAIR)
                    q_here = query[:, columns]
                    top = jnp.full((8, PAIR), NEG_FILL, F32)
                    for first in range(0, PROMPT, KEYS):
                        score = dot_nn(kv[first : first + KEYS, k_cols], q_here)
                        score = self.masked(score, first, columns)
                        s_scr[head, first : first + KEYS] = score
                        top = jnp.maximum(top, fold(score, jnp.max))
                    own_scores = []
                    if b == 1:
                        for n in range(2):
                            keys = slice(PROMPT + n * BLOCK, PROMPT + (n + 1) * BLOCK)
                            score = dot_nn(kv[keys, k_cols], q_here[:, n * BLOCK : (n + 1) * BLOCK])
                            own_scores.append(self.masked_own(score, n))
                        own_top = [fold(score, jnp.max) for score in own_scores]
                        top = jnp.maximum(top, jnp.concatenate(own_top, axis=1))
                    top = jnp.max(top, axis=0, keepdims=True)
                    total = jnp.zeros((8, PAIR), F32)
                    for first in range(0, PROMPT, KEYS):
                        prob = jnp.exp(s_scr[head, first : first + KEYS] - top)
                        total = total + fold(prob, jnp.sum)
                        p_scr[head, first : first + KEYS] = prob.astype(BF16)
                    out = dot_nn(kvt[r, v_rows, :PROMPT], p_scr[head])
                    if b == 1:
                        own_out, own_total = [], []
                        for n in range(2):
                            lanes = slice(n * BLOCK, (n + 1) * BLOCK)
                            prob = jnp.exp(own_scores[n] - top[:, lanes])
                            own_total.append(fold(prob, jnp.sum))
                            keys = slice(PROMPT + n * BLOCK, PROMPT + (n + 1) * BLOCK)
                            own_out.append(dot_nn(kvt[r, v_rows, keys], prob.astype(BF16)))
                        total = total + jnp.concatenate(own_total, axis=1)
                        out = out + jnp.concatenate(own_out, axis=1)
                    total = jnp.sum(total, axis=0, keepdims=True)
                    rows = pl.ds(pl.multiple_of(r * BLOCK + head * HD, HD), HD)
                    att[rows, columns] = (out / total).astype(BF16)
                    lse[pl.ds(2 * r + head, 1), columns] = top + jnp.log(total)
            if between is not None:
                between(r)
            return carry

        lax.fori_loop(0, kvt.shape[0], step, 0)

    def attend_back(
        self, kv, kvt, qt, lse, delta, d_att, dkvt, dqt, p_scr, ds_scr, between=None, grads=None
    ):
        def step(n, carry):
            r = self.order(n)
            k_cols = pl.ds(pl.multiple_of(r * PAIR, PAIR), BLOCK)
            v_cols = pl.ds(pl.multiple_of(r * PAIR + BLOCK, BLOCK), BLOCK)
            pair = pl.ds(pl.multiple_of(r * BLOCK, BLOCK), BLOCK)
            q_pair, d_pair = qt[pair], d_att[pair]
            for head in range(2):
                query, d_out = self.one_head(q_pair, head), self.one_head(d_pair, head)
                q_mine = q_pair[head * HD : (head + 1) * HD]
                d_mine = d_pair[head * HD : (head + 1) * HD]
                k_rows = slice(head * HD, (head + 1) * HD)
                v_rows = slice(BLOCK + head * HD, BLOCK + (head + 1) * HD)
                norm = lse[pl.ds(2 * r + head, 1)]
                dlt = delta[pl.ds(2 * r + head, 1)]
                for b in range(2):
                    columns = slice(b * PAIR, (b + 1) * PAIR)
                    for first in range(0, PROMPT, KEYS):
                        keys = slice(first, first + KEYS)
                        score = dot_nn(kv[keys, k_cols], query[:, columns])
                        score = self.masked(score, first, columns)
                        prob = jnp.exp(score - norm[:, columns])
                        dprob = dot_nn(kv[keys, v_cols], d_out[:, columns])
                        p_scr[head, keys, columns] = prob.astype(BF16)
                        ds_scr[head, keys, columns] = (prob * (dprob - dlt[:, columns])).astype(BF16)
                d_query = dot_nn(kvt[r, k_rows, :PROMPT], ds_scr[head])
                own_dq = [jnp.zeros((HD, PAIR), F32)]
                for m in range(2):
                    keys = slice(PROMPT + m * BLOCK, PROMPT + (m + 1) * BLOCK)
                    lanes = slice(PAIR + m * BLOCK, PAIR + (m + 1) * BLOCK)
                    score = self.masked_own(dot_nn(kv[keys, k_cols], query[:, lanes]), m)
                    prob = jnp.exp(score - norm[:, lanes])
                    dprob = dot_nn(kv[keys, v_cols], d_out[:, lanes])
                    d_score = (prob * (dprob - dlt[:, lanes])).astype(BF16)
                    own_dq.append(dot_nn(kvt[r, k_rows, keys], d_score))
                    dkvt[r, k_rows, keys] = dot_nt(q_mine[:, lanes], d_score).astype(BF16)
                    dkvt[r, v_rows, keys] = dot_nt(d_mine[:, lanes], prob.astype(BF16)).astype(BF16)
                d_query = (d_query + jnp.concatenate(own_dq, axis=1)) * HD ** (-0.5)
                rows = pl.ds(pl.multiple_of(r * BLOCK + head * HD, HD), HD)
                dqt[rows] = d_query.astype(BF16)
                dkvt[r, k_rows, :PROMPT] = dot_nt(q_mine, ds_scr[head]).astype(BF16)
                dkvt[r, v_rows, :PROMPT] = dot_nt(d_mine, p_scr[head]).astype(BF16)
            if grads is not None:
                self.projection_grads(r, pair, *grads, dkvt, dqt)
            if between is not None:
                between(n)
            return carry

        lax.fori_loop(0, kvt.shape[0], step, 0)

    def projection_grads(self, r, rows, xp, xc, xo, gw, dkvt, dqt):
        put(gw, r, slice(0, BLOCK), dot_nt(xo[...], dqt[rows]))
        both = dot_nt(xp[...], dkvt[r, :, :PROMPT]) + dot_nt(xc[...], dkvt[r, :, PROMPT:])
        put(gw, r, slice(BLOCK, 3 * BLOCK), both)

    def input_grads(self, xp, xc, xo, w, dkvt, dqt, dsa, gp, gc, gw, dx, dxo):
        for r in range(w.shape[0]):
            wq, wkv = w[r, :, :BLOCK], w[r, :, BLOCK : 3 * BLOCK]
            part = dot_nn(wkv, dkvt[r])
            rows = slice(r * BLOCK, (r + 1) * BLOCK)
            own = dot_nn(wq, dqt[rows])
            if r == 0:
                dx[...] = part
                dxo[...] = dsa[...] + own
            else:
                dx[...] += part
                dxo[...] += own
            self.projection_grads(r, rows, xp, xc, xo, gw, dkvt, dqt)
        low, high = self.own_columns()
        dx[:, low] += dxo[:, :BLOCK]
        dx[:, high] += dxo[:, BLOCK:PAIR]
        gp[...] = dx[:, :PROMPT].astype(BF16)
        gc[...] = (dx[:, PROMPT:] + dxo[:, PAIR:]).astype(BF16)

    def middle(
        self, xo, tdo, w, vec, att, xb, gw, sm, d_att, delta, dsa, hid, acc, ba,
        tokens_ready=None, outputs_ready=None, grads_ready=None, back_done=None,
    ):
        nrow, full = w.shape[0], w.shape[1]
        ff = (w.shape[2] - 4 * BLOCK) // 2
        up, down = slice(4 * BLOCK, 4 * BLOCK + ff), slice(4 * BLOCK + ff, 4 * BLOCK + 2 * ff)
        gain_a, bias_a, gain_f, bias_f = (vec[:, i : i + 1].astype(F32) for i in range(4))
        w_o = jnp.concatenate([w[r, :, 3 * BLOCK : 4 * BLOCK] for r in range(nrow)], axis=1)
        ba[...] = dot_nn(w_o, att[...])
        x_one, unit_a, inv_a = norm_forward(xo[...].astype(F32) + ba[...], gain_a, bias_a)
        x_low = x_one.astype(BF16)
        x_low_t = x_low.T
        acc[...] = jnp.zeros_like(acc)

        def up_down(r, carry):
            pre = dot_nn(x_low_t, w[r, :, up])
            hidden = jnp.maximum(pre, 0.0).astype(BF16)
            hid[r] = hidden
            acc[...] += dot_nt(w[r, :, down], hidden)
            return carry

        lax.fori_loop(0, nrow, up_down, 0)
        branch_f = acc[...]
        x_two, unit_f, inv_f = norm_forward(x_one + branch_f, gain_f, bias_f)
        branch = ba[...] + branch_f
        xb[0] = x_two.astype(BF16)
        xb[1] = branch.astype(BF16)
        if outputs_ready is not None:
            outputs_ready()
            tokens_ready()
        diff_x = x_two - tdo[0].astype(F32)
        diff_y = branch + tdo[1].astype(F32)
        loss = jnp.sum(self.live * (diff_x * diff_x + diff_y * diff_y))
        weight = self.live * (self.total_tokens / self.count)
        grad_y = diff_y * weight
        d_sum_f, gain_grad_f, bias_grad_f = norm_backward(diff_x * weight, unit_f, inv_f, gain_f)
        d_branch_f = (d_sum_f + grad_y).astype(BF16)
        d_branch_t = d_branch_f.T
        acc[...] = d_sum_f

        def back(n, carry):
            r = self.order(n)
            hidden = hid[r]
            d_hidden = dot_nn(d_branch_t, w[r, :, down])
            d_pre = jnp.where(hidden.astype(F32) > 0, d_hidden, 0.0).astype(BF16)
            put(gw, r, up, dot_nn(x_low, d_pre))
            put(gw, r, down, dot_nn(d_branch_f, hidden))
            acc[...] += dot_nt(w[r, :, up], d_pre)
            if grads_ready is not None:
                grads_ready(n)
            return carry

        lax.fori_loop(0, nrow, back, 0)
        if back_done is not None:
            back_done()
        d_sum_a, gain_grad_a, bias_grad_a = norm_backward(acc[...], unit_a, inv_a, gain_a)
        dsa[...] = d_sum_a
        d_branch_a = (d_sum_a + grad_y).astype(BF16)
        for r in range(nrow):
            rows = slice(r * BLOCK, (r + 1) * BLOCK)
            attended = att[rows]
            put(gw, r, slice(3 * BLOCK, 4 * BLOCK), dot_nt(d_branch_a, attended))
            d_here = dot_tn(w[r, :, 3 * BLOCK : 4 * BLOCK], d_branch_a).astype(BF16)
            d_att[rows] = d_here
            product = attended.astype(F32) * d_here.astype(F32)
            for head in range(2):
                delta[2 * r + head : 2 * r + head + 1] = jnp.sum(
                    product[head * HD : (head + 1) * HD], axis=0, keepdims=True
                )
        lane = iota((full, 128), 1)
        sums = jnp.zeros((full, 128), F32)
        for i, vector in enumerate((gain_grad_a, bias_grad_a, gain_grad_f, bias_grad_f)):
            sums = jnp.where(lane == i, vector, sums)
        sums = jnp.where(lane == 4, loss, sums)
        sums = sums.T[:8]
        for s in range(sm.shape[0]):
            sm[s] = sums[:, s * sm.shape[2] : (s + 1) * sm.shape[2]]


def layer_kernel(
    parts, lens_ref, len_table, xp, xc, tdo, w, vec, xb, gp, gc, gw, sm,
    xo, xt, kv, kvt, qt, att, lse, delta, d_att, dkvt, dqt, s_scr, pf_scr, p_scr, ds_scr,
    dsa, hid, acc, ba, dx,
):
    col = lax.axis_index("col")
    groups = lax.axis_size("col") // parts
    chip = lax.axis_index("dp") * lax.axis_size("row") + lax.axis_index("row")
    group = chip * groups + col // parts
    part = col % parts
    lens = [lens_ref[group, 0]] + [lens_ref[group, 1 + 2 * part + n] for n in range(2)]
    count = jnp.sum(len_table[...].astype(F32))
    layer = Layer(part, parts, lens, lens_ref.shape[0] * GROUP, count)
    layer.project(xp, xc, w, xo, xt, kv, kvt, qt)
    layer.attend(kv, kvt, qt, att, lse, s_scr, pf_scr)
    layer.middle(xo, tdo, w, vec, att, xb, gw, sm, d_att, delta, dsa, hid, acc, ba)
    layer.attend_back(kv, kvt, qt, lse, delta, d_att, dkvt, dqt, p_scr, ds_scr)
    layer.input_grads(xp, xc, xo, w, dkvt, dqt, dsa, gp, gc, gw, dx, acc)


def run_layer(lengths, xp, xc, tdo, weights, vec, parts):
    nrow, full, width = weights.shape
    own, keys = tdo.shape[2], xp.shape[1] + xc.shape[1]
    heads = full // HD
    vmem = pl.BlockSpec(memory_space=pltpu.VMEM)
    return pl.pallas_call(
        functools.partial(layer_kernel, parts),
        out_shape=(
            jax.ShapeDtypeStruct((2, full, own), BF16),
            jax.ShapeDtypeStruct(xp.shape, BF16),
            jax.ShapeDtypeStruct(xc.shape, BF16),
            jax.ShapeDtypeStruct(weights.shape, BF16),
            jax.ShapeDtypeStruct((1, 8, full), F32),
        ),
        in_specs=[pl.BlockSpec(memory_space=pltpu.SMEM)] + [vmem] * 6,
        out_specs=[vmem] * 5,
        scratch_shapes=[
            pltpu.VMEM((full, own), BF16),
            pltpu.VMEM((keys, full), BF16),
            pltpu.VMEM((keys, nrow * PAIR), BF16),
            pltpu.VMEM((nrow, PAIR, keys), BF16),
            pltpu.VMEM((full, own), BF16),
            pltpu.VMEM((full, own), BF16),
            pltpu.VMEM((heads, own), F32),
            pltpu.VMEM((heads, own), F32),
            pltpu.VMEM((full, own), BF16),
            pltpu.VMEM((nrow, PAIR, keys), BF16),
            pltpu.VMEM((full, own), BF16),
            pltpu.VMEM((2, PROMPT, PAIR), F32),
            pltpu.VMEM((2, PROMPT, PAIR), BF16),
            pltpu.VMEM((2, PROMPT, own), BF16),
            pltpu.VMEM((2, PROMPT, own), BF16),
            pltpu.VMEM((full, own), F32),
            pltpu.VMEM((nrow, own, (width - 4 * BLOCK) // 2), BF16),
            pltpu.VMEM((full, own), F32),
            pltpu.VMEM((full, own), F32),
            pltpu.VMEM((full, keys), F32),
        ],
        compiler_params=pltpu.CompilerParams(vmem_limit_bytes=60 << 20),
        name="layer",
    )(lengths, lengths, xp, xc, tdo, weights, vec)


class Line:
    def __init__(self, c):
        self.c = c
        self.mid = c * (3 - c) // 2 == 1
        self.end = c * (3 - c) // 2 == 0
        inner = c * (3 - c) // 2
        far = 3 * (1 - c // 2)
        one = c - 1 + 2 * ((4 - c) // 4)
        self.near = [c, one, 6 - c - one - far, far]
        self.pass_to = [None, c + 1, c - 1, 3 * (c - 1)]
        last = 1 + c % 2
        second = 6 - c - far - last
        self.far = [far, second, last, c]
        self.sum_to = [last, last + inner * (second - last), last]
        self.slot = [far, second + 4 * inner * (2 - c), last + c // 2 * (4 - last)]


class Traffic:
    def __init__(self, at):
        self.at = at
        self.pending = {}

    def start(self, key, make, cond=None):
        if cond is None:
            make().start()
        else:
            pl.when(cond)(lambda: make().start())
        self.pending[key] = (make, cond)

    def send(self, key, src, dst, send_sem, recv_sem, device, cond=None):
        self.start(key, lambda: remote(src(), dst(), send_sem(), recv_sem(), device), cond)

    def landed(self, dst, recv_sem):
        remote(dst, dst, recv_sem, recv_sem, self.at.sibling).wait_recv()

    def drain(self):
        for make, cond in self.pending.values():
            if cond is None:
                make().wait_send()
            else:
                pl.when(cond)(lambda make=make: make().wait_send())


def at_index(ref, *index):
    return ref.at[index]


class WeightGather:
    def __init__(self, tag, traffic, line, w, cols, feat, sems):
        self.tag, self.t, self.at, self.line = tag, traffic, traffic.at, line
        self.w, self.cols, self.feat = w, cols, feat
        self.col_s, self.col_r, self.one_s, self.one_r, self.two_s, self.two_r, self.sib_s, self.sib_r = sems

    def piece(self, row, c, core):
        half = self.feat // 2
        rows = pl.ds(pl.multiple_of(c * self.feat + core * half, half), half)
        return self.w.at[row, rows, self.cols]

    def move(self, key, row, c, send_sem, recv_sem, device, cond=None):
        here = functools.partial(self.piece, row, c, self.at.dp)
        self.t.send(
            (self.tag,) + key, here, here,
            lambda: at_index(*send_sem), lambda: at_index(*recv_sem), device, cond,
        )

    def own(self):
        at, line = self.at, self.line
        c = line.c
        for i in range(2):
            self.move(
                ("own", i), at.row, c, (self.col_s, i), (self.col_r, c),
                at.col_dev(line.near[1 + i]), line.mid if i else None,
            )
        self.rows(0)

    def rows(self, j):
        at, c = self.at, self.line.near[j]
        self.move(("one", j), at.row, c, (self.one_s, j), (self.one_r, j), at.first_dev)
        self.move(("two", j), at.row, c, (self.two_s, 0, j), (self.two_r, 0, j), at.second_dev)
        if j:
            self.move(("sib", j), at.row, c, (self.sib_s, 0, j), (self.sib_r, 0, j), at.sibling)

    def arrive(self, j):
        at, c = self.at, self.line.near[j]
        self.t.landed(self.piece(at.row, c, at.dp), self.col_r.at[c])
        self.move(
            ("pass", j), at.row, c, (self.col_s, 1 + j), (self.col_r, c),
            at.col_dev(self.line.pass_to[j]), self.line.mid,
        )
        self.rows(j)

    def first(self, j):
        at, c = self.at, self.line.near[j]
        self.t.landed(self.piece(at.first, c, at.dp), self.one_r.at[j])
        self.move(("far", j), at.first, c, (self.two_s, 1, j), (self.two_r, 1, j), at.second_dev)
        self.move(("sib1", j), at.first, c, (self.sib_s, 1, j), (self.sib_r, 1, j), at.sibling)

    def second(self, j):
        at, c = self.at, self.line.near[j]
        for i, row in ((0, at.second), (1, at.both)):
            self.t.landed(self.piece(row, c, at.dp), self.two_r.at[i, j])
            self.move(
                ("sib2", i, j), row, c, (self.sib_s, 2 + i, j), (self.sib_r, 2 + i, j), at.sibling
            )

    def finish(self):
        at = self.at
        for j in range(4):
            c, core = self.line.near[j], 1 - at.dp
            if j:
                self.t.landed(self.piece(at.row, c, core), self.sib_r.at[0, j])
            self.t.landed(self.piece(at.second, c, core), self.sib_r.at[1, j])
            self.t.landed(self.piece(at.first, c, core), self.sib_r.at[2, j])
            self.t.landed(self.piece(at.both, c, core), self.sib_r.at[3, j])


def row_order(row, n):
    return (row % 2 + (3 - n) // 2) % 2 + 2 * ((row // 2 + n + 1) % 2)


class LineSum:
    def __init__(self, tag, traffic, line, out, landing, sems):
        self.tag, self.t, self.line = tag, traffic, line
        self.out, self.landing = out, landing
        self.send_s, self.recv_s = sems

    def send(self, i, value):
        line = self.line
        s = line.far[i]

        @pl.when(line.mid)
        def _():
            self.t.landed(self.landing.at[s], self.recv_s.at[s])
            self.out[i] = (value() + self.landing[s].astype(F32)).astype(BF16)

        @pl.when(line.end)
        def _():
            self.out[i] = value().astype(BF16)

        self.t.send(
            (self.tag, "col", i),
            lambda: self.out.at[i], lambda: self.landing.at[line.slot[i]],
            lambda: self.send_s.at[i], lambda: self.recv_s.at[line.slot[i]],
            self.t.at.col_dev(line.sum_to[i]),
        )

    def receive(self, add):
        for slot, cond in ((self.line.c, self.line.c > 0), (4, self.line.c < 3)):

            @pl.when(cond)
            def _(slot=slot):
                self.t.landed(self.landing.at[slot], self.recv_s.at[slot])
                add(self.landing[slot].astype(F32))


class WeightScatter:
    def __init__(self, tag, traffic, line, gw, cols, sib, two, one, zs, zb, out, sems):
        self.tag, self.t, self.at, self.line = tag, traffic, traffic.at, line
        self.gw, self.cols = gw, cols
        self.sib, self.two, self.one, self.out = sib, two, one, out
        self.sib_s, self.sib_r, self.two_s, self.two_r, self.one_s, self.one_r = sems[:6]
        self.fin_s, self.fin_r = sems[8:]
        self.zs, self.zb, self.col_s, self.col_r = zs, zb, sems[6], sems[7]
        self.half = out.shape[0] // 2

    def begin(self, n):
        self.t.send(
            (self.tag, "sib", n),
            lambda: self.gw.at[row_order(self.at.row, n), :, 1 - self.at.dp, :, self.cols],
            lambda: self.sib.at[row_order(self.at.row, n)],
            lambda: self.sib_s.at[n], lambda: self.sib_r.at[n], self.at.sibling,
        )

    def across(self, n, row):
        self.t.send(
            (self.tag, "two", n),
            lambda: self.sib.at[row], lambda: self.two.at[n],
            lambda: self.two_s.at[n], lambda: self.two_r.at[n], self.at.second_dev,
        )

    def merge(self, n):
        r = row_order(self.at.row, n)
        self.t.landed(self.sib.at[r], self.sib_r.at[n])
        for c in range(4):
            here = self.gw[r, c, self.at.dp, :, self.cols]
            self.sib[r, c] = here + self.sib[r, c]
        if n == 0:
            self.across(1, self.at.both)
        if n == 2:
            self.across(0, self.at.second)

    def step2(self):
        self.t.landed(self.two.at[1], self.two_r.at[1])
        for c in range(4):
            self.two[1, c] = self.sib[self.at.first, c] + self.two[1, c]
        self.t.send(
            (self.tag, "one"),
            lambda: self.two.at[1], lambda: self.one,
            lambda: self.one_s, lambda: self.one_r, self.at.first_dev,
        )

    def total(self, c):
        near = self.sib[self.at.row, c].astype(F32) + self.two[0, c].astype(F32)
        return near + self.one[c].astype(F32)

    def step3(self):
        self.t.landed(self.two.at[0], self.two_r.at[0])
        self.t.landed(self.one, self.one_r)
        for k in range(1, 4):
            to = self.at.ahead(k)
            self.zs[k - 1] = self.total(to).astype(BF16)
            self.t.send(
                (self.tag, "col", k),
                lambda k=k: self.zs.at[k - 1], lambda k=k: self.zb.at[k - 1],
                lambda k=k: self.col_s.at[k - 1], lambda k=k: self.col_r.at[k - 1], self.at.col_dev(to),
            )

    def step4(self):
        mine = pl.ds(pl.multiple_of(self.at.dp * self.half, self.half), self.half)
        total = self.total(self.line.c)
        for k in range(3):
            self.t.landed(self.zb.at[k], self.col_r.at[k])
            total = total + self.zb[k].astype(F32)
        self.out[mine] = total
        self.t.send(
            (self.tag, "fin"),
            lambda: self.out.at[mine], lambda: self.out.at[mine],
            lambda: self.fin_s, lambda: self.fin_r, self.at.sibling,
        )

    def finish(self):
        other = pl.ds(pl.multiple_of((1 - self.at.dp) * self.half, self.half), self.half)
        self.t.landed(self.out.at[other], self.fin_r)


def step_kernel(
    parts, lens_ref, len_table, x_ref, y_hbm, tx_hbm, ty_hbm, wq_ref, wo_ref, wu_ref, wd_ref,
    va_ref, vb_ref, vc_ref, vd_ref,
    xbo, gco, gx_ref, out1, out2, gv_ref,
    y_ref, tx_ref, ty_ref, w, gw, xp, xc, xo, xt, kv, kvt, qt, att, lse, delta, d_att, s_scr, pf_scr, p_scr, ds_scr,
    dsa, hid, acc, ba, dx, dxo, tdp, tdo, xb, vrow, gpb, gxz, gcb, sm, smb, smz,
    sib1, two1, one1, zs1, zb1, sib2, two2, one2, zs2, zb2,
    xs, xr, cs, cr, ts, tr, vs, vr, bs, br, gs, gr, ks, kr, ss, sr, zs, zr, ls, *wsems,
):
    ncol = 4
    at = Places(ncol)
    t = Traffic(at)
    c = at.col
    line = Line(c)
    feat = x_ref.shape[0]
    own = xo.shape[1]
    cont = xc.shape[1]
    near, rest = slice(0, 4 * BLOCK), slice(4 * BLOCK, w.shape[2])

    def rows_of(s):
        return pl.ds(pl.multiple_of(s * feat, feat), feat)

    def own_cols(s):
        return pl.ds(pl.multiple_of(s * own, own), own)

    def cont_cols(s, first=0):
        return pl.ds(pl.multiple_of(first + s * cont, cont), cont)

    mine = rows_of(c)
    staged = [
        pltpu.make_async_copy(src, dst, ls.at[i])
        for i, (src, dst) in enumerate(((y_hbm, y_ref), (tx_hbm, tx_ref), (ty_hbm, ty_ref)))
    ]
    for copy in staged:
        copy.start()
    at.meet()
    gather1 = WeightGather("w1", t, line, w, near, feat, wsems[0:8])
    gather2 = WeightGather("w2", t, line, w, rest, feat, wsems[8:16])

    for i in range(3):
        w[at.row, mine, i * BLOCK : (i + 1) * BLOCK] = wq_ref[:, i, :]
    w[at.row, mine, 3 * BLOCK : 4 * BLOCK] = wo_ref[...].T
    gather1.own()
    ff = wu_ref.shape[1]
    w[at.row, mine, 4 * BLOCK : 4 * BLOCK + ff] = wu_ref[...]
    w[at.row, mine, 4 * BLOCK + ff :] = wd_ref[...].T
    gather2.own()
    for i in range(2):
        t.send(
            ("x", i),
            lambda: x_ref.at[:, :PROMPT], lambda: xp.at[mine],
            lambda i=i: xs.at[i], lambda: xr.at[c],
            at.col_dev(line.near[1 + i]), line.mid if i else None,
        )
    for k in range(1, ncol):
        to = at.ahead(k)
        t.send(
            ("xc", k),
            lambda to=to: x_ref.at[:, cont_cols(to, PROMPT)], lambda: xc.at[mine],
            lambda k=k: cs.at[k], lambda k=k: cr.at[k], at.col_dev(to),
        )
    local = [
        lambda: pltpu.make_async_copy(x_ref.at[:, :PROMPT], xp.at[mine], cs.at[0]),
        lambda: pltpu.make_async_copy(x_ref.at[:, cont_cols(c, PROMPT)], xc.at[mine], cr.at[0]),
    ]
    for make in local:
        make().start()
    rows = [ref[...].astype(F32).reshape(1, feat) for ref in (va_ref, vb_ref, vc_ref, vd_ref)]
    vrow[c] = jnp.concatenate(rows + rows, axis=0)
    for k in range(1, ncol):
        to = at.ahead(k)
        t.send(
            ("v", k),
            lambda: vrow.at[c], lambda: vrow.at[c],
            lambda k=k: vs.at[k], lambda k=k: vr.at[k], at.col_dev(to),
        )
    pieces = order_pieces(parts)
    for copy in staged:
        copy.wait()
    for to, frm, width in pieces:
        tdp[0, :, to : to + width] = tx_ref[:, frm : frm + width]
        y_here = y_ref[:, frm : frm + width].astype(F32)
        tdp[1, :, to : to + width] = (y_here - ty_ref[:, frm : frm + width].astype(F32)).astype(BF16)

    def x_arrive(j):
        s = line.near[j]
        t.landed(xp.at[rows_of(s)], xr.at[s])
        t.send(
            ("xpass", j),
            lambda: xp.at[rows_of(s)], lambda: xp.at[rows_of(s)],
            lambda: xs.at[1 + j], lambda: xr.at[s],
            at.col_dev(line.pass_to[j]), line.mid,
        )

    gather1.arrive(1)
    gather1.arrive(2)
    gather2.arrive(1)
    gather2.arrive(2)
    gather1.first(0)
    gather2.first(0)
    gather1.arrive(3)
    gather2.arrive(3)
    x_arrive(1)
    x_arrive(2)
    for j in range(1, 4):
        gather1.first(j)
    for j in range(4):
        gather1.second(j)
    gather2.first(1)
    gather2.first(2)
    gather2.second(0)
    x_arrive(3)
    gather2.first(3)
    for k in range(1, ncol):
        t.landed(xc.at[rows_of(at.behind(k))], cr.at[k])
    for make in local:
        make().wait()
    gather1.finish()

    group = at.dp * lax.axis_size("row") + at.row
    lens = [lens_ref[group, 0]] + [lens_ref[group, 1 + 2 * c + n] for n in range(2)]
    count = jnp.sum(len_table[...].astype(F32))
    total_tokens = lens_ref.shape[0] * GROUP
    layer = Layer(c, parts, lens, total_tokens, count, functools.partial(row_order, at.row))
    layer.project(xp, xc, w, xo, xt, kv, kvt, qt)

    for k in range(1, ncol):
        to = at.ahead(k)
        t.send(
            ("td", k),
            lambda to=to: tdp.at[:, :, own_cols(to)], lambda: tdo.at[:, mine],
            lambda k=k: ts.at[k], lambda k=k: tr.at[k], at.col_dev(to),
        )
    tdo[:, mine] = tdp[:, :, own_cols(c)]

    def forward_steps(r):
        @pl.when(r == 0)
        def _():
            gather2.second(1)

        @pl.when(r == 1)
        def _():
            gather2.second(2)

        @pl.when(r == 2)
        def _():
            gather2.second(3)

    layer.attend(kv, kvt, qt, att, lse, s_scr, pf_scr, forward_steps)
    for k in range(1, ncol):
        t.landed(vrow.at[at.behind(k)], vr.at[k])
    gather2.finish()
    vec = jnp.concatenate([vrow[s].T for s in range(ncol)], axis=0)

    def tokens_ready():
        for k in range(1, ncol):
            t.landed(tdo.at[:, rows_of(at.behind(k))], tr.at[k])

    def outputs_ready():
        for k in range(1, ncol):
            to = at.ahead(k)
            t.send(
                ("xb", k),
                lambda to=to: xb.at[:, rows_of(to)], lambda: xbo.at[:, :, own_cols(c)],
                lambda k=k: bs.at[k], lambda k=k: br.at[k], at.col_dev(to),
            )
        pltpu.make_async_copy(xb.at[:, mine], xbo.at[:, :, own_cols(c)], bs.at[0]).start()

    scatter1 = WeightScatter(
        "g1", t, line, gw, near, sib1, two1, one1, zs1, zb1, out1, wsems[16:26]
    )
    scatter2 = WeightScatter(
        "g2", t, line, gw, rest, sib2, two2, one2, zs2, zb2, out2, wsems[26:36]
    )
    x_sum = LineSum("gx", t, line, gpb, gxz, (gs, gr))

    def begin_after(scatter, n):
        for i in range(4):
            pl.when(n == i)(lambda i=i: scatter.begin(i))

    def back_done():
        scatter2.merge(0)
        scatter2.merge(1)

    layer.middle(
        xo, tdo, w, vec, att, xb, gw, sm, d_att, delta, dsa, hid, acc, ba,
        tokens_ready, outputs_ready, lambda n: begin_after(scatter2, n), back_done,
    )

    def small_send(i, src, device):
        t.send(
            ("sm", i), src, lambda: smb.at[i], lambda: ss.at[i], lambda: sr.at[i], device
        )

    small_send(0, lambda: sm, at.sibling)
    scatter2.merge(2)
    scatter2.merge(3)

    def back_steps(n):
        begin_after(scatter1, n)

        @pl.when(n == 0)
        def _():
            t.landed(smb.at[0], sr.at[0])
            smb[3] = sm[...] + smb[0]
            small_send(1, lambda: smb.at[3], at.second_dev)

        @pl.when(n == 1)
        def _():
            t.landed(smb.at[1], sr.at[1])
            smb[4] = smb[3] + smb[1]
            small_send(2, lambda: smb.at[4], at.first_dev)
            scatter2.step2()
            scatter1.merge(0)

        @pl.when(n == 2)
        def _():
            t.landed(smb.at[2], sr.at[2])
            smb[5] = smb[4] + smb[2]
            for k in range(1, ncol):
                to = at.ahead(k)
                t.send(
                    ("smz", k),
                    lambda to=to: smb.at[5, to], lambda k=k: smz.at[k],
                    lambda k=k: zs.at[k], lambda k=k: zr.at[k], at.col_dev(to),
                )
            scatter1.merge(1)

        @pl.when(n == 3)
        def _():
            scatter1.merge(2)

    layer.attend_back(
        kv, kvt, qt, lse, delta, d_att, kvt, qt, p_scr, ds_scr, back_steps, (xp, xc, xo, gw)
    )

    def grad_block(s):
        rows = rows_of(s)
        for r in range(w.shape[0]):
            part = dot_nn(w[r, rows, BLOCK : 3 * BLOCK], kvt[r])
            mine_part = dot_nn(w[r, rows, :BLOCK], qt[r * BLOCK : (r + 1) * BLOCK])
            if r == 0:
                dx[...] = part
                dxo[...] = dsa[rows] + mine_part
            else:
                dx[...] += part
                dxo[...] += mine_part
        low, high = layer.own_columns()
        dx[:, low] += dxo[:, :BLOCK]
        dx[:, high] += dxo[:, BLOCK:PAIR]
        dx[:, PROMPT:] += dxo[:, PAIR:]

    def grad_send(i):
        s = line.far[i]
        grad_block(s)
        x_sum.send(i, lambda: dx[:, :PROMPT])
        gcb[i] = dx[:, PROMPT:].astype(BF16)
        t.send(
            ("gc", i),
            lambda: gcb.at[i], lambda: gco.at[c],
            lambda: ks.at[i], lambda: kr.at[c], at.col_dev(s),
        )

    grad_send(0)
    scatter1.merge(3)
    scatter2.step3()
    grad_send(1)
    scatter1.step2()
    scatter1.step3()
    grad_send(2)
    grad_block(c)
    gx_ref[...] = dx[:, :PROMPT]
    gcb[3] = dx[:, PROMPT:].astype(BF16)
    own_copies = [
        pltpu.make_async_copy(xb.at[:, mine], xbo.at[:, :, own_cols(c)], bs.at[0]),
        pltpu.make_async_copy(gcb.at[3], gco.at[c], kr.at[4]),
    ]
    own_copies[1].start()

    for k in range(1, ncol):
        t.landed(xbo.at[:, :, own_cols(at.behind(k))], br.at[k])
    scatter2.step4()
    scatter1.step4()
    small = smb[5, c]
    for k in range(1, ncol):
        t.landed(smz.at[k], zr.at[k])
        small = small + smz[k]
    gv_ref[...] = small
    for k in range(1, ncol):
        s = at.behind(k)
        t.landed(gco.at[s], kr.at[s])

    def add_grad(value):
        gx_ref[...] += value

    x_sum.receive(add_grad)
    scatter2.finish()
    scatter1.finish()
    for copy in own_copies:
        copy.wait()
    t.drain()


def order_pieces(parts):
    own, cont = GROUP // parts, NCONT * CONT // parts
    pieces = []
    for p in range(parts):
        pieces.append((p * own, p * BLOCK, BLOCK))
        pieces.append((p * own + BLOCK, (2 * parts - 1 - p) * BLOCK, BLOCK))
        pieces.append((p * own + PAIR, PROMPT + p * cont, cont))
    return pieces


def finish_kernel(
    parts, full, lens_ref, len_table, y_ref, ty_ref, xbo, gco, gp_ref, out1, out2, sums,
    xout_ref, yout_ref, gx_ref, gy_ref, gq_ref, go_ref, gu_ref, gd_ref,
    ga_ref, gb_ref, gc_ref, gd2_ref, loss_ref,
):
    group = lax.axis_index("dp") * lax.axis_size("row") + lax.axis_index("row")
    count = jnp.sum(len_table[...].astype(F32))
    slot = iota((1, CONT), 1)
    live = [(iota((1, PROMPT), 1) < lens_ref[group, 0]).astype(F32)]
    live += [(slot < lens_ref[group, 1 + n]).astype(F32) for n in range(NCONT)]
    weight = jnp.concatenate(live, axis=1) * (lens_ref.shape[0] * GROUP / count)
    for frm, to, width in order_pieces(parts):
        cols = slice(to, to + width)
        xout_ref[:, cols] = xbo[0, :, frm : frm + width]
        branch = xbo[1, :, frm : frm + width].astype(F32)
        y_here = y_ref[:, cols].astype(F32)
        yout_ref[:, cols] = (y_here + branch).astype(BF16)
        gy_ref[:, cols] = (y_here - ty_ref[:, cols].astype(F32) + branch) * weight[:, cols]
    gx_ref[:, :PROMPT] = gp_ref[...]
    cont = gco.shape[2]
    for p in range(parts):
        gx_ref[:, PROMPT + p * cont : PROMPT + (p + 1) * cont] = gco[p].astype(F32)
    ff = gu_ref.shape[1]
    for i in range(3):
        gq_ref[:, i, :] = out1[:, i * BLOCK : (i + 1) * BLOCK]
    go_ref[...] = out1[:, 3 * BLOCK :].T
    gu_ref[...] = out2[:, :ff]
    gd_ref[...] = out2[:, ff:].T
    for i, ref in enumerate((ga_ref, gb_ref, gc_ref, gd2_ref)):
        ref[...] = sums[i : i + 1].reshape(ref.shape)
    loss_ref[...] = sums[4:5, :1] / (2.0 * count * full)


def run_step(lengths, x, y, tx, ty, wq, wo, wu, wd, vecs):
    feat, tokens = x.shape
    full = 4 * feat
    ff = wu.shape[1]
    width = 4 * BLOCK + 2 * ff
    rest = 2 * ff
    half = feat // 2
    own, cont = tokens // 4, NCONT * CONT // 4
    keys = PROMPT + cont
    heads = full // HD
    vmem = pl.BlockSpec(memory_space=pltpu.VMEM)
    dma = pltpu.SemaphoreType.DMA

    def bf(*shape):
        return pltpu.VMEM(shape, BF16)

    def f32(*shape):
        return pltpu.VMEM(shape, F32)

    def reduce_buffers(cols):
        return [
            bf(4, 4, half, cols), bf(2, 4, half, cols), bf(4, half, cols), bf(3, half, cols),
            bf(3, half, cols),
        ]

    gather_sems = [
        dma((5,)), dma((4,)), dma((4,)), dma((4,)), dma((2, 4)), dma((2, 4)), dma((4, 4)), dma((4, 4)),
    ]
    scatter_sems = [
        dma((4,)), dma((4,)), dma((2,)), dma((2,)), dma(()), dma(()), dma((3,)), dma((3,)),
        dma(()), dma(()),
    ]
    sums = (4, 8, feat)
    smem, anywhere = pl.BlockSpec(memory_space=pltpu.SMEM), pl.BlockSpec(memory_space=pl.ANY)

    def shape(*dims, dtype=F32):
        return jax.ShapeDtypeStruct(dims, dtype)

    raw = pl.pallas_call(
        functools.partial(step_kernel, 4),
        out_shape=(
            shape(2, feat, tokens, dtype=BF16), shape(4, feat, cont, dtype=BF16), shape(feat, PROMPT),
            shape(feat, 4 * BLOCK), shape(feat, rest), shape(8, feat),
        ),
        in_specs=[smem, vmem] + [anywhere] * 4 + [vmem] * 8,
        out_specs=[anywhere] * 2 + [vmem] * 4,
        scratch_shapes=[
            bf(feat, tokens), bf(feat, tokens), bf(feat, tokens),
            bf(4, full, width), bf(4, 4, 2, half, width), bf(full, PROMPT), bf(full, cont), bf(full, own),
            bf(keys, full), bf(keys, 4 * PAIR), bf(4, PAIR, keys), bf(full, own), bf(full, own),
            f32(heads, own), f32(heads, own), bf(full, own), f32(2, PROMPT, PAIR), bf(2, PROMPT, PAIR),
            bf(2, PROMPT, own), bf(2, PROMPT, own), f32(full, own), bf(4, own, ff), f32(full, own),
            f32(full, own), f32(feat, keys), f32(feat, own), bf(2, feat, tokens), bf(2, full, own),
            bf(2, full, own), f32(4, 8, feat), bf(3, feat, PROMPT),
            bf(5, feat, PROMPT), bf(4, feat, cont),
            f32(*sums), f32(6, *sums), f32(*sums),
        ]
        + reduce_buffers(4 * BLOCK)
        + reduce_buffers(rest)
        + [
            dma((5,)), dma((4,)), dma((4,)), dma((4,)), dma((4,)), dma((4,)), dma((4,)), dma((4,)),
            dma((4,)), dma((4,)), dma((3,)), dma((5,)), dma((3,)), dma((5,)), dma((3,)), dma((3,)),
            dma((4,)), dma((4,)), dma((3,)),
        ]
        + gather_sems * 2
        + scatter_sems * 2,
        compiler_params=pltpu.CompilerParams(
            collective_id=2, has_side_effects=True, vmem_limit_bytes=61 << 20
        ),
        name="layer_step",
    )(lengths, lengths, x, y, tx, ty, wq, wo, wu, wd, *vecs)
    return pl.pallas_call(
        functools.partial(finish_kernel, 4, full),
        out_shape=(
            shape(feat, tokens, dtype=BF16), shape(feat, tokens, dtype=BF16), shape(feat, tokens),
            shape(feat, tokens), shape(*wq.shape), shape(*wo.shape), shape(*wu.shape),
            shape(*wd.shape), shape(feat), shape(feat), shape(feat), shape(feat), shape(1, 1),
        ),
        in_specs=[smem] + [vmem] * 9,
        out_specs=[vmem] * 13,
        compiler_params=pltpu.CompilerParams(vmem_limit_bytes=61 << 20),
        name="layer_results",
    )(lengths, lengths, y, ty, *raw)


def body(
    x_stream, y_stream, w_qkv, w_out, gain_attn, bias_attn, w_up, w_down, gain_ffn, bias_ffn,
    teach_x, teach_y, lengths,
):
    ncol, nrow = lax.axis_size("col"), lax.axis_size("row")
    feat, tokens = x_stream.shape
    full = feat * ncol
    groups_here = tokens // GROUP
    parts = ncol // groups_here
    assert parts * 2 * BLOCK == PROMPT and nrow == 4
    block = w_qkv.shape[2]
    ff_block = w_up.shape[1]

    if ncol == parts:
        (
            x_out, y_out, grad_x, grad_y, g_q, g_o, g_u, g_d, g_ga, g_ba, g_gf, g_bf, loss,
        ) = run_step(
            lengths, x_stream, y_stream, teach_x, teach_y, w_qkv, w_out, w_up, w_down,
            (gain_attn, bias_attn, gain_ffn, bias_ffn),
        )
        return (
            x_out, y_out, grad_x, grad_y, g_q, g_o, g_ga, g_ba, g_u, g_d, g_gf, g_bf,
            loss.reshape(()),
        )

    y_f32 = y_stream.astype(F32)
    dy = y_f32 - teach_y.astype(F32)
    teach_dy = to_parts(jnp.stack([teach_x, dy.astype(BF16)]), parts)
    packed = jnp.concatenate([w_qkv.reshape(feat, 3 * block), w_out.T, w_up, w_down.T], axis=1)
    small_vecs = jnp.stack([gain_attn, bias_attn, gain_ffn, bias_ffn])
    vecs = lax.all_gather(small_vecs, "col", axis=1, tiled=True)

    x_prompt, x_cont, tdo, weights = gather_all(x_stream, teach_dy, packed, ncol, nrow, parts)

    first = (lax.axis_index("dp") * nrow + lax.axis_index("row")) * groups_here
    count_all = jnp.sum(lengths).astype(F32)
    total_tokens = lengths.shape[0] * GROUP
    vec = jnp.pad(vecs.T, ((0, 0), (0, 124)))
    xb, gp, gc, gw, small = run_layer(lengths, x_prompt, x_cont, tdo, weights, vec, parts)
    lanes = max(feat, 128)
    small = small[0].reshape(8, ncol, feat).transpose(1, 0, 2)
    small = jnp.pad(small, ((0, 0), (0, 0), (0, lanes - feat)))
    xb, gp, gc, gw, sums = scatter_all(xb, gp, gc, gw, small, ncol, parts)

    xb = from_parts(xb, parts)
    branch = xb[1].astype(F32)
    live_all = live_slots(
        lax.dynamic_slice_in_dim(lengths, first, groups_here, 0)
    ).reshape(1, tokens)
    y_out = (y_f32 + branch).astype(BF16)
    grad_y_out = (dy + branch) * (live_all * (total_tokens / count_all))
    gp = jnp.sum(gp.astype(F32), axis=0).reshape(feat, groups_here, PROMPT)
    gc = gc.astype(F32).reshape(feat, groups_here, NCONT * CONT)
    grad_x = jnp.concatenate([gp, gc], axis=2).reshape(feat, tokens)
    loss = sums[4, 0] / (2.0 * count_all * full)
    first_up = 4 * block
    return (
        xb[0],
        y_out,
        grad_x,
        grad_y_out,
        gw[:, : 3 * block].reshape(feat, 3, block),
        gw[:, 3 * block : 4 * block].T,
        sums[0, :feat],
        sums[1, :feat],
        gw[:, first_up : first_up + ff_block],
        gw[:, first_up + ff_block :].T,
        sums[2, :feat],
        sums[3, :feat],
        loss,
    )


def live_slots(lens):
    prompt = jnp.arange(PROMPT, dtype=jnp.int32)[None, :] < lens[:, 0:1]
    cont = jnp.arange(CONT, dtype=jnp.int32)[None, None, :] < lens[:, 1:, None]
    cont = cont.reshape(lens.shape[0], NCONT * CONT)
    return jnp.concatenate([prompt, cont], axis=1).astype(F32)


def solution(mesh):
    stream = P("col", ("dp", "row"))
    up, down = P("col", "row"), P("row", "col")
    qkv, vec = P("col", None, "row"), P("col")
    return jax.shard_map(
        body,
        mesh=mesh,
        in_specs=(
            stream, stream, qkv, down, vec, vec, up, down, vec, vec, stream, stream, P(),
        ),
        out_specs=(
            stream, stream, stream, stream, qkv, down, vec, vec, up, down, vec, vec, P(),
        ),
        check_vma=False,
    )
```

```python
import functools

import jax
import jax.numpy as jnp
from jax import lax
from jax.experimental import pallas as pl
from jax.experimental.pallas import tpu as pltpu
from jax.sharding import PartitionSpec as P

HD = 64
PROMPT = 1024
CONT = 128
NCONT = 8
GROUP = 2048
BLOCK = 128

EPS_NORM = 1e-05
NEG_FILL = -1000000000.0
MESH = pl.DeviceIdType.MESH
F32 = jnp.float32
BF16 = jnp.bfloat16


def flip_low(r):
    return r + 1 - 2 * (r % 2)


def flip_high(r):
    return (r + 2) % 4


class Places:
    def __init__(self, ncol):
        self.dp = lax.axis_index("dp")
        self.row = lax.axis_index("row")
        self.col = lax.axis_index("col")
        self.ncol = ncol
        low, high = flip_low(self.row), flip_high(self.row)
        self.first = low * (1 - self.dp) + high * self.dp
        self.second = high * (1 - self.dp) + low * self.dp
        self.both = 3 - self.row
        self.sibling = (1 - self.dp, self.row, self.col)
        self.first_dev = (self.dp, self.first, self.col)
        self.second_dev = (self.dp, self.second, self.col)
        self.aheads = [(self.col + k) % ncol for k in range(ncol)]
        self.behinds = [(self.col + ncol - k) % ncol for k in range(ncol)]

    def ahead(self, k):
        return self.aheads[k]

    def behind(self, k):
        return self.behinds[k]

    def col_dev(self, c):
        return (self.dp, self.row, c)

    def meet(self):
        barrier = pltpu.get_barrier_semaphore()
        partners = [self.sibling, self.first_dev, self.second_dev]
        partners += [self.col_dev(self.ahead(k)) for k in range(1, self.ncol)]
        for partner in partners:
            pl.semaphore_signal(barrier, inc=1, device_id=partner, device_id_type=MESH)
        pl.semaphore_wait(barrier, len(partners))


def remote(src, dst, send_sem, recv_sem, device):
    return pltpu.make_async_remote_copy(
        src_ref=src,
        dst_ref=dst,
        send_sem=send_sem,
        recv_sem=recv_sem,
        device_id=device,
        device_id_type=MESH,
    )


def gather_kernel(
    ncol, parts, x_ref, td_ref, w_ref, xp_ref, xc_ref, tdo_ref, g_ref,
    act_send, act_recv, col_send, col_recv, one_send, one_recv, two_send, two_recv,
    sib_send, sib_recv, local_sem,
):
    at = Places(ncol)
    feat = x_ref.shape[0]
    half = feat // 2
    own_tokens = tdo_ref.shape[2]
    own_cont = xc_ref.shape[1]

    def rows_of(c):
        return pl.ds(pl.multiple_of(c * feat, feat), feat)

    def half_rows(c, core):
        return pl.ds(pl.multiple_of(c * feat + core * half, half), half)

    def prompt_cols(c):
        return pl.ds(pl.multiple_of(c // parts * GROUP, GROUP), PROMPT)

    def cont_cols(c):
        return pl.ds(
            pl.multiple_of(c // parts * GROUP + PROMPT + c % parts * own_cont, own_cont), own_cont
        )

    def own_cols(c):
        return pl.ds(pl.multiple_of(c * own_tokens, own_tokens), own_tokens)

    at.meet()
    my_half = w_ref.at[pl.ds(pl.multiple_of(at.dp * half, half), half)]
    pending = []

    def start(copy):
        copy.start()
        pending.append(copy)
        return copy

    mine = rows_of(at.col)
    for i, (src, dst) in enumerate(
        (
            (x_ref.at[:, prompt_cols(at.col)], xp_ref.at[mine]),
            (x_ref.at[:, cont_cols(at.col)], xc_ref.at[mine]),
            (td_ref.at[:, :, own_cols(at.col)], tdo_ref.at[:, mine]),
            (w_ref, g_ref.at[at.row, mine]),
        )
    ):
        pltpu.make_async_copy(src, dst, local_sem.at[i]).start()

    for k in range(1, ncol):
        start(
            remote(
                my_half,
                g_ref.at[at.row, half_rows(at.col, at.dp)],
                col_send.at[k],
                col_recv.at[k],
                at.col_dev(at.ahead(k)),
            )
        )
    for k in range(1, ncol):
        to = at.ahead(k)
        dev = at.col_dev(to)
        start(
            remote(
                x_ref.at[:, prompt_cols(to)], xp_ref.at[mine],
                act_send.at[0, k], act_recv.at[0, k], dev,
            )
        )
        start(
            remote(
                x_ref.at[:, cont_cols(to)], xc_ref.at[mine],
                act_send.at[1, k], act_recv.at[1, k], dev,
            )
        )
    for k in range(1, ncol):
        to = at.ahead(k)
        start(
            remote(
                td_ref.at[:, :, own_cols(to)], tdo_ref.at[:, mine],
                act_send.at[2, k], act_recv.at[2, k], at.col_dev(to),
            )
        )

    def piece(row, k, core):
        return g_ref.at[row, half_rows(at.behind(k), core)]

    def landed(dst, recv_sem):
        remote(dst, dst, recv_sem, recv_sem, at.sibling).wait_recv()

    def chunk(k):
        return my_half if k == 0 else piece(at.row, k, at.dp)

    for k in range(ncol):
        if k:
            landed(piece(at.row, k, at.dp), col_recv.at[k])
        start(remote(chunk(k), piece(at.row, k, at.dp), one_send.at[k], one_recv.at[k], at.first_dev))
        start(
            remote(chunk(k), piece(at.row, k, at.dp), two_send.at[0, k], two_recv.at[0, k], at.second_dev)
        )
        if k:
            start(
                remote(chunk(k), piece(at.row, k, at.dp), sib_send.at[0, k], sib_recv.at[0, k], at.sibling)
            )
    for k in range(ncol):
        got = piece(at.first, k, at.dp)
        landed(got, one_recv.at[k])
        start(remote(got, got, two_send.at[1, k], two_recv.at[1, k], at.second_dev))
        start(remote(got, got, sib_send.at[1, k], sib_recv.at[1, k], at.sibling))
    for k in range(ncol):
        for i, row in ((0, at.second), (1, at.both)):
            got = piece(row, k, at.dp)
            landed(got, two_recv.at[i, k])
            start(remote(got, got, sib_send.at[2 + i, k], sib_recv.at[2 + i, k], at.sibling))

    for k in range(1, ncol):
        frm = rows_of(at.behind(k))
        landed(xp_ref.at[frm], act_recv.at[0, k])
        landed(xc_ref.at[frm], act_recv.at[1, k])
        landed(tdo_ref.at[:, frm], act_recv.at[2, k])
    other = 1 - at.dp
    for k in range(ncol):
        if k:
            landed(piece(at.row, k, other), sib_recv.at[0, k])
        landed(piece(at.second, k, other), sib_recv.at[1, k])
        landed(piece(at.first, k, other), sib_recv.at[2, k])
        landed(piece(at.both, k, other), sib_recv.at[3, k])
    for copy in pending:
        copy.wait_send()
    for i, (src, dst) in enumerate(
        (
            (x_ref.at[:, prompt_cols(at.col)], xp_ref.at[mine]),
            (x_ref.at[:, cont_cols(at.col)], xc_ref.at[mine]),
            (td_ref.at[:, :, own_cols(at.col)], tdo_ref.at[:, mine]),
            (w_ref, g_ref.at[at.row, mine]),
        )
    ):
        pltpu.make_async_copy(src, dst, local_sem.at[i]).wait()


def gather_all(x_stream, teach_dy, packed, ncol, nrow, parts):
    feat = x_stream.shape[0]
    full = feat * ncol
    own_tokens = GROUP // parts
    own_cont = NCONT * CONT // parts
    dma = pltpu.SemaphoreType.DMA
    anywhere = pl.BlockSpec(memory_space=pl.ANY)
    return pl.pallas_call(
        functools.partial(gather_kernel, ncol, parts),
        out_shape=(
            jax.ShapeDtypeStruct((full, PROMPT), BF16),
            jax.ShapeDtypeStruct((full, own_cont), BF16),
            jax.ShapeDtypeStruct((2, full, own_tokens), BF16),
            jax.ShapeDtypeStruct((nrow, full, packed.shape[1]), BF16),
        ),
        in_specs=[anywhere] * 3,
        out_specs=[anywhere] * 4,
        scratch_shapes=[
            dma((3, ncol)), dma((3, ncol)), dma((ncol,)), dma((ncol,)), dma((ncol,)), dma((ncol,)),
            dma((2, ncol)), dma((2, ncol)), dma((4, ncol)), dma((4, ncol)), dma((4,)),
        ],
        compiler_params=pltpu.CompilerParams(collective_id=0, has_side_effects=True),
        name="gather_all",
    )(x_stream, teach_dy, packed)


def scatter_kernel(
    ncol, parts, xb_ref, gp_ref, gc_ref, gw_ref, sm_ref,
    xbo_ref, gpo_ref, gco_ref, gwo_ref, smo_ref,
    sib_buf, two_buf, one_buf, col_buf, sm_buf, smc_buf,
    act_send, act_recv, sib_send, sib_recv, two_send, two_recv, one_send, one_recv,
    col_send, col_recv, fin_send, fin_recv, sm_send, sm_recv, smc_send, smc_recv, local_sem,
):
    at = Places(ncol)
    feat = xbo_ref.shape[1]
    half = feat // 2
    own_tokens = xb_ref.shape[2]
    own_cont = gc_ref.shape[1]
    part = at.col % parts

    def rows_of(c):
        return pl.ds(pl.multiple_of(c * feat, feat), feat)

    def half_rows(c, core):
        return pl.ds(pl.multiple_of(c * feat + core * half, half), half)

    def prompt_cols(c):
        return pl.ds(pl.multiple_of(c // parts * PROMPT, PROMPT), PROMPT)

    def cont_cols(c):
        return pl.ds(pl.multiple_of(c * own_cont, own_cont), own_cont)

    def own_cols(c):
        return pl.ds(pl.multiple_of(c * own_tokens, own_tokens), own_tokens)

    at.meet()
    pending = []

    def start(copy):
        copy.start()
        pending.append(copy)
        return copy

    def landed(dst, recv_sem):
        remote(dst, dst, recv_sem, recv_sem, at.sibling).wait_recv()

    other = 1 - at.dp
    order = list(range(1, ncol)) + [0]
    for k in order:
        start(
            remote(
                gw_ref.at[:, half_rows(at.ahead(k), other)], sib_buf.at[k],
                sib_send.at[k], sib_recv.at[k], at.sibling,
            )
        )
    start(remote(sm_ref, sm_buf.at[0], sm_send.at[0], sm_recv.at[0], at.sibling))

    def local_copies():
        mine = rows_of(at.col)
        return [
            pltpu.make_async_copy(src, dst, local_sem.at[i])
            for i, (src, dst) in enumerate(
                (
                    (xb_ref.at[:, mine], xbo_ref.at[:, :, own_cols(at.col)]),
                    (gp_ref.at[mine], gpo_ref.at[part, :, prompt_cols(at.col)]),
                    (gc_ref.at[mine], gco_ref.at[:, cont_cols(at.col)]),
                )
            )
        ]

    for copy in local_copies():
        copy.start()
    for k in range(1, ncol):
        to = at.ahead(k)
        dev = at.col_dev(to)
        start(
            remote(
                xb_ref.at[:, rows_of(to)], xbo_ref.at[:, :, own_cols(at.col)],
                act_send.at[0, k], act_recv.at[0, k], dev,
            )
        )
        start(
            remote(
                gp_ref.at[rows_of(to)], gpo_ref.at[part, :, prompt_cols(at.col)],
                act_send.at[1, k], act_recv.at[1, k], dev,
            )
        )
        start(
            remote(
                gc_ref.at[rows_of(to)], gco_ref.at[:, cont_cols(at.col)],
                act_send.at[2, k], act_recv.at[2, k], dev,
            )
        )

    for k in order:
        landed(sib_buf.at[k], sib_recv.at[k])
        for row in range(gw_ref.shape[0]):
            here = gw_ref.at[row, half_rows(at.ahead(k), at.dp)]
            sib_buf[k, row] = (here[...].astype(F32) + sib_buf[k, row].astype(F32)).astype(BF16)
        for i, row in ((0, at.second), (1, at.both)):
            start(
                remote(
                    sib_buf.at[k, row], two_buf.at[i, k],
                    two_send.at[i, k], two_recv.at[i, k], at.second_dev,
                )
            )
    landed(sm_buf.at[0], sm_recv.at[0])
    sm_buf[3] = sm_ref[...] + sm_buf[0]
    start(remote(sm_buf.at[3], sm_buf.at[1], sm_send.at[1], sm_recv.at[1], at.second_dev))
    for k in order:
        landed(two_buf.at[1, k], two_recv.at[1, k])
        two_buf[1, k] = (sib_buf[k, at.first].astype(F32) + two_buf[1, k].astype(F32)).astype(BF16)
        start(
            remote(
                two_buf.at[1, k], one_buf.at[k], one_send.at[k], one_recv.at[k], at.first_dev
            )
        )
    landed(sm_buf.at[1], sm_recv.at[1])
    sm_buf[4] = sm_buf[3] + sm_buf[1]
    start(remote(sm_buf.at[4], sm_buf.at[2], sm_send.at[2], sm_recv.at[2], at.first_dev))
    for k in order:
        landed(two_buf.at[0, k], two_recv.at[0, k])
        landed(one_buf.at[k], one_recv.at[k])
        total = sib_buf[k, at.row].astype(F32) + two_buf[0, k].astype(F32) + one_buf[k].astype(F32)
        if k:
            two_buf[0, k] = total.astype(BF16)
            start(
                remote(
                    two_buf.at[0, k], col_buf.at[k],
                    col_send.at[k], col_recv.at[k], at.col_dev(at.ahead(k)),
                )
            )
        else:
            own_total = total
    landed(sm_buf.at[2], sm_recv.at[2])
    sm_buf[5] = sm_buf[4] + sm_buf[2]
    for k in range(1, ncol):
        to = at.ahead(k)
        start(
            remote(
                sm_buf.at[5, to], smc_buf.at[k], smc_send.at[k], smc_recv.at[k], at.col_dev(to)
            )
        )
    for k in range(1, ncol):
        landed(col_buf.at[k], col_recv.at[k])
        own_total = own_total + col_buf[k].astype(F32)
    my_rows = pl.ds(pl.multiple_of(at.dp * half, half), half)
    gwo_ref[my_rows] = own_total
    start(remote(gwo_ref.at[my_rows], gwo_ref.at[my_rows], fin_send, fin_recv, at.sibling))
    small = sm_buf[5, at.col]
    for k in range(1, ncol):
        landed(smc_buf.at[k], smc_recv.at[k])
        small = small + smc_buf[k]
    smo_ref[...] = small
    landed(gwo_ref.at[pl.ds(pl.multiple_of(other * half, half), half)], fin_recv)
    for k in range(1, ncol):
        frm = at.behind(k)
        landed(xbo_ref.at[:, :, own_cols(frm)], act_recv.at[0, k])
        landed(gpo_ref.at[frm % parts, :, prompt_cols(frm)], act_recv.at[1, k])
        landed(gco_ref.at[:, cont_cols(frm)], act_recv.at[2, k])
    for copy in pending:
        copy.wait_send()
    for copy in local_copies():
        copy.wait()


def scatter_all(xb, gp, gc, gw, small, ncol, parts):
    nrow, full, width = gw.shape
    feat = full // ncol
    half = feat // 2
    groups = ncol // parts
    own_tokens, own_cont = xb.shape[2], gc.shape[1]
    dma = pltpu.SemaphoreType.DMA
    anywhere = pl.BlockSpec(memory_space=pl.ANY)
    vmem = pl.BlockSpec(memory_space=pltpu.VMEM)
    small_shape = small.shape
    return pl.pallas_call(
        functools.partial(scatter_kernel, ncol, parts),
        out_shape=(
            jax.ShapeDtypeStruct((2, feat, ncol * own_tokens), BF16),
            jax.ShapeDtypeStruct((parts, feat, groups * PROMPT), BF16),
            jax.ShapeDtypeStruct((feat, ncol * own_cont), BF16),
            jax.ShapeDtypeStruct((feat, width), F32),
            jax.ShapeDtypeStruct(small_shape[1:], F32),
        ),
        in_specs=[anywhere, anywhere, anywhere, vmem, vmem],
        out_specs=[anywhere, anywhere, anywhere, vmem, vmem],
        scratch_shapes=[
            pltpu.VMEM((ncol, nrow, half, width), BF16),
            pltpu.VMEM((2, ncol, half, width), BF16),
            pltpu.VMEM((ncol, half, width), BF16),
            pltpu.VMEM((ncol, half, width), BF16),
            pltpu.VMEM((6,) + small_shape, F32),
            pltpu.VMEM((ncol,) + small_shape[1:], F32),
            dma((3, ncol)), dma((3, ncol)), dma((ncol,)), dma((ncol,)), dma((2, ncol)), dma((2, ncol)),
            dma((ncol,)), dma((ncol,)), dma((ncol,)), dma((ncol,)), dma(()), dma(()),
            dma((3,)), dma((3,)), dma((ncol,)), dma((ncol,)), dma((3,)),
        ],
        compiler_params=pltpu.CompilerParams(
            collective_id=1, has_side_effects=True, vmem_limit_bytes=56 << 20
        ),
        name="scatter_all",
    )(xb, gp, gc, gw, small)


def to_parts(array_in, parts):
    lead = array_in.shape[:-1]
    groups = array_in.shape[-1] // GROUP
    split = array_in.reshape(lead + (groups, GROUP))
    prompt = split[..., :PROMPT].reshape(lead + (groups, 2, parts, BLOCK))
    prompt = jnp.stack([prompt[..., 0, :, :], prompt[..., 1, ::-1, :]], axis=-2)
    prompt = prompt.reshape(lead + (groups, parts, PROMPT // parts))
    cont = split[..., PROMPT:].reshape(lead + (groups, parts, NCONT * CONT // parts))
    return jnp.concatenate([prompt, cont], axis=-1).reshape(array_in.shape)


def from_parts(array_in, parts):
    lead = array_in.shape[:-1]
    groups = array_in.shape[-1] // GROUP
    split = array_in.reshape(lead + (groups, parts, GROUP // parts))
    prompt = split[..., : PROMPT // parts].reshape(lead + (groups, parts, 2, BLOCK))
    prompt = jnp.concatenate(
        [prompt[..., :, 0, :], prompt[..., ::-1, 1, :]], axis=-2
    ).reshape(lead + (groups, PROMPT))
    cont = split[..., PROMPT // parts :].reshape(lead + (groups, NCONT * CONT))
    return jnp.concatenate([prompt, cont], axis=-1).reshape(array_in.shape)


def norm_forward(summed, gain_vec, bias_vec):
    average = jnp.mean(summed, axis=0, keepdims=True)
    squares = jnp.mean(summed * summed, axis=0, keepdims=True)
    inv_scale = lax.rsqrt(squares - average * average + EPS_NORM)
    unit_val = (summed - average) * inv_scale
    return (unit_val * gain_vec + bias_vec, unit_val, inv_scale)


def norm_backward(upstream, unit_val, inv_scale, gain_vec):
    scaled = upstream * gain_vec
    first = jnp.mean(scaled, axis=0, keepdims=True)
    second = jnp.mean(scaled * unit_val, axis=0, keepdims=True)
    d_summed = inv_scale * (scaled - first - unit_val * second)
    sums = [jnp.sum(v, axis=1, keepdims=True) for v in (upstream * unit_val, upstream)]
    return (d_summed, *sums)


def dot_tn(lhs, rhs):
    return lax.dot_general(lhs, rhs, (((0,), (0,)), ((), ())), preferred_element_type=F32)


def dot_nn(lhs, rhs):
    return lax.dot_general(lhs, rhs, (((1,), (0,)), ((), ())), preferred_element_type=F32)


def dot_nt(lhs, rhs):
    return lax.dot_general(lhs, rhs, (((1,), (1,)), ((), ())), preferred_element_type=F32)


def iota(shape, axis):
    return lax.broadcasted_iota(jnp.int32, shape, axis)


def fold(array_in, op):
    return op(array_in.reshape(array_in.shape[0] // 8, 8, array_in.shape[1]), axis=0)


KEYS = 256
PAIR = 2 * BLOCK


def put(ref, r, cols, value):
    lead = ref.shape[1:-1]
    index = (r,) + (slice(None),) * len(lead) + (cols,)
    ref[index] = value.astype(BF16).reshape(lead + (value.shape[1],))


class Layer:
    def __init__(self, part, parts, lens, total_tokens, count, order=lambda n: n):
        self.part, self.parts = part, parts
        self.order = order
        self.lens = lens
        self.total_tokens, self.count = total_tokens, count
        slot = iota((1, BLOCK), 1)
        low, high = part * BLOCK + slot, (2 * parts - 1 - part) * BLOCK + slot
        last = lens[0] - 1
        self.bound = jnp.concatenate(
            [jnp.minimum(low, last), jnp.minimum(high, last), jnp.full((1, PAIR), last, jnp.int32)],
            axis=1,
        )
        live = [low < lens[0], high < lens[0]] + [slot < n for n in lens[1:]]
        self.live = jnp.concatenate([m.astype(F32) for m in live], axis=1)

    def own_columns(self):
        low = pl.ds(pl.multiple_of(self.part * BLOCK, BLOCK), BLOCK)
        high = pl.ds(pl.multiple_of((2 * self.parts - 1 - self.part) * BLOCK, BLOCK), BLOCK)
        return low, high

    def project(self, xp, xc, w, xo, xt, kv, kvt, qt):
        low, high = self.own_columns()
        xo[:, :BLOCK] = xp[:, low]
        xo[:, BLOCK:PAIR] = xp[:, high]
        xo[:, PAIR:] = xc[...]
        xt[:PROMPT] = xp[...].T
        xt[PROMPT:] = xc[...].T

        def step(r, carry):
            wq, wkv = w[r, :, :BLOCK], w[r, :, BLOCK : 3 * BLOCK]
            cols = pl.ds(pl.multiple_of(r * PAIR, PAIR), PAIR)
            kv[:, cols] = dot_nn(xt[...], wkv).astype(BF16)
            kvt[r, :, :PROMPT] = dot_tn(wkv, xp[...]).astype(BF16)
            kvt[r, :, PROMPT:] = dot_tn(wkv, xc[...]).astype(BF16)
            rows = pl.ds(pl.multiple_of(r * BLOCK, BLOCK), BLOCK)
            qt[rows] = (dot_tn(wq, xo[...]).astype(BF16).astype(F32) * HD ** (-0.5)).astype(BF16)
            return carry

        lax.fori_loop(0, w.shape[0], step, 0)

    def one_head(self, array_in, head):
        zeros = jnp.zeros((HD, array_in.shape[1]), array_in.dtype)
        mine = array_in[head * HD : (head + 1) * HD]
        return jnp.concatenate([mine, zeros] if head == 0 else [zeros, mine], axis=0)

    def masked(self, score, first_key, columns):
        keys = iota(score.shape, 0) + first_key
        return jnp.where(keys <= self.bound[:, columns], score, NEG_FILL)

    def masked_own(self, score, n):
        keys = iota(score.shape, 0)
        return jnp.where(
            (keys <= iota(score.shape, 1)) & (keys < self.lens[1 + n]), score, NEG_FILL
        )

    def attend(self, kv, kvt, qt, att, lse, s_scr, p_scr, between=None):
        def step(r, carry):
            k_cols = pl.ds(pl.multiple_of(r * PAIR, PAIR), BLOCK)
            q_pair = qt[pl.ds(pl.multiple_of(r * BLOCK, BLOCK), BLOCK)]
            for head in range(2):
                query = self.one_head(q_pair, head)
                v_rows = slice(BLOCK + head * HD, BLOCK + (head + 1) * HD)
                for b in range(2):
                    columns = slice(b * PAIR, (b + 1) * PAIR)
                    q_here = query[:, columns]
                    top = jnp.full((8, PAIR), NEG_FILL, F32)
                    for first in range(0, PROMPT, KEYS):
                        score = dot_nn(kv[first : first + KEYS, k_cols], q_here)
                        score = self.masked(score, first, columns)
                        s_scr[head, first : first + KEYS] = score
                        top = jnp.maximum(top, fold(score, jnp.max))
                    own_scores = []
                    if b == 1:
                        for n in range(2):
                            keys = slice(PROMPT + n * BLOCK, PROMPT + (n + 1) * BLOCK)
                            score = dot_nn(kv[keys, k_cols], q_here[:, n * BLOCK : (n + 1) * BLOCK])
                            own_scores.append(self.masked_own(score, n))
                        own_top = [fold(score, jnp.max) for score in own_scores]
                        top = jnp.maximum(top, jnp.concatenate(own_top, axis=1))
                    top = jnp.max(top, axis=0, keepdims=True)
                    total = jnp.zeros((8, PAIR), F32)
                    for first in range(0, PROMPT, KEYS):
                        prob = jnp.exp(s_scr[head, first : first + KEYS] - top)
                        total = total + fold(prob, jnp.sum)
                        p_scr[head, first : first + KEYS] = prob.astype(BF16)
                    out = dot_nn(kvt[r, v_rows, :PROMPT], p_scr[head])
                    if b == 1:
                        own_out, own_total = [], []
                        for n in range(2):
                            lanes = slice(n * BLOCK, (n + 1) * BLOCK)
                            prob = jnp.exp(own_scores[n] - top[:, lanes])
                            own_total.append(fold(prob, jnp.sum))
                            keys = slice(PROMPT + n * BLOCK, PROMPT + (n + 1) * BLOCK)
                            own_out.append(dot_nn(kvt[r, v_rows, keys], prob.astype(BF16)))
                        total = total + jnp.concatenate(own_total, axis=1)
                        out = out + jnp.concatenate(own_out, axis=1)
                    total = jnp.sum(total, axis=0, keepdims=True)
                    rows = pl.ds(pl.multiple_of(r * BLOCK + head * HD, HD), HD)
                    att[rows, columns] = (out / total).astype(BF16)
                    lse[pl.ds(2 * r + head, 1), columns] = top + jnp.log(total)
            if between is not None:
                between(r)
            return carry

        lax.fori_loop(0, kvt.shape[0], step, 0)

    def attend_back(
        self, kv, kvt, qt, lse, delta, d_att, dkvt, dqt, p_scr, ds_scr, between=None, grads=None,
        inputs=None,
    ):
        def step(n, carry):
            r = self.order(n)
            k_cols = pl.ds(pl.multiple_of(r * PAIR, PAIR), BLOCK)
            v_cols = pl.ds(pl.multiple_of(r * PAIR + BLOCK, BLOCK), BLOCK)
            pair = pl.ds(pl.multiple_of(r * BLOCK, BLOCK), BLOCK)
            q_pair, d_pair = qt[pair], d_att[pair]
            for head in range(2):
                query, d_out = self.one_head(q_pair, head), self.one_head(d_pair, head)
                q_mine = q_pair[head * HD : (head + 1) * HD]
                d_mine = d_pair[head * HD : (head + 1) * HD]
                k_rows = slice(head * HD, (head + 1) * HD)
                v_rows = slice(BLOCK + head * HD, BLOCK + (head + 1) * HD)
                norm = lse[pl.ds(2 * r + head, 1)]
                dlt = delta[pl.ds(2 * r + head, 1)]
                for b in range(2):
                    columns = slice(b * PAIR, (b + 1) * PAIR)
                    for first in range(0, PROMPT, KEYS):
                        keys = slice(first, first + KEYS)
                        score = dot_nn(kv[keys, k_cols], query[:, columns])
                        score = self.masked(score, first, columns)
                        prob = jnp.exp(score - norm[:, columns])
                        dprob = dot_nn(kv[keys, v_cols], d_out[:, columns])
                        p_scr[head, keys, columns] = prob.astype(BF16)
                        ds_scr[head, keys, columns] = (prob * (dprob - dlt[:, columns])).astype(BF16)
                d_query = dot_nn(kvt[r, k_rows, :PROMPT], ds_scr[head])
                own_dq = [jnp.zeros((HD, PAIR), F32)]
                for m in range(2):
                    keys = slice(PROMPT + m * BLOCK, PROMPT + (m + 1) * BLOCK)
                    lanes = slice(PAIR + m * BLOCK, PAIR + (m + 1) * BLOCK)
                    score = self.masked_own(dot_nn(kv[keys, k_cols], query[:, lanes]), m)
                    prob = jnp.exp(score - norm[:, lanes])
                    dprob = dot_nn(kv[keys, v_cols], d_out[:, lanes])
                    d_score = (prob * (dprob - dlt[:, lanes])).astype(BF16)
                    own_dq.append(dot_nn(kvt[r, k_rows, keys], d_score))
                    dkvt[r, k_rows, keys] = dot_nt(q_mine[:, lanes], d_score).astype(BF16)
                    dkvt[r, v_rows, keys] = dot_nt(d_mine[:, lanes], prob.astype(BF16)).astype(BF16)
                d_query = (d_query + jnp.concatenate(own_dq, axis=1)) * HD ** (-0.5)
                rows = pl.ds(pl.multiple_of(r * BLOCK + head * HD, HD), HD)
                dqt[rows] = d_query.astype(BF16)
                dkvt[r, k_rows, :PROMPT] = dot_nt(q_mine, ds_scr[head]).astype(BF16)
                dkvt[r, v_rows, :PROMPT] = dot_nt(d_mine, p_scr[head]).astype(BF16)
            if grads is not None:
                self.projection_grads(r, pair, *grads, dkvt, dqt)
            if inputs is not None:
                w, dx, dxo = inputs
                dx[...] += dot_nn(w[r, :, BLOCK : 3 * BLOCK], dkvt[r])
                dxo[...] += dot_nn(w[r, :, :BLOCK], dqt[pair])
            if between is not None:
                between(n)
            return carry

        lax.fori_loop(0, kvt.shape[0], step, 0)

    def projection_grads(self, r, rows, xp, xc, xo, gw, dkvt, dqt):
        put(gw, r, slice(0, BLOCK), dot_nt(xo[...], dqt[rows]))
        both = dot_nt(xp[...], dkvt[r, :, :PROMPT]) + dot_nt(xc[...], dkvt[r, :, PROMPT:])
        put(gw, r, slice(BLOCK, 3 * BLOCK), both)

    def input_grads(self, xp, xc, xo, w, dkvt, dqt, dsa, gp, gc, gw, dx, dxo):
        for r in range(w.shape[0]):
            wq, wkv = w[r, :, :BLOCK], w[r, :, BLOCK : 3 * BLOCK]
            part = dot_nn(wkv, dkvt[r])
            rows = slice(r * BLOCK, (r + 1) * BLOCK)
            own = dot_nn(wq, dqt[rows])
            if r == 0:
                dx[...] = part
                dxo[...] = dsa[...] + own
            else:
                dx[...] += part
                dxo[...] += own
            self.projection_grads(r, rows, xp, xc, xo, gw, dkvt, dqt)
        low, high = self.own_columns()
        dx[:, low] += dxo[:, :BLOCK]
        dx[:, high] += dxo[:, BLOCK:PAIR]
        gp[...] = dx[:, :PROMPT].astype(BF16)
        gc[...] = (dx[:, PROMPT:] + dxo[:, PAIR:]).astype(BF16)

    def middle(
        self, xo, tdo, w, vec, att, xb, gw, sm, d_att, delta, dsa, hid, acc, ba,
        tokens_ready=None, outputs_ready=None, grads_ready=None, back_done=None,
    ):
        nrow, full = w.shape[0], w.shape[1]
        ff = (w.shape[2] - 4 * BLOCK) // 2
        up, down = slice(4 * BLOCK, 4 * BLOCK + ff), slice(4 * BLOCK + ff, 4 * BLOCK + 2 * ff)
        gain_a, bias_a, gain_f, bias_f = (vec[:, i : i + 1].astype(F32) for i in range(4))
        w_o = jnp.concatenate([w[r, :, 3 * BLOCK : 4 * BLOCK] for r in range(nrow)], axis=1)
        ba[...] = dot_nn(w_o, att[...])
        x_one, unit_a, inv_a = norm_forward(xo[...].astype(F32) + ba[...], gain_a, bias_a)
        x_low = x_one.astype(BF16)
        x_low_t = x_low.T
        acc[...] = jnp.zeros_like(acc)

        def up_down(r, carry):
            pre = dot_nn(x_low_t, w[r, :, up])
            hidden = jnp.maximum(pre, 0.0).astype(BF16)
            hid[r] = hidden
            acc[...] += dot_nt(w[r, :, down], hidden)
            return carry

        lax.fori_loop(0, nrow, up_down, 0)
        branch_f = acc[...]
        x_two, unit_f, inv_f = norm_forward(x_one + branch_f, gain_f, bias_f)
        branch = ba[...] + branch_f
        xb[0] = x_two.astype(BF16)
        xb[1] = branch.astype(BF16)
        if outputs_ready is not None:
            outputs_ready()
            tokens_ready()
        diff_x = x_two - tdo[0].astype(F32)
        diff_y = branch + tdo[1].astype(F32)
        loss = jnp.sum(self.live * (diff_x * diff_x + diff_y * diff_y))
        weight = self.live * (self.total_tokens / self.count)
        grad_y = diff_y * weight
        d_sum_f, gain_grad_f, bias_grad_f = norm_backward(diff_x * weight, unit_f, inv_f, gain_f)
        d_branch_f = (d_sum_f + grad_y).astype(BF16)
        d_branch_t = d_branch_f.T
        acc[...] = d_sum_f

        def back(n, carry):
            r = self.order(n)
            hidden = hid[r]
            d_hidden = dot_nn(d_branch_t, w[r, :, down])
            d_pre = jnp.where(hidden.astype(F32) > 0, d_hidden, 0.0).astype(BF16)
            put(gw, r, up, dot_nn(x_low, d_pre))
            put(gw, r, down, dot_nn(d_branch_f, hidden))
            acc[...] += dot_nt(w[r, :, up], d_pre)
            if grads_ready is not None:
                grads_ready(n)
            return carry

        lax.fori_loop(0, nrow, back, 0)
        if back_done is not None:
            back_done()
        d_sum_a, gain_grad_a, bias_grad_a = norm_backward(acc[...], unit_a, inv_a, gain_a)
        dsa[...] = d_sum_a
        d_branch_a = (d_sum_a + grad_y).astype(BF16)
        for r in range(nrow):
            rows = slice(r * BLOCK, (r + 1) * BLOCK)
            attended = att[rows]
            put(gw, r, slice(3 * BLOCK, 4 * BLOCK), dot_nt(d_branch_a, attended))
            d_here = dot_tn(w[r, :, 3 * BLOCK : 4 * BLOCK], d_branch_a).astype(BF16)
            d_att[rows] = d_here
            product = attended.astype(F32) * d_here.astype(F32)
            for head in range(2):
                delta[2 * r + head : 2 * r + head + 1] = jnp.sum(
                    product[head * HD : (head + 1) * HD], axis=0, keepdims=True
                )
        lane = iota((full, 128), 1)
        sums = jnp.zeros((full, 128), F32)
        for i, vector in enumerate((gain_grad_a, bias_grad_a, gain_grad_f, bias_grad_f)):
            sums = jnp.where(lane == i, vector, sums)
        sums = jnp.where(lane == 4, loss, sums)
        sums = sums.T[:8]
        for s in range(sm.shape[0]):
            sm[s] = sums[:, s * sm.shape[2] : (s + 1) * sm.shape[2]]


def layer_kernel(
    parts, lens_ref, len_table, xp, xc, tdo, w, vec, xb, gp, gc, gw, sm,
    xo, xt, kv, kvt, qt, att, lse, delta, d_att, dkvt, dqt, s_scr, pf_scr, p_scr, ds_scr,
    dsa, hid, acc, ba, dx,
):
    col = lax.axis_index("col")
    groups = lax.axis_size("col") // parts
    chip = lax.axis_index("dp") * lax.axis_size("row") + lax.axis_index("row")
    group = chip * groups + col // parts
    part = col % parts
    lens = [lens_ref[group, 0]] + [lens_ref[group, 1 + 2 * part + n] for n in range(2)]
    count = jnp.sum(len_table[...].astype(F32))
    layer = Layer(part, parts, lens, lens_ref.shape[0] * GROUP, count)
    layer.project(xp, xc, w, xo, xt, kv, kvt, qt)
    layer.attend(kv, kvt, qt, att, lse, s_scr, pf_scr)
    layer.middle(xo, tdo, w, vec, att, xb, gw, sm, d_att, delta, dsa, hid, acc, ba)
    layer.attend_back(kv, kvt, qt, lse, delta, d_att, dkvt, dqt, p_scr, ds_scr)
    layer.input_grads(xp, xc, xo, w, dkvt, dqt, dsa, gp, gc, gw, dx, acc)


def run_layer(lengths, xp, xc, tdo, weights, vec, parts):
    nrow, full, width = weights.shape
    own, keys = tdo.shape[2], xp.shape[1] + xc.shape[1]
    heads = full // HD
    vmem = pl.BlockSpec(memory_space=pltpu.VMEM)
    return pl.pallas_call(
        functools.partial(layer_kernel, parts),
        out_shape=(
            jax.ShapeDtypeStruct((2, full, own), BF16),
            jax.ShapeDtypeStruct(xp.shape, BF16),
            jax.ShapeDtypeStruct(xc.shape, BF16),
            jax.ShapeDtypeStruct(weights.shape, BF16),
            jax.ShapeDtypeStruct((1, 8, full), F32),
        ),
        in_specs=[pl.BlockSpec(memory_space=pltpu.SMEM)] + [vmem] * 6,
        out_specs=[vmem] * 5,
        scratch_shapes=[
            pltpu.VMEM((full, own), BF16),
            pltpu.VMEM((keys, full), BF16),
            pltpu.VMEM((keys, nrow * PAIR), BF16),
            pltpu.VMEM((nrow, PAIR, keys), BF16),
            pltpu.VMEM((full, own), BF16),
            pltpu.VMEM((full, own), BF16),
            pltpu.VMEM((heads, own), F32),
            pltpu.VMEM((heads, own), F32),
            pltpu.VMEM((full, own), BF16),
            pltpu.VMEM((nrow, PAIR, keys), BF16),
            pltpu.VMEM((full, own), BF16),
            pltpu.VMEM((2, PROMPT, PAIR), F32),
            pltpu.VMEM((2, PROMPT, PAIR), BF16),
            pltpu.VMEM((2, PROMPT, own), BF16),
            pltpu.VMEM((2, PROMPT, own), BF16),
            pltpu.VMEM((full, own), F32),
            pltpu.VMEM((nrow, own, (width - 4 * BLOCK) // 2), BF16),
            pltpu.VMEM((full, own), F32),
            pltpu.VMEM((full, own), F32),
            pltpu.VMEM((full, keys), F32),
        ],
        compiler_params=pltpu.CompilerParams(vmem_limit_bytes=60 << 20),
        name="layer",
    )(lengths, lengths, xp, xc, tdo, weights, vec)


class Line:
    def __init__(self, c):
        self.c = c
        self.mid = c * (3 - c) // 2 == 1
        self.end = c * (3 - c) // 2 == 0
        inner = c * (3 - c) // 2
        far = 3 * (1 - c // 2)
        one = c - 1 + 2 * ((4 - c) // 4)
        self.near = [c, one, 6 - c - one - far, far]
        self.pass_to = [None, c + 1, c - 1, 3 * (c - 1)]
        last = 1 + c % 2
        second = 6 - c - far - last
        self.far = [far, second, last, c]
        self.sum_to = [last, last + inner * (second - last), last]
        self.slot = [far, second + 4 * inner * (2 - c), last + c // 2 * (4 - last)]


class Traffic:
    def __init__(self, at):
        self.at = at
        self.pending = {}

    def start(self, key, make, cond=None):
        if cond is None:
            make().start()
        else:
            pl.when(cond)(lambda: make().start())
        self.pending[key] = (make, cond)

    def send(self, key, src, dst, send_sem, recv_sem, device, cond=None):
        self.start(key, lambda: remote(src(), dst(), send_sem(), recv_sem(), device), cond)

    def landed(self, dst, recv_sem):
        remote(dst, dst, recv_sem, recv_sem, self.at.sibling).wait_recv()

    def drain(self):
        for make, cond in self.pending.values():
            if cond is None:
                make().wait_send()
            else:
                pl.when(cond)(lambda make=make: make().wait_send())


def at_index(ref, *index):
    return ref.at[index]


class WeightGather:
    def __init__(self, tag, traffic, line, w, cols, feat, sems):
        self.tag, self.t, self.at, self.line = tag, traffic, traffic.at, line
        self.w, self.cols, self.feat = w, cols, feat
        self.col_s, self.col_r, self.one_s, self.one_r, self.two_s, self.two_r, self.sib_s, self.sib_r = sems

    def piece(self, row, c, core):
        half = self.feat // 2
        rows = pl.ds(pl.multiple_of(c * self.feat + core * half, half), half)
        return self.w.at[row, rows, self.cols]

    def move(self, key, row, c, send_sem, recv_sem, device, cond=None):
        here = functools.partial(self.piece, row, c, self.at.dp)
        self.t.send(
            (self.tag,) + key, here, here,
            lambda: at_index(*send_sem), lambda: at_index(*recv_sem), device, cond,
        )

    def own(self):
        at, line = self.at, self.line
        c = line.c
        for i in range(2):
            self.move(
                ("own", i), at.row, c, (self.col_s, i), (self.col_r, c),
                at.col_dev(line.near[1 + i]), line.mid if i else None,
            )
        self.rows(0)

    def rows(self, j):
        at, c = self.at, self.line.near[j]
        self.move(("one", j), at.row, c, (self.one_s, j), (self.one_r, j), at.first_dev)
        self.move(("two", j), at.row, c, (self.two_s, 0, j), (self.two_r, 0, j), at.second_dev)
        if j:
            self.move(("sib", j), at.row, c, (self.sib_s, 0, j), (self.sib_r, 0, j), at.sibling)

    def arrive(self, j):
        at, c = self.at, self.line.near[j]
        self.t.landed(self.piece(at.row, c, at.dp), self.col_r.at[c])
        self.move(
            ("pass", j), at.row, c, (self.col_s, 1 + j), (self.col_r, c),
            at.col_dev(self.line.pass_to[j]), self.line.mid,
        )
        self.rows(j)

    def first(self, j):
        at, c = self.at, self.line.near[j]
        self.t.landed(self.piece(at.first, c, at.dp), self.one_r.at[j])
        self.move(("far", j), at.first, c, (self.two_s, 1, j), (self.two_r, 1, j), at.second_dev)
        self.move(("sib1", j), at.first, c, (self.sib_s, 1, j), (self.sib_r, 1, j), at.sibling)

    def second(self, j):
        at, c = self.at, self.line.near[j]
        for i, row in ((0, at.second), (1, at.both)):
            self.t.landed(self.piece(row, c, at.dp), self.two_r.at[i, j])
            self.move(
                ("sib2", i, j), row, c, (self.sib_s, 2 + i, j), (self.sib_r, 2 + i, j), at.sibling
            )

    def finish(self):
        at = self.at
        for j in range(4):
            c, core = self.line.near[j], 1 - at.dp
            if j:
                self.t.landed(self.piece(at.row, c, core), self.sib_r.at[0, j])
            self.t.landed(self.piece(at.second, c, core), self.sib_r.at[1, j])
            self.t.landed(self.piece(at.first, c, core), self.sib_r.at[2, j])
            self.t.landed(self.piece(at.both, c, core), self.sib_r.at[3, j])


def row_order(row, n):
    return (row % 2 + (3 - n) // 2) % 2 + 2 * ((row // 2 + n + 1) % 2)


class LineSum:
    def __init__(self, tag, traffic, line, out, landing, sems):
        self.tag, self.t, self.line = tag, traffic, line
        self.out, self.landing = out, landing
        self.send_s, self.recv_s = sems

    def move(self, i, cond):
        line = self.line
        self.t.send(
            (self.tag, "col", i, cond is line.mid),
            lambda: self.out.at[i], lambda: self.landing.at[line.slot[i]],
            lambda: self.send_s.at[i], lambda: self.recv_s.at[line.slot[i]],
            self.t.at.col_dev(line.sum_to[i]), cond,
        )

    def put(self, i, value):
        self.out[i] = value.astype(BF16)
        self.move(i, self.line.end)

    def relay(self, i):
        s = self.line.far[i]

        @pl.when(self.line.mid)
        def _():
            self.t.landed(self.landing.at[s], self.recv_s.at[s])
            self.out[i] = self.out[i] + self.landing[s]

        self.move(i, self.line.mid)

    def receive(self, add):
        for slot, cond in ((self.line.c, self.line.c > 0), (4, self.line.c < 3)):

            @pl.when(cond)
            def _(slot=slot):
                self.t.landed(self.landing.at[slot], self.recv_s.at[slot])
                add(self.landing[slot].astype(F32))


class WeightScatter:
    def __init__(self, tag, traffic, line, gw, cols, sib, two, one, zs, zb, out, sems):
        self.tag, self.t, self.at, self.line = tag, traffic, traffic.at, line
        self.gw, self.cols = gw, cols
        self.sib, self.two, self.one, self.out = sib, two, one, out
        self.sib_s, self.sib_r, self.two_s, self.two_r, self.one_s, self.one_r = sems[:6]
        self.fin_s, self.fin_r = sems[8:]
        self.zs, self.zb, self.col_s, self.col_r = zs, zb, sems[6], sems[7]
        self.half = out.shape[0] // 2

    def begin(self, n):
        self.t.send(
            (self.tag, "sib", n),
            lambda: self.gw.at[row_order(self.at.row, n), :, 1 - self.at.dp, :, self.cols],
            lambda: self.sib.at[row_order(self.at.row, n)],
            lambda: self.sib_s.at[n], lambda: self.sib_r.at[n], self.at.sibling,
        )

    def across(self, n, row):
        self.t.send(
            (self.tag, "two", n),
            lambda: self.sib.at[row], lambda: self.two.at[n],
            lambda: self.two_s.at[n], lambda: self.two_r.at[n], self.at.second_dev,
        )

    def merge(self, n):
        r = row_order(self.at.row, n)
        self.t.landed(self.sib.at[r], self.sib_r.at[n])
        for c in range(4):
            here = self.gw[r, c, self.at.dp, :, self.cols]
            self.sib[r, c] = here + self.sib[r, c]
        if n == 0:
            self.across(1, self.at.both)
        if n == 2:
            self.across(0, self.at.second)

    def step2(self):
        self.t.landed(self.two.at[1], self.two_r.at[1])
        for c in range(4):
            self.two[1, c] = self.sib[self.at.first, c] + self.two[1, c]
        self.t.send(
            (self.tag, "one"),
            lambda: self.two.at[1], lambda: self.one,
            lambda: self.one_s, lambda: self.one_r, self.at.first_dev,
        )

    def total(self, c):
        near = self.sib[self.at.row, c].astype(F32) + self.two[0, c].astype(F32)
        return near + self.one[c].astype(F32)

    def step3(self):
        self.t.landed(self.two.at[0], self.two_r.at[0])
        self.t.landed(self.one, self.one_r)
        c = self.line.c
        for i in range(3):
            to = self.line.far[i]
            self.zs[i] = self.total(to).astype(BF16)
            self.t.send(
                (self.tag, "col", i),
                lambda i=i: self.zs.at[i], lambda: self.zb.at[c],
                lambda i=i: self.col_s.at[i], lambda: self.col_r.at[c], self.at.col_dev(to),
            )

    def step4(self):
        mine = pl.ds(pl.multiple_of(self.at.dp * self.half, self.half), self.half)
        total = self.total(self.line.c)
        for s in self.line.near[1:]:
            self.t.landed(self.zb.at[s], self.col_r.at[s])
            total = total + self.zb[s].astype(F32)
        self.out[mine] = total
        self.t.send(
            (self.tag, "fin"),
            lambda: self.out.at[mine], lambda: self.out.at[mine],
            lambda: self.fin_s, lambda: self.fin_r, self.at.sibling,
        )

    def finish(self):
        other = pl.ds(pl.multiple_of((1 - self.at.dp) * self.half, self.half), self.half)
        self.t.landed(self.out.at[other], self.fin_r)


def step_kernel(
    parts, lens_ref, len_table, x_ref, y_hbm, tx_hbm, ty_hbm, wq_ref, wo_ref, wu_ref, wd_ref,
    va_ref, vb_ref, vc_ref, vd_ref,
    xbo, gco, gx_ref, out1, out2, gv_ref,
    y_ref, tx_ref, ty_ref, w, gw, xp, xc, xo, xt, kv, kvt, qt, att, lse, delta, d_att, s_scr, pf_scr, p_scr, ds_scr,
    dsa, hid, acc, ba, dx, tdp, tdo, xb, vrow, gpb, gxz, gcb, sm, smb, smz,
    sib1, two1, one1, zs1, zb1, sib2, two2, one2, zs2, zb2,
    xs, xr, cs, cr, ts, tr, vs, vr, bs, br, gs, gr, ks, kr, ss, sr, zs, zr, ls, *wsems,
):
    ncol = 4
    at = Places(ncol)
    t = Traffic(at)
    c = at.col
    line = Line(c)
    feat = x_ref.shape[0]
    own = xo.shape[1]
    cont = xc.shape[1]
    near, rest = slice(0, 4 * BLOCK), slice(4 * BLOCK, w.shape[2])

    def rows_of(s):
        return pl.ds(pl.multiple_of(s * feat, feat), feat)

    def own_cols(s):
        return pl.ds(pl.multiple_of(s * own, own), own)

    def cont_cols(s, first=0):
        return pl.ds(pl.multiple_of(first + s * cont, cont), cont)

    mine = rows_of(c)
    staged = [
        pltpu.make_async_copy(src, dst, ls.at[i])
        for i, (src, dst) in enumerate(((y_hbm, y_ref), (tx_hbm, tx_ref), (ty_hbm, ty_ref)))
    ]
    for copy in staged:
        copy.start()
    at.meet()
    gather1 = WeightGather("w1", t, line, w, near, feat, wsems[0:8])
    gather2 = WeightGather("w2", t, line, w, rest, feat, wsems[8:16])

    for i in range(3):
        w[at.row, mine, i * BLOCK : (i + 1) * BLOCK] = wq_ref[:, i, :]
    w[at.row, mine, 3 * BLOCK : 4 * BLOCK] = wo_ref[...].T
    gather1.own()
    ff = wu_ref.shape[1]
    w[at.row, mine, 4 * BLOCK : 4 * BLOCK + ff] = wu_ref[...]
    w[at.row, mine, 4 * BLOCK + ff :] = wd_ref[...].T
    gather2.own()
    for i in range(2):
        t.send(
            ("x", i),
            lambda: x_ref.at[:, :PROMPT], lambda: xp.at[mine],
            lambda i=i: xs.at[i], lambda: xr.at[c],
            at.col_dev(line.near[1 + i]), line.mid if i else None,
        )
    local = [
        lambda: pltpu.make_async_copy(x_ref.at[:, :PROMPT], xp.at[mine], ls.at[3]),
        lambda: pltpu.make_async_copy(x_ref.at[:, cont_cols(c, PROMPT)], xc.at[mine], ls.at[4]),
    ]
    for make in local:
        make().start()
    rows = [ref[...].astype(F32).reshape(1, feat) for ref in (va_ref, vb_ref, vc_ref, vd_ref)]
    vrow[c] = jnp.concatenate(rows + rows, axis=0)
    for k in range(1, ncol):
        to = at.ahead(k)
        t.send(
            ("v", k),
            lambda: vrow.at[c], lambda: vrow.at[c],
            lambda k=k: vs.at[k], lambda k=k: vr.at[k], at.col_dev(to),
        )
    pieces = order_pieces(parts)
    for copy in staged:
        copy.wait()
    for to, frm, width in pieces:
        tdp[0, :, to : to + width] = tx_ref[:, frm : frm + width]
        y_here = y_ref[:, frm : frm + width].astype(F32)
        tdp[1, :, to : to + width] = (y_here - ty_ref[:, frm : frm + width].astype(F32)).astype(BF16)

    def x_arrive(j):
        s = line.near[j]
        t.landed(xp.at[rows_of(s)], xr.at[s])
        t.send(
            ("xpass", j),
            lambda: xp.at[rows_of(s)], lambda: xp.at[rows_of(s)],
            lambda: xs.at[1 + j], lambda: xr.at[s],
            at.col_dev(line.pass_to[j]), line.mid,
        )

    gather1.arrive(1)
    gather1.arrive(2)
    gather1.first(0)
    gather2.arrive(1)
    gather2.arrive(2)
    gather2.first(0)
    gather1.arrive(3)
    gather1.first(1)
    gather1.first(2)
    gather2.arrive(3)
    x_arrive(1)
    x_arrive(2)
    for k, to in enumerate(line.near[1:]):
        t.send(
            ("xc", k),
            lambda to=to: x_ref.at[:, cont_cols(to, PROMPT)], lambda: xc.at[mine],
            lambda k=k: cs.at[k], lambda: cr.at[c], at.col_dev(to),
        )
    gather2.first(1)
    gather1.first(3)
    gather2.first(2)
    gather1.second(0)
    gather1.second(1)
    gather1.second(2)
    gather1.second(3)
    x_arrive(3)
    for s in line.near[1:]:
        t.landed(xc.at[rows_of(s)], cr.at[s])
    for make in local:
        make().wait()
    gather1.finish()

    group = at.dp * lax.axis_size("row") + at.row
    lens = [lens_ref[group, 0]] + [lens_ref[group, 1 + 2 * c + n] for n in range(2)]
    count = jnp.sum(len_table[...].astype(F32))
    total_tokens = lens_ref.shape[0] * GROUP
    layer = Layer(c, parts, lens, total_tokens, count, functools.partial(row_order, at.row))
    layer.project(xp, xc, w, xo, xt, kv, kvt, qt)

    for k, to in enumerate(line.near[1:]):
        t.send(
            ("td", k),
            lambda to=to: tdp.at[:, :, own_cols(to)], lambda: tdo.at[:, mine],
            lambda k=k: ts.at[k], lambda: tr.at[c], at.col_dev(to),
        )
    tdo[:, mine] = tdp[:, :, own_cols(c)]

    def forward_steps(r):
        @pl.when(r == 0)
        def _():
            gather2.first(3)

        @pl.when(r == 1)
        def _():
            gather2.second(0)
            gather2.second(1)

        @pl.when(r == 2)
        def _():
            gather2.second(2)

        @pl.when(r == 3)
        def _():
            gather2.second(3)

    layer.attend(kv, kvt, qt, att, lse, s_scr, pf_scr, forward_steps)
    for k in range(1, ncol):
        t.landed(vrow.at[at.behind(k)], vr.at[k])
    gather2.finish()
    vec = jnp.concatenate([vrow[s].T for s in range(ncol)], axis=0)

    def tokens_ready():
        for s in line.near[1:]:
            t.landed(tdo.at[:, rows_of(s)], tr.at[s])

    def outputs_ready():
        for k, to in enumerate(line.near[1:]):
            t.send(
                ("xb", k),
                lambda to=to: xb.at[:, rows_of(to)], lambda: xbo.at[:, :, own_cols(c)],
                lambda k=k: bs.at[k], lambda: br.at[c], at.col_dev(to),
            )
        pltpu.make_async_copy(xb.at[:, mine], xbo.at[:, :, own_cols(c)], ls.at[5]).start()

    scatter1 = WeightScatter(
        "g1", t, line, gw, near, sib1, two1, one1, zs1, zb1, out1, wsems[16:26]
    )
    scatter2 = WeightScatter(
        "g2", t, line, gw, rest, sib2, two2, one2, zs2, zb2, out2, wsems[26:36]
    )
    x_sum = LineSum("gx", t, line, gpb, gxz, (gs, gr))

    def begin_after(scatter, n):
        for i in range(4):
            pl.when(n == i)(lambda i=i: scatter.begin(i))

    def back_done():
        scatter2.merge(0)
        scatter2.merge(1)

    layer.middle(
        xo, tdo, w, vec, att, xb, gw, sm, d_att, delta, dsa, hid, acc, ba,
        tokens_ready, outputs_ready, lambda n: begin_after(scatter2, n), back_done,
    )

    def small_send(i, src, device):
        t.send(
            ("sm", i), src, lambda: smb.at[i], lambda: ss.at[i], lambda: sr.at[i], device
        )

    small_send(0, lambda: sm, at.sibling)
    scatter2.merge(2)
    scatter2.merge(3)

    def back_steps(n):
        begin_after(scatter1, n)

        @pl.when(n == 0)
        def _():
            t.landed(smb.at[0], sr.at[0])
            smb[3] = sm[...] + smb[0]
            small_send(1, lambda: smb.at[3], at.second_dev)

        @pl.when(n == 1)
        def _():
            t.landed(smb.at[1], sr.at[1])
            smb[4] = smb[3] + smb[1]
            small_send(2, lambda: smb.at[4], at.first_dev)
            scatter2.step2()
            scatter1.merge(0)

        @pl.when(n == 2)
        def _():
            t.landed(smb.at[2], sr.at[2])
            smb[5] = smb[4] + smb[2]
            for k in range(1, ncol):
                to = at.ahead(k)
                t.send(
                    ("smz", k),
                    lambda to=to: smb.at[5, to], lambda k=k: smz.at[k],
                    lambda k=k: zs.at[k], lambda k=k: zr.at[k], at.col_dev(to),
                )
            scatter1.merge(1)

        @pl.when(n == 3)
        def _():
            scatter1.merge(2)
            scatter1.step2()

    dx[...] = jnp.zeros_like(dx)
    acc[...] = dsa[...]
    layer.attend_back(
        kv, kvt, qt, lse, delta, d_att, kvt, qt, p_scr, ds_scr, back_steps, (xp, xc, xo, gw),
        (w, dx, acc),
    )

    low, high = layer.own_columns()
    dx[:, low] += acc[:, :BLOCK]
    dx[:, high] += acc[:, BLOCK:PAIR]
    dx[:, PROMPT:] += acc[:, PAIR:]

    def grad_send(i):
        s = line.far[i]
        x_sum.put(i, dx[rows_of(s), :PROMPT])
        gcb[i] = dx[rows_of(s), PROMPT:].astype(BF16)
        t.send(
            ("gc", i),
            lambda: gcb.at[i], lambda: gco.at[c],
            lambda: ks.at[i], lambda: kr.at[c], at.col_dev(s),
        )

    grad_send(0)
    scatter1.merge(3)
    scatter2.step3()
    grad_send(1)
    grad_send(2)
    gx_ref[...] = dx[mine, :PROMPT]
    gcb[3] = dx[mine, PROMPT:].astype(BF16)
    own_copies = [
        pltpu.make_async_copy(xb.at[:, mine], xbo.at[:, :, own_cols(c)], ls.at[5]),
        pltpu.make_async_copy(gcb.at[3], gco.at[c], ls.at[6]),
    ]
    own_copies[1].start()
    x_sum.relay(0)
    scatter1.step3()
    x_sum.relay(1)
    x_sum.relay(2)

    for s in line.near[1:]:
        t.landed(xbo.at[:, :, own_cols(s)], br.at[s])
    scatter2.step4()
    scatter1.step4()
    small = smb[5, c]
    for k in range(1, ncol):
        t.landed(smz.at[k], zr.at[k])
        small = small + smz[k]
    gv_ref[...] = small
    for k in range(1, ncol):
        s = at.behind(k)
        t.landed(gco.at[s], kr.at[s])

    def add_grad(value):
        gx_ref[...] += value

    x_sum.receive(add_grad)
    scatter2.finish()
    scatter1.finish()
    for copy in own_copies:
        copy.wait()
    t.drain()


def order_pieces(parts):
    own, cont = GROUP // parts, NCONT * CONT // parts
    pieces = []
    for p in range(parts):
        pieces.append((p * own, p * BLOCK, BLOCK))
        pieces.append((p * own + BLOCK, (2 * parts - 1 - p) * BLOCK, BLOCK))
        pieces.append((p * own + PAIR, PROMPT + p * cont, cont))
    return pieces


def finish_kernel(
    parts, full, lens_ref, len_table, y_ref, ty_ref, xbo, gco, gp_ref, out1, out2, sums,
    xout_ref, yout_ref, gx_ref, gy_ref, gq_ref, go_ref, gu_ref, gd_ref,
    ga_ref, gb_ref, gc_ref, gd2_ref, loss_ref,
):
    group = lax.axis_index("dp") * lax.axis_size("row") + lax.axis_index("row")
    count = jnp.sum(len_table[...].astype(F32))
    slot = iota((1, CONT), 1)
    live = [(iota((1, PROMPT), 1) < lens_ref[group, 0]).astype(F32)]
    live += [(slot < lens_ref[group, 1 + n]).astype(F32) for n in range(NCONT)]
    weight = jnp.concatenate(live, axis=1) * (lens_ref.shape[0] * GROUP / count)
    for frm, to, width in order_pieces(parts):
        cols = slice(to, to + width)
        xout_ref[:, cols] = xbo[0, :, frm : frm + width]
        branch = xbo[1, :, frm : frm + width].astype(F32)
        y_here = y_ref[:, cols].astype(F32)
        yout_ref[:, cols] = (y_here + branch).astype(BF16)
        gy_ref[:, cols] = (y_here - ty_ref[:, cols].astype(F32) + branch) * weight[:, cols]
    gx_ref[:, :PROMPT] = gp_ref[...]
    cont = gco.shape[2]
    for p in range(parts):
        gx_ref[:, PROMPT + p * cont : PROMPT + (p + 1) * cont] = gco[p].astype(F32)
    ff = gu_ref.shape[1]
    for i in range(3):
        gq_ref[:, i, :] = out1[:, i * BLOCK : (i + 1) * BLOCK]
    go_ref[...] = out1[:, 3 * BLOCK :].T
    gu_ref[...] = out2[:, :ff]
    gd_ref[...] = out2[:, ff:].T
    for i, ref in enumerate((ga_ref, gb_ref, gc_ref, gd2_ref)):
        ref[...] = sums[i : i + 1].reshape(ref.shape)
    loss_ref[...] = sums[4:5, :1] / (2.0 * count * full)


def run_step(lengths, x, y, tx, ty, wq, wo, wu, wd, vecs):
    feat, tokens = x.shape
    full = 4 * feat
    ff = wu.shape[1]
    width = 4 * BLOCK + 2 * ff
    rest = 2 * ff
    half = feat // 2
    own, cont = tokens // 4, NCONT * CONT // 4
    keys = PROMPT + cont
    heads = full // HD
    vmem = pl.BlockSpec(memory_space=pltpu.VMEM)
    dma = pltpu.SemaphoreType.DMA

    def bf(*shape):
        return pltpu.VMEM(shape, BF16)

    def f32(*shape):
        return pltpu.VMEM(shape, F32)

    def reduce_buffers(cols):
        return [
            bf(4, 4, half, cols), bf(2, 4, half, cols), bf(4, half, cols), bf(3, half, cols),
            bf(4, half, cols),
        ]

    gather_sems = [
        dma((5,)), dma((4,)), dma((4,)), dma((4,)), dma((2, 4)), dma((2, 4)), dma((4, 4)), dma((4, 4)),
    ]
    scatter_sems = [
        dma((4,)), dma((4,)), dma((2,)), dma((2,)), dma(()), dma(()), dma((3,)), dma((4,)),
        dma(()), dma(()),
    ]
    sums = (4, 8, feat)
    smem, anywhere = pl.BlockSpec(memory_space=pltpu.SMEM), pl.BlockSpec(memory_space=pl.ANY)

    def shape(*dims, dtype=F32):
        return jax.ShapeDtypeStruct(dims, dtype)

    raw = pl.pallas_call(
        functools.partial(step_kernel, 4),
        out_shape=(
            shape(2, feat, tokens, dtype=BF16), shape(4, feat, cont, dtype=BF16), shape(feat, PROMPT),
            shape(feat, 4 * BLOCK), shape(feat, rest), shape(8, feat),
        ),
        in_specs=[smem, vmem] + [anywhere] * 4 + [vmem] * 8,
        out_specs=[anywhere] * 2 + [vmem] * 4,
        scratch_shapes=[
            bf(feat, tokens), bf(feat, tokens), bf(feat, tokens),
            bf(4, full, width), bf(4, 4, 2, half, width), bf(full, PROMPT), bf(full, cont), bf(full, own),
            bf(keys, full), bf(keys, 4 * PAIR), bf(4, PAIR, keys), bf(full, own), bf(full, own),
            f32(heads, own), f32(heads, own), bf(full, own), f32(2, PROMPT, PAIR), bf(2, PROMPT, PAIR),
            bf(2, PROMPT, own), bf(2, PROMPT, own), f32(full, own), bf(4, own, ff), f32(full, own),
            f32(full, own), f32(full, keys), bf(2, feat, tokens), bf(2, full, own),
            bf(2, full, own), f32(4, 8, feat), bf(3, feat, PROMPT),
            bf(5, feat, PROMPT), bf(4, feat, cont),
            f32(*sums), f32(6, *sums), f32(*sums),
        ]
        + reduce_buffers(4 * BLOCK)
        + reduce_buffers(rest)
        + [
            dma((5,)), dma((4,)), dma((4,)), dma((4,)), dma((4,)), dma((4,)), dma((4,)), dma((4,)),
            dma((4,)), dma((4,)), dma((3,)), dma((5,)), dma((3,)), dma((5,)), dma((3,)), dma((3,)),
            dma((4,)), dma((4,)), dma((7,)),
        ]
        + gather_sems * 2
        + scatter_sems * 2,
        compiler_params=pltpu.CompilerParams(
            collective_id=2, has_side_effects=True, vmem_limit_bytes=61 << 20
        ),
        name="layer_step",
    )(lengths, lengths, x, y, tx, ty, wq, wo, wu, wd, *vecs)
    return pl.pallas_call(
        functools.partial(finish_kernel, 4, full),
        out_shape=(
            shape(feat, tokens, dtype=BF16), shape(feat, tokens, dtype=BF16), shape(feat, tokens),
            shape(feat, tokens), shape(*wq.shape), shape(*wo.shape), shape(*wu.shape),
            shape(*wd.shape), shape(feat), shape(feat), shape(feat), shape(feat), shape(1, 1),
        ),
        in_specs=[smem] + [vmem] * 9,
        out_specs=[vmem] * 13,
        compiler_params=pltpu.CompilerParams(vmem_limit_bytes=61 << 20),
        name="layer_results",
    )(lengths, lengths, y, ty, *raw)


def body(
    x_stream, y_stream, w_qkv, w_out, gain_attn, bias_attn, w_up, w_down, gain_ffn, bias_ffn,
    teach_x, teach_y, lengths,
):
    ncol, nrow = lax.axis_size("col"), lax.axis_size("row")
    feat, tokens = x_stream.shape
    full = feat * ncol
    groups_here = tokens // GROUP
    parts = ncol // groups_here
    assert parts * 2 * BLOCK == PROMPT and nrow == 4
    block = w_qkv.shape[2]
    ff_block = w_up.shape[1]

    if ncol == parts:
        (
            x_out, y_out, grad_x, grad_y, g_q, g_o, g_u, g_d, g_ga, g_ba, g_gf, g_bf, loss,
        ) = run_step(
            lengths, x_stream, y_stream, teach_x, teach_y, w_qkv, w_out, w_up, w_down,
            (gain_attn, bias_attn, gain_ffn, bias_ffn),
        )
        return (
            x_out, y_out, grad_x, grad_y, g_q, g_o, g_ga, g_ba, g_u, g_d, g_gf, g_bf,
            loss.reshape(()),
        )

    y_f32 = y_stream.astype(F32)
    dy = y_f32 - teach_y.astype(F32)
    teach_dy = to_parts(jnp.stack([teach_x, dy.astype(BF16)]), parts)
    packed = jnp.concatenate([w_qkv.reshape(feat, 3 * block), w_out.T, w_up, w_down.T], axis=1)
    small_vecs = jnp.stack([gain_attn, bias_attn, gain_ffn, bias_ffn])
    vecs = lax.all_gather(small_vecs, "col", axis=1, tiled=True)

    x_prompt, x_cont, tdo, weights = gather_all(x_stream, teach_dy, packed, ncol, nrow, parts)

    first = (lax.axis_index("dp") * nrow + lax.axis_index("row")) * groups_here
    count_all = jnp.sum(lengths).astype(F32)
    total_tokens = lengths.shape[0] * GROUP
    vec = jnp.pad(vecs.T, ((0, 0), (0, 124)))
    xb, gp, gc, gw, small = run_layer(lengths, x_prompt, x_cont, tdo, weights, vec, parts)
    lanes = max(feat, 128)
    small = small[0].reshape(8, ncol, feat).transpose(1, 0, 2)
    small = jnp.pad(small, ((0, 0), (0, 0), (0, lanes - feat)))
    xb, gp, gc, gw, sums = scatter_all(xb, gp, gc, gw, small, ncol, parts)

    xb = from_parts(xb, parts)
    branch = xb[1].astype(F32)
    live_all = live_slots(
        lax.dynamic_slice_in_dim(lengths, first, groups_here, 0)
    ).reshape(1, tokens)
    y_out = (y_f32 + branch).astype(BF16)
    grad_y_out = (dy + branch) * (live_all * (total_tokens / count_all))
    gp = jnp.sum(gp.astype(F32), axis=0).reshape(feat, groups_here, PROMPT)
    gc = gc.astype(F32).reshape(feat, groups_here, NCONT * CONT)
    grad_x = jnp.concatenate([gp, gc], axis=2).reshape(feat, tokens)
    loss = sums[4, 0] / (2.0 * count_all * full)
    first_up = 4 * block
    return (
        xb[0],
        y_out,
        grad_x,
        grad_y_out,
        gw[:, : 3 * block].reshape(feat, 3, block),
        gw[:, 3 * block : 4 * block].T,
        sums[0, :feat],
        sums[1, :feat],
        gw[:, first_up : first_up + ff_block],
        gw[:, first_up + ff_block :].T,
        sums[2, :feat],
        sums[3, :feat],
        loss,
    )


def live_slots(lens):
    prompt = jnp.arange(PROMPT, dtype=jnp.int32)[None, :] < lens[:, 0:1]
    cont = jnp.arange(CONT, dtype=jnp.int32)[None, None, :] < lens[:, 1:, None]
    cont = cont.reshape(lens.shape[0], NCONT * CONT)
    return jnp.concatenate([prompt, cont], axis=1).astype(F32)


def solution(mesh):
    stream = P("col", ("dp", "row"))
    up, down = P("col", "row"), P("row", "col")
    qkv, vec = P("col", None, "row"), P("col")
    return jax.shard_map(
        body,
        mesh=mesh,
        in_specs=(
            stream, stream, qkv, down, vec, vec, up, down, vec, vec, stream, stream, P(),
        ),
        out_specs=(
            stream, stream, stream, stream, qkv, down, vec, vec, up, down, vec, vec, P(),
        ),
        check_vma=False,
    )
```

```python
import functools

import jax
import jax.numpy as jnp
from jax import lax
from jax.experimental import pallas as pl
from jax.experimental.pallas import tpu as pltpu
from jax.sharding import PartitionSpec as P

HD = 64
PROMPT = 1024
CONT = 128
NCONT = 8
GROUP = 2048
BLOCK = 128

EPS_NORM = 1e-05
NEG_FILL = -1000000000.0
MESH = pl.DeviceIdType.MESH
F32 = jnp.float32
BF16 = jnp.bfloat16


def flip_low(r):
    return r + 1 - 2 * (r % 2)


def flip_high(r):
    return (r + 2) % 4


class Places:
    def __init__(self, ncol):
        self.dp = lax.axis_index("dp")
        self.row = lax.axis_index("row")
        self.col = lax.axis_index("col")
        self.ncol = ncol
        low, high = flip_low(self.row), flip_high(self.row)
        self.first = low * (1 - self.dp) + high * self.dp
        self.second = high * (1 - self.dp) + low * self.dp
        self.both = 3 - self.row
        self.sibling = (1 - self.dp, self.row, self.col)
        self.first_dev = (self.dp, self.first, self.col)
        self.second_dev = (self.dp, self.second, self.col)
        self.aheads = [(self.col + k) % ncol for k in range(ncol)]
        self.behinds = [(self.col + ncol - k) % ncol for k in range(ncol)]

    def ahead(self, k):
        return self.aheads[k]

    def behind(self, k):
        return self.behinds[k]

    def col_dev(self, c):
        return (self.dp, self.row, c)

    def meet(self):
        barrier = pltpu.get_barrier_semaphore()
        partners = [self.sibling, self.first_dev, self.second_dev]
        partners += [self.col_dev(self.ahead(k)) for k in range(1, self.ncol)]
        for partner in partners:
            pl.semaphore_signal(barrier, inc=1, device_id=partner, device_id_type=MESH)
        pl.semaphore_wait(barrier, len(partners))


def remote(src, dst, send_sem, recv_sem, device):
    return pltpu.make_async_remote_copy(
        src_ref=src,
        dst_ref=dst,
        send_sem=send_sem,
        recv_sem=recv_sem,
        device_id=device,
        device_id_type=MESH,
    )


def gather_kernel(
    ncol, parts, x_ref, td_ref, w_ref, xp_ref, xc_ref, tdo_ref, g_ref,
    act_send, act_recv, col_send, col_recv, one_send, one_recv, two_send, two_recv,
    sib_send, sib_recv, local_sem,
):
    at = Places(ncol)
    feat = x_ref.shape[0]
    half = feat // 2
    own_tokens = tdo_ref.shape[2]
    own_cont = xc_ref.shape[1]

    def rows_of(c):
        return pl.ds(pl.multiple_of(c * feat, feat), feat)

    def half_rows(c, core):
        return pl.ds(pl.multiple_of(c * feat + core * half, half), half)

    def prompt_cols(c):
        return pl.ds(pl.multiple_of(c // parts * GROUP, GROUP), PROMPT)

    def cont_cols(c):
        return pl.ds(
            pl.multiple_of(c // parts * GROUP + PROMPT + c % parts * own_cont, own_cont), own_cont
        )

    def own_cols(c):
        return pl.ds(pl.multiple_of(c * own_tokens, own_tokens), own_tokens)

    at.meet()
    my_half = w_ref.at[pl.ds(pl.multiple_of(at.dp * half, half), half)]
    pending = []

    def start(copy):
        copy.start()
        pending.append(copy)
        return copy

    mine = rows_of(at.col)
    for i, (src, dst) in enumerate(
        (
            (x_ref.at[:, prompt_cols(at.col)], xp_ref.at[mine]),
            (x_ref.at[:, cont_cols(at.col)], xc_ref.at[mine]),
            (td_ref.at[:, :, own_cols(at.col)], tdo_ref.at[:, mine]),
            (w_ref, g_ref.at[at.row, mine]),
        )
    ):
        pltpu.make_async_copy(src, dst, local_sem.at[i]).start()

    for k in range(1, ncol):
        start(
            remote(
                my_half,
                g_ref.at[at.row, half_rows(at.col, at.dp)],
                col_send.at[k],
                col_recv.at[k],
                at.col_dev(at.ahead(k)),
            )
        )
    for k in range(1, ncol):
        to = at.ahead(k)
        dev = at.col_dev(to)
        start(
            remote(
                x_ref.at[:, prompt_cols(to)], xp_ref.at[mine],
                act_send.at[0, k], act_recv.at[0, k], dev,
            )
        )
        start(
            remote(
                x_ref.at[:, cont_cols(to)], xc_ref.at[mine],
                act_send.at[1, k], act_recv.at[1, k], dev,
            )
        )
    for k in range(1, ncol):
        to = at.ahead(k)
        start(
            remote(
                td_ref.at[:, :, own_cols(to)], tdo_ref.at[:, mine],
                act_send.at[2, k], act_recv.at[2, k], at.col_dev(to),
            )
        )

    def piece(row, k, core):
        return g_ref.at[row, half_rows(at.behind(k), core)]

    def landed(dst, recv_sem):
        remote(dst, dst, recv_sem, recv_sem, at.sibling).wait_recv()

    def chunk(k):
        return my_half if k == 0 else piece(at.row, k, at.dp)

    for k in range(ncol):
        if k:
            landed(piece(at.row, k, at.dp), col_recv.at[k])
        start(remote(chunk(k), piece(at.row, k, at.dp), one_send.at[k], one_recv.at[k], at.first_dev))
        start(
            remote(chunk(k), piece(at.row, k, at.dp), two_send.at[0, k], two_recv.at[0, k], at.second_dev)
        )
        if k:
            start(
                remote(chunk(k), piece(at.row, k, at.dp), sib_send.at[0, k], sib_recv.at[0, k], at.sibling)
            )
    for k in range(ncol):
        got = piece(at.first, k, at.dp)
        landed(got, one_recv.at[k])
        start(remote(got, got, two_send.at[1, k], two_recv.at[1, k], at.second_dev))
        start(remote(got, got, sib_send.at[1, k], sib_recv.at[1, k], at.sibling))
    for k in range(ncol):
        for i, row in ((0, at.second), (1, at.both)):
            got = piece(row, k, at.dp)
            landed(got, two_recv.at[i, k])
            start(remote(got, got, sib_send.at[2 + i, k], sib_recv.at[2 + i, k], at.sibling))

    for k in range(1, ncol):
        frm = rows_of(at.behind(k))
        landed(xp_ref.at[frm], act_recv.at[0, k])
        landed(xc_ref.at[frm], act_recv.at[1, k])
        landed(tdo_ref.at[:, frm], act_recv.at[2, k])
    other = 1 - at.dp
    for k in range(ncol):
        if k:
            landed(piece(at.row, k, other), sib_recv.at[0, k])
        landed(piece(at.second, k, other), sib_recv.at[1, k])
        landed(piece(at.first, k, other), sib_recv.at[2, k])
        landed(piece(at.both, k, other), sib_recv.at[3, k])
    for copy in pending:
        copy.wait_send()
    for i, (src, dst) in enumerate(
        (
            (x_ref.at[:, prompt_cols(at.col)], xp_ref.at[mine]),
            (x_ref.at[:, cont_cols(at.col)], xc_ref.at[mine]),
            (td_ref.at[:, :, own_cols(at.col)], tdo_ref.at[:, mine]),
            (w_ref, g_ref.at[at.row, mine]),
        )
    ):
        pltpu.make_async_copy(src, dst, local_sem.at[i]).wait()


def gather_all(x_stream, teach_dy, packed, ncol, nrow, parts):
    feat = x_stream.shape[0]
    full = feat * ncol
    own_tokens = GROUP // parts
    own_cont = NCONT * CONT // parts
    dma = pltpu.SemaphoreType.DMA
    anywhere = pl.BlockSpec(memory_space=pl.ANY)
    return pl.pallas_call(
        functools.partial(gather_kernel, ncol, parts),
        out_shape=(
            jax.ShapeDtypeStruct((full, PROMPT), BF16),
            jax.ShapeDtypeStruct((full, own_cont), BF16),
            jax.ShapeDtypeStruct((2, full, own_tokens), BF16),
            jax.ShapeDtypeStruct((nrow, full, packed.shape[1]), BF16),
        ),
        in_specs=[anywhere] * 3,
        out_specs=[anywhere] * 4,
        scratch_shapes=[
            dma((3, ncol)), dma((3, ncol)), dma((ncol,)), dma((ncol,)), dma((ncol,)), dma((ncol,)),
            dma((2, ncol)), dma((2, ncol)), dma((4, ncol)), dma((4, ncol)), dma((4,)),
        ],
        compiler_params=pltpu.CompilerParams(collective_id=0, has_side_effects=True),
        name="gather_all",
    )(x_stream, teach_dy, packed)


def scatter_kernel(
    ncol, parts, xb_ref, gp_ref, gc_ref, gw_ref, sm_ref,
    xbo_ref, gpo_ref, gco_ref, gwo_ref, smo_ref,
    sib_buf, two_buf, one_buf, col_buf, sm_buf, smc_buf,
    act_send, act_recv, sib_send, sib_recv, two_send, two_recv, one_send, one_recv,
    col_send, col_recv, fin_send, fin_recv, sm_send, sm_recv, smc_send, smc_recv, local_sem,
):
    at = Places(ncol)
    feat = xbo_ref.shape[1]
    half = feat // 2
    own_tokens = xb_ref.shape[2]
    own_cont = gc_ref.shape[1]
    part = at.col % parts

    def rows_of(c):
        return pl.ds(pl.multiple_of(c * feat, feat), feat)

    def half_rows(c, core):
        return pl.ds(pl.multiple_of(c * feat + core * half, half), half)

    def prompt_cols(c):
        return pl.ds(pl.multiple_of(c // parts * PROMPT, PROMPT), PROMPT)

    def cont_cols(c):
        return pl.ds(pl.multiple_of(c * own_cont, own_cont), own_cont)

    def own_cols(c):
        return pl.ds(pl.multiple_of(c * own_tokens, own_tokens), own_tokens)

    at.meet()
    pending = []

    def start(copy):
        copy.start()
        pending.append(copy)
        return copy

    def landed(dst, recv_sem):
        remote(dst, dst, recv_sem, recv_sem, at.sibling).wait_recv()

    other = 1 - at.dp
    order = list(range(1, ncol)) + [0]
    for k in order:
        start(
            remote(
                gw_ref.at[:, half_rows(at.ahead(k), other)], sib_buf.at[k],
                sib_send.at[k], sib_recv.at[k], at.sibling,
            )
        )
    start(remote(sm_ref, sm_buf.at[0], sm_send.at[0], sm_recv.at[0], at.sibling))

    def local_copies():
        mine = rows_of(at.col)
        return [
            pltpu.make_async_copy(src, dst, local_sem.at[i])
            for i, (src, dst) in enumerate(
                (
                    (xb_ref.at[:, mine], xbo_ref.at[:, :, own_cols(at.col)]),
                    (gp_ref.at[mine], gpo_ref.at[part, :, prompt_cols(at.col)]),
                    (gc_ref.at[mine], gco_ref.at[:, cont_cols(at.col)]),
                )
            )
        ]

    for copy in local_copies():
        copy.start()
    for k in range(1, ncol):
        to = at.ahead(k)
        dev = at.col_dev(to)
        start(
            remote(
                xb_ref.at[:, rows_of(to)], xbo_ref.at[:, :, own_cols(at.col)],
                act_send.at[0, k], act_recv.at[0, k], dev,
            )
        )
        start(
            remote(
                gp_ref.at[rows_of(to)], gpo_ref.at[part, :, prompt_cols(at.col)],
                act_send.at[1, k], act_recv.at[1, k], dev,
            )
        )
        start(
            remote(
                gc_ref.at[rows_of(to)], gco_ref.at[:, cont_cols(at.col)],
                act_send.at[2, k], act_recv.at[2, k], dev,
            )
        )

    for k in order:
        landed(sib_buf.at[k], sib_recv.at[k])
        for row in range(gw_ref.shape[0]):
            here = gw_ref.at[row, half_rows(at.ahead(k), at.dp)]
            sib_buf[k, row] = (here[...].astype(F32) + sib_buf[k, row].astype(F32)).astype(BF16)
        for i, row in ((0, at.second), (1, at.both)):
            start(
                remote(
                    sib_buf.at[k, row], two_buf.at[i, k],
                    two_send.at[i, k], two_recv.at[i, k], at.second_dev,
                )
            )
    landed(sm_buf.at[0], sm_recv.at[0])
    sm_buf[3] = sm_ref[...] + sm_buf[0]
    start(remote(sm_buf.at[3], sm_buf.at[1], sm_send.at[1], sm_recv.at[1], at.second_dev))
    for k in order:
        landed(two_buf.at[1, k], two_recv.at[1, k])
        two_buf[1, k] = (sib_buf[k, at.first].astype(F32) + two_buf[1, k].astype(F32)).astype(BF16)
        start(
            remote(
                two_buf.at[1, k], one_buf.at[k], one_send.at[k], one_recv.at[k], at.first_dev
            )
        )
    landed(sm_buf.at[1], sm_recv.at[1])
    sm_buf[4] = sm_buf[3] + sm_buf[1]
    start(remote(sm_buf.at[4], sm_buf.at[2], sm_send.at[2], sm_recv.at[2], at.first_dev))
    for k in order:
        landed(two_buf.at[0, k], two_recv.at[0, k])
        landed(one_buf.at[k], one_recv.at[k])
        total = sib_buf[k, at.row].astype(F32) + two_buf[0, k].astype(F32) + one_buf[k].astype(F32)
        if k:
            two_buf[0, k] = total.astype(BF16)
            start(
                remote(
                    two_buf.at[0, k], col_buf.at[k],
                    col_send.at[k], col_recv.at[k], at.col_dev(at.ahead(k)),
                )
            )
        else:
            own_total = total
    landed(sm_buf.at[2], sm_recv.at[2])
    sm_buf[5] = sm_buf[4] + sm_buf[2]
    for k in range(1, ncol):
        to = at.ahead(k)
        start(
            remote(
                sm_buf.at[5, to], smc_buf.at[k], smc_send.at[k], smc_recv.at[k], at.col_dev(to)
            )
        )
    for k in range(1, ncol):
        landed(col_buf.at[k], col_recv.at[k])
        own_total = own_total + col_buf[k].astype(F32)
    my_rows = pl.ds(pl.multiple_of(at.dp * half, half), half)
    gwo_ref[my_rows] = own_total
    start(remote(gwo_ref.at[my_rows], gwo_ref.at[my_rows], fin_send, fin_recv, at.sibling))
    small = sm_buf[5, at.col]
    for k in range(1, ncol):
        landed(smc_buf.at[k], smc_recv.at[k])
        small = small + smc_buf[k]
    smo_ref[...] = small
    landed(gwo_ref.at[pl.ds(pl.multiple_of(other * half, half), half)], fin_recv)
    for k in range(1, ncol):
        frm = at.behind(k)
        landed(xbo_ref.at[:, :, own_cols(frm)], act_recv.at[0, k])
        landed(gpo_ref.at[frm % parts, :, prompt_cols(frm)], act_recv.at[1, k])
        landed(gco_ref.at[:, cont_cols(frm)], act_recv.at[2, k])
    for copy in pending:
        copy.wait_send()
    for copy in local_copies():
        copy.wait()


def scatter_all(xb, gp, gc, gw, small, ncol, parts):
    nrow, full, width = gw.shape
    feat = full // ncol
    half = feat // 2
    groups = ncol // parts
    own_tokens, own_cont = xb.shape[2], gc.shape[1]
    dma = pltpu.SemaphoreType.DMA
    anywhere = pl.BlockSpec(memory_space=pl.ANY)
    vmem = pl.BlockSpec(memory_space=pltpu.VMEM)
    small_shape = small.shape
    return pl.pallas_call(
        functools.partial(scatter_kernel, ncol, parts),
        out_shape=(
            jax.ShapeDtypeStruct((2, feat, ncol * own_tokens), BF16),
            jax.ShapeDtypeStruct((parts, feat, groups * PROMPT), BF16),
            jax.ShapeDtypeStruct((feat, ncol * own_cont), BF16),
            jax.ShapeDtypeStruct((feat, width), F32),
            jax.ShapeDtypeStruct(small_shape[1:], F32),
        ),
        in_specs=[anywhere, anywhere, anywhere, vmem, vmem],
        out_specs=[anywhere, anywhere, anywhere, vmem, vmem],
        scratch_shapes=[
            pltpu.VMEM((ncol, nrow, half, width), BF16),
            pltpu.VMEM((2, ncol, half, width), BF16),
            pltpu.VMEM((ncol, half, width), BF16),
            pltpu.VMEM((ncol, half, width), BF16),
            pltpu.VMEM((6,) + small_shape, F32),
            pltpu.VMEM((ncol,) + small_shape[1:], F32),
            dma((3, ncol)), dma((3, ncol)), dma((ncol,)), dma((ncol,)), dma((2, ncol)), dma((2, ncol)),
            dma((ncol,)), dma((ncol,)), dma((ncol,)), dma((ncol,)), dma(()), dma(()),
            dma((3,)), dma((3,)), dma((ncol,)), dma((ncol,)), dma((3,)),
        ],
        compiler_params=pltpu.CompilerParams(
            collective_id=1, has_side_effects=True, vmem_limit_bytes=56 << 20
        ),
        name="scatter_all",
    )(xb, gp, gc, gw, small)


def to_parts(array_in, parts):
    lead = array_in.shape[:-1]
    groups = array_in.shape[-1] // GROUP
    split = array_in.reshape(lead + (groups, GROUP))
    prompt = split[..., :PROMPT].reshape(lead + (groups, 2, parts, BLOCK))
    prompt = jnp.stack([prompt[..., 0, :, :], prompt[..., 1, ::-1, :]], axis=-2)
    prompt = prompt.reshape(lead + (groups, parts, PROMPT // parts))
    cont = split[..., PROMPT:].reshape(lead + (groups, parts, NCONT * CONT // parts))
    return jnp.concatenate([prompt, cont], axis=-1).reshape(array_in.shape)


def from_parts(array_in, parts):
    lead = array_in.shape[:-1]
    groups = array_in.shape[-1] // GROUP
    split = array_in.reshape(lead + (groups, parts, GROUP // parts))
    prompt = split[..., : PROMPT // parts].reshape(lead + (groups, parts, 2, BLOCK))
    prompt = jnp.concatenate(
        [prompt[..., :, 0, :], prompt[..., ::-1, 1, :]], axis=-2
    ).reshape(lead + (groups, PROMPT))
    cont = split[..., PROMPT // parts :].reshape(lead + (groups, NCONT * CONT))
    return jnp.concatenate([prompt, cont], axis=-1).reshape(array_in.shape)


def norm_forward(summed, gain_vec, bias_vec):
    average = jnp.mean(summed, axis=0, keepdims=True)
    squares = jnp.mean(summed * summed, axis=0, keepdims=True)
    inv_scale = lax.rsqrt(squares - average * average + EPS_NORM)
    unit_val = (summed - average) * inv_scale
    return (unit_val * gain_vec + bias_vec, unit_val, inv_scale)


def norm_backward(upstream, unit_val, inv_scale, gain_vec):
    scaled = upstream * gain_vec
    first = jnp.mean(scaled, axis=0, keepdims=True)
    second = jnp.mean(scaled * unit_val, axis=0, keepdims=True)
    d_summed = inv_scale * (scaled - first - unit_val * second)
    sums = [jnp.sum(v, axis=1, keepdims=True) for v in (upstream * unit_val, upstream)]
    return (d_summed, *sums)


def dot_tn(lhs, rhs):
    return lax.dot_general(lhs, rhs, (((0,), (0,)), ((), ())), preferred_element_type=F32)


def dot_nn(lhs, rhs):
    return lax.dot_general(lhs, rhs, (((1,), (0,)), ((), ())), preferred_element_type=F32)


def dot_nt(lhs, rhs):
    return lax.dot_general(lhs, rhs, (((1,), (1,)), ((), ())), preferred_element_type=F32)


def iota(shape, axis):
    return lax.broadcasted_iota(jnp.int32, shape, axis)


def fold(array_in, op):
    return op(array_in.reshape(array_in.shape[0] // 8, 8, array_in.shape[1]), axis=0)


KEYS = 256
PAIR = 2 * BLOCK


def put(ref, r, cols, value):
    lead = ref.shape[1:-1]
    index = (r,) + (slice(None),) * len(lead) + (cols,)
    ref[index] = value.astype(BF16).reshape(lead + (value.shape[1],))


class Layer:
    def __init__(self, part, parts, lens, total_tokens, count, order=lambda n: n):
        self.part, self.parts = part, parts
        self.order = order
        self.lens = lens
        self.total_tokens, self.count = total_tokens, count
        slot = iota((1, BLOCK), 1)
        low, high = part * BLOCK + slot, (2 * parts - 1 - part) * BLOCK + slot
        last = lens[0] - 1
        self.bound = jnp.concatenate(
            [jnp.minimum(low, last), jnp.minimum(high, last), jnp.full((1, PAIR), last, jnp.int32)],
            axis=1,
        )
        live = [low < lens[0], high < lens[0]] + [slot < n for n in lens[1:]]
        self.live = jnp.concatenate([m.astype(F32) for m in live], axis=1)

    def own_columns(self):
        low = pl.ds(pl.multiple_of(self.part * BLOCK, BLOCK), BLOCK)
        high = pl.ds(pl.multiple_of((2 * self.parts - 1 - self.part) * BLOCK, BLOCK), BLOCK)
        return low, high

    def project(self, xp, xc, w, xo, xt, kv, kvt, qt):
        low, high = self.own_columns()
        xo[:, :BLOCK] = xp[:, low]
        xo[:, BLOCK:PAIR] = xp[:, high]
        xo[:, PAIR:] = xc[...]
        xt[:PROMPT] = xp[...].T
        xt[PROMPT:] = xc[...].T

        def step(r, carry):
            wq, wkv = w[r, :, :BLOCK], w[r, :, BLOCK : 3 * BLOCK]
            cols = pl.ds(pl.multiple_of(r * PAIR, PAIR), PAIR)
            kv[:, cols] = dot_nn(xt[...], wkv).astype(BF16)
            kvt[r, :, :PROMPT] = dot_tn(wkv, xp[...]).astype(BF16)
            kvt[r, :, PROMPT:] = dot_tn(wkv, xc[...]).astype(BF16)
            rows = pl.ds(pl.multiple_of(r * BLOCK, BLOCK), BLOCK)
            qt[rows] = (dot_tn(wq, xo[...]).astype(BF16).astype(F32) * HD ** (-0.5)).astype(BF16)
            return carry

        lax.fori_loop(0, w.shape[0], step, 0)

    def one_head(self, array_in, head):
        zeros = jnp.zeros((HD, array_in.shape[1]), array_in.dtype)
        mine = array_in[head * HD : (head + 1) * HD]
        return jnp.concatenate([mine, zeros] if head == 0 else [zeros, mine], axis=0)

    def masked(self, score, first_key, columns):
        keys = iota(score.shape, 0) + first_key
        return jnp.where(keys <= self.bound[:, columns], score, NEG_FILL)

    def masked_own(self, score, n):
        keys = iota(score.shape, 0)
        return jnp.where(
            (keys <= iota(score.shape, 1)) & (keys < self.lens[1 + n]), score, NEG_FILL
        )

    def attend(self, kv, kvt, qt, att, lse, s_scr, p_scr, between=None):
        def step(r, carry):
            k_cols = pl.ds(pl.multiple_of(r * PAIR, PAIR), BLOCK)
            q_pair = qt[pl.ds(pl.multiple_of(r * BLOCK, BLOCK), BLOCK)]
            for head in range(2):
                query = self.one_head(q_pair, head)
                v_rows = slice(BLOCK + head * HD, BLOCK + (head + 1) * HD)
                for b in range(2):
                    columns = slice(b * PAIR, (b + 1) * PAIR)
                    q_here = query[:, columns]
                    top = jnp.full((8, PAIR), NEG_FILL, F32)
                    for first in range(0, PROMPT, KEYS):
                        score = dot_nn(kv[first : first + KEYS, k_cols], q_here)
                        score = self.masked(score, first, columns)
                        s_scr[head, first : first + KEYS] = score
                        top = jnp.maximum(top, fold(score, jnp.max))
                    own_scores = []
                    if b == 1:
                        for n in range(2):
                            keys = slice(PROMPT + n * BLOCK, PROMPT + (n + 1) * BLOCK)
                            score = dot_nn(kv[keys, k_cols], q_here[:, n * BLOCK : (n + 1) * BLOCK])
                            own_scores.append(self.masked_own(score, n))
                        own_top = [fold(score, jnp.max) for score in own_scores]
                        top = jnp.maximum(top, jnp.concatenate(own_top, axis=1))
                    top = jnp.max(top, axis=0, keepdims=True)
                    total = jnp.zeros((8, PAIR), F32)
                    for first in range(0, PROMPT, KEYS):
                        prob = jnp.exp(s_scr[head, first : first + KEYS] - top)
                        total = total + fold(prob, jnp.sum)
                        p_scr[head, first : first + KEYS] = prob.astype(BF16)
                    out = dot_nn(kvt[r, v_rows, :PROMPT], p_scr[head])
                    if b == 1:
                        own_out, own_total = [], []
                        for n in range(2):
                            lanes = slice(n * BLOCK, (n + 1) * BLOCK)
                            prob = jnp.exp(own_scores[n] - top[:, lanes])
                            own_total.append(fold(prob, jnp.sum))
                            keys = slice(PROMPT + n * BLOCK, PROMPT + (n + 1) * BLOCK)
                            own_out.append(dot_nn(kvt[r, v_rows, keys], prob.astype(BF16)))
                        total = total + jnp.concatenate(own_total, axis=1)
                        out = out + jnp.concatenate(own_out, axis=1)
                    total = jnp.sum(total, axis=0, keepdims=True)
                    rows = pl.ds(pl.multiple_of(r * BLOCK + head * HD, HD), HD)
                    att[rows, columns] = (out / total).astype(BF16)
                    lse[pl.ds(2 * r + head, 1), columns] = top + jnp.log(total)
            if between is not None:
                between(r)
            return carry

        lax.fori_loop(0, kvt.shape[0], step, 0)

    def attend_back(
        self, kv, kvt, qt, lse, delta, d_att, dkvt, dqt, p_scr, ds_scr, between=None, grads=None,
        inputs=None,
    ):
        def step(n, carry):
            r = self.order(n)
            k_cols = pl.ds(pl.multiple_of(r * PAIR, PAIR), BLOCK)
            v_cols = pl.ds(pl.multiple_of(r * PAIR + BLOCK, BLOCK), BLOCK)
            pair = pl.ds(pl.multiple_of(r * BLOCK, BLOCK), BLOCK)
            q_pair, d_pair = qt[pair], d_att[pair]
            for head in range(2):
                query, d_out = self.one_head(q_pair, head), self.one_head(d_pair, head)
                q_mine = q_pair[head * HD : (head + 1) * HD]
                d_mine = d_pair[head * HD : (head + 1) * HD]
                k_rows = slice(head * HD, (head + 1) * HD)
                v_rows = slice(BLOCK + head * HD, BLOCK + (head + 1) * HD)
                norm = lse[pl.ds(2 * r + head, 1)]
                dlt = delta[pl.ds(2 * r + head, 1)]
                for b in range(2):
                    columns = slice(b * PAIR, (b + 1) * PAIR)
                    for first in range(0, PROMPT, KEYS):
                        keys = slice(first, first + KEYS)
                        score = dot_nn(kv[keys, k_cols], query[:, columns])
                        score = self.masked(score, first, columns)
                        prob = jnp.exp(score - norm[:, columns])
                        dprob = dot_nn(kv[keys, v_cols], d_out[:, columns])
                        p_scr[head, keys, columns] = prob.astype(BF16)
                        ds_scr[head, keys, columns] = (prob * (dprob - dlt[:, columns])).astype(BF16)
                d_query = dot_nn(kvt[r, k_rows, :PROMPT], ds_scr[head])
                own_dq = [jnp.zeros((HD, PAIR), F32)]
                for m in range(2):
                    keys = slice(PROMPT + m * BLOCK, PROMPT + (m + 1) * BLOCK)
                    lanes = slice(PAIR + m * BLOCK, PAIR + (m + 1) * BLOCK)
                    score = self.masked_own(dot_nn(kv[keys, k_cols], query[:, lanes]), m)
                    prob = jnp.exp(score - norm[:, lanes])
                    dprob = dot_nn(kv[keys, v_cols], d_out[:, lanes])
                    d_score = (prob * (dprob - dlt[:, lanes])).astype(BF16)
                    own_dq.append(dot_nn(kvt[r, k_rows, keys], d_score))
                    dkvt[r, k_rows, keys] = dot_nt(q_mine[:, lanes], d_score).astype(BF16)
                    dkvt[r, v_rows, keys] = dot_nt(d_mine[:, lanes], prob.astype(BF16)).astype(BF16)
                d_query = (d_query + jnp.concatenate(own_dq, axis=1)) * HD ** (-0.5)
                rows = pl.ds(pl.multiple_of(r * BLOCK + head * HD, HD), HD)
                dqt[rows] = d_query.astype(BF16)
                dkvt[r, k_rows, :PROMPT] = dot_nt(q_mine, ds_scr[head]).astype(BF16)
                dkvt[r, v_rows, :PROMPT] = dot_nt(d_mine, p_scr[head]).astype(BF16)
            if grads is not None:
                self.projection_grads(r, pair, *grads, dkvt, dqt)
            if inputs is not None:
                w, dx, dxo = inputs
                dx[...] += dot_nn(w[r, :, BLOCK : 3 * BLOCK], dkvt[r])
                dxo[...] += dot_nn(w[r, :, :BLOCK], dqt[pair])
            if between is not None:
                between(n)
            return carry

        lax.fori_loop(0, kvt.shape[0], step, 0)

    def projection_grads(self, r, rows, xp, xc, xo, gw, dkvt, dqt):
        put(gw, r, slice(0, BLOCK), dot_nt(xo[...], dqt[rows]))
        both = dot_nt(xp[...], dkvt[r, :, :PROMPT]) + dot_nt(xc[...], dkvt[r, :, PROMPT:])
        put(gw, r, slice(BLOCK, 3 * BLOCK), both)

    def input_grads(self, xp, xc, xo, w, dkvt, dqt, dsa, gp, gc, gw, dx, dxo):
        for r in range(w.shape[0]):
            wq, wkv = w[r, :, :BLOCK], w[r, :, BLOCK : 3 * BLOCK]
            part = dot_nn(wkv, dkvt[r])
            rows = slice(r * BLOCK, (r + 1) * BLOCK)
            own = dot_nn(wq, dqt[rows])
            if r == 0:
                dx[...] = part
                dxo[...] = dsa[...] + own
            else:
                dx[...] += part
                dxo[...] += own
            self.projection_grads(r, rows, xp, xc, xo, gw, dkvt, dqt)
        low, high = self.own_columns()
        dx[:, low] += dxo[:, :BLOCK]
        dx[:, high] += dxo[:, BLOCK:PAIR]
        gp[...] = dx[:, :PROMPT].astype(BF16)
        gc[...] = (dx[:, PROMPT:] + dxo[:, PAIR:]).astype(BF16)

    def middle(
        self, xo, tdo, w, vec, att, xb, gw, sm, d_att, delta, dsa, hid, acc, ba,
        tokens_ready=None, outputs_ready=None, grads_ready=None, back_done=None,
    ):
        nrow, full = w.shape[0], w.shape[1]
        ff = (w.shape[2] - 4 * BLOCK) // 2
        up, down = slice(4 * BLOCK, 4 * BLOCK + ff), slice(4 * BLOCK + ff, 4 * BLOCK + 2 * ff)
        gain_a, bias_a, gain_f, bias_f = (vec[:, i : i + 1].astype(F32) for i in range(4))
        w_o = jnp.concatenate([w[r, :, 3 * BLOCK : 4 * BLOCK] for r in range(nrow)], axis=1)
        ba[...] = dot_nn(w_o, att[...])
        x_one, unit_a, inv_a = norm_forward(xo[...].astype(F32) + ba[...], gain_a, bias_a)
        x_low = x_one.astype(BF16)
        x_low_t = x_low.T
        acc[...] = jnp.zeros_like(acc)

        def up_down(r, carry):
            pre = dot_nn(x_low_t, w[r, :, up])
            hidden = jnp.maximum(pre, 0.0).astype(BF16)
            hid[r] = hidden
            acc[...] += dot_nt(w[r, :, down], hidden)
            return carry

        lax.fori_loop(0, nrow, up_down, 0)
        branch_f = acc[...]
        x_two, unit_f, inv_f = norm_forward(x_one + branch_f, gain_f, bias_f)
        branch = ba[...] + branch_f
        xb[0] = x_two.astype(BF16)
        xb[1] = branch.astype(BF16)
        if outputs_ready is not None:
            outputs_ready()
            tokens_ready()
        diff_x = x_two - tdo[0].astype(F32)
        diff_y = branch + tdo[1].astype(F32)
        loss = jnp.sum(self.live * (diff_x * diff_x + diff_y * diff_y))
        weight = self.live * (self.total_tokens / self.count)
        grad_y = diff_y * weight
        d_sum_f, gain_grad_f, bias_grad_f = norm_backward(diff_x * weight, unit_f, inv_f, gain_f)
        d_branch_f = (d_sum_f + grad_y).astype(BF16)
        d_branch_t = d_branch_f.T
        acc[...] = d_sum_f

        def back(n, carry):
            r = self.order(n)
            hidden = hid[r]
            d_hidden = dot_nn(d_branch_t, w[r, :, down])
            d_pre = jnp.where(hidden.astype(F32) > 0, d_hidden, 0.0).astype(BF16)
            put(gw, r, up, dot_nn(x_low, d_pre))
            put(gw, r, down, dot_nn(d_branch_f, hidden))
            acc[...] += dot_nt(w[r, :, up], d_pre)
            if grads_ready is not None:
                grads_ready(n)
            return carry

        lax.fori_loop(0, nrow, back, 0)
        if back_done is not None:
            back_done()
        d_sum_a, gain_grad_a, bias_grad_a = norm_backward(acc[...], unit_a, inv_a, gain_a)
        dsa[...] = d_sum_a
        d_branch_a = (d_sum_a + grad_y).astype(BF16)
        for r in range(nrow):
            rows = slice(r * BLOCK, (r + 1) * BLOCK)
            attended = att[rows]
            put(gw, r, slice(3 * BLOCK, 4 * BLOCK), dot_nt(d_branch_a, attended))
            d_here = dot_tn(w[r, :, 3 * BLOCK : 4 * BLOCK], d_branch_a).astype(BF16)
            d_att[rows] = d_here
            product = attended.astype(F32) * d_here.astype(F32)
            for head in range(2):
                delta[2 * r + head : 2 * r + head + 1] = jnp.sum(
                    product[head * HD : (head + 1) * HD], axis=0, keepdims=True
                )
        lane = iota((full, 128), 1)
        sums = jnp.zeros((full, 128), F32)
        for i, vector in enumerate((gain_grad_a, bias_grad_a, gain_grad_f, bias_grad_f)):
            sums = jnp.where(lane == i, vector, sums)
        sums = jnp.where(lane == 4, loss, sums)
        sums = sums.T[:8]
        for s in range(sm.shape[0]):
            sm[s] = sums[:, s * sm.shape[2] : (s + 1) * sm.shape[2]]


def layer_kernel(
    parts, lens_ref, len_table, xp, xc, tdo, w, vec, xb, gp, gc, gw, sm,
    xo, xt, kv, kvt, qt, att, lse, delta, d_att, dkvt, dqt, s_scr, pf_scr, p_scr, ds_scr,
    dsa, hid, acc, ba, dx,
):
    col = lax.axis_index("col")
    groups = lax.axis_size("col") // parts
    chip = lax.axis_index("dp") * lax.axis_size("row") + lax.axis_index("row")
    group = chip * groups + col // parts
    part = col % parts
    lens = [lens_ref[group, 0]] + [lens_ref[group, 1 + 2 * part + n] for n in range(2)]
    count = jnp.sum(len_table[...].astype(F32))
    layer = Layer(part, parts, lens, lens_ref.shape[0] * GROUP, count)
    layer.project(xp, xc, w, xo, xt, kv, kvt, qt)
    layer.attend(kv, kvt, qt, att, lse, s_scr, pf_scr)
    layer.middle(xo, tdo, w, vec, att, xb, gw, sm, d_att, delta, dsa, hid, acc, ba)
    layer.attend_back(kv, kvt, qt, lse, delta, d_att, dkvt, dqt, p_scr, ds_scr)
    layer.input_grads(xp, xc, xo, w, dkvt, dqt, dsa, gp, gc, gw, dx, acc)


def run_layer(lengths, xp, xc, tdo, weights, vec, parts):
    nrow, full, width = weights.shape
    own, keys = tdo.shape[2], xp.shape[1] + xc.shape[1]
    heads = full // HD
    vmem = pl.BlockSpec(memory_space=pltpu.VMEM)
    return pl.pallas_call(
        functools.partial(layer_kernel, parts),
        out_shape=(
            jax.ShapeDtypeStruct((2, full, own), BF16),
            jax.ShapeDtypeStruct(xp.shape, BF16),
            jax.ShapeDtypeStruct(xc.shape, BF16),
            jax.ShapeDtypeStruct(weights.shape, BF16),
            jax.ShapeDtypeStruct((1, 8, full), F32),
        ),
        in_specs=[pl.BlockSpec(memory_space=pltpu.SMEM)] + [vmem] * 6,
        out_specs=[vmem] * 5,
        scratch_shapes=[
            pltpu.VMEM((full, own), BF16),
            pltpu.VMEM((keys, full), BF16),
            pltpu.VMEM((keys, nrow * PAIR), BF16),
            pltpu.VMEM((nrow, PAIR, keys), BF16),
            pltpu.VMEM((full, own), BF16),
            pltpu.VMEM((full, own), BF16),
            pltpu.VMEM((heads, own), F32),
            pltpu.VMEM((heads, own), F32),
            pltpu.VMEM((full, own), BF16),
            pltpu.VMEM((nrow, PAIR, keys), BF16),
            pltpu.VMEM((full, own), BF16),
            pltpu.VMEM((2, PROMPT, PAIR), F32),
            pltpu.VMEM((2, PROMPT, PAIR), BF16),
            pltpu.VMEM((2, PROMPT, own), BF16),
            pltpu.VMEM((2, PROMPT, own), BF16),
            pltpu.VMEM((full, own), F32),
            pltpu.VMEM((nrow, own, (width - 4 * BLOCK) // 2), BF16),
            pltpu.VMEM((full, own), F32),
            pltpu.VMEM((full, own), F32),
            pltpu.VMEM((full, keys), F32),
        ],
        compiler_params=pltpu.CompilerParams(vmem_limit_bytes=60 << 20),
        name="layer",
    )(lengths, lengths, xp, xc, tdo, weights, vec)


class Line:
    def __init__(self, c):
        self.c = c
        self.mid = c * (3 - c) // 2 == 1
        self.end = c * (3 - c) // 2 == 0
        inner = c * (3 - c) // 2
        far = 3 * (1 - c // 2)
        one = c - 1 + 2 * ((4 - c) // 4)
        self.near = [c, one, 6 - c - one - far, far]
        self.pass_to = [None, c + 1, c - 1, 3 * (c - 1)]
        last = 1 + c % 2
        second = 6 - c - far - last
        self.far = [far, second, last, c]
        self.sum_to = [last, last + inner * (second - last), last]
        self.slot = [far, second + 4 * inner * (2 - c), last + c // 2 * (4 - last)]


class Traffic:
    def __init__(self, at):
        self.at = at
        self.pending = {}

    def start(self, key, make, cond=None):
        if cond is None:
            make().start()
        else:
            pl.when(cond)(lambda: make().start())
        self.pending[key] = (make, cond)

    def send(self, key, src, dst, send_sem, recv_sem, device, cond=None):
        self.start(key, lambda: remote(src(), dst(), send_sem(), recv_sem(), device), cond)

    def landed(self, dst, recv_sem):
        remote(dst, dst, recv_sem, recv_sem, self.at.sibling).wait_recv()

    def drain(self):
        for make, cond in self.pending.values():
            if cond is None:
                make().wait_send()
            else:
                pl.when(cond)(lambda make=make: make().wait_send())


def at_index(ref, *index):
    return ref.at[index]


class WeightGather:
    def __init__(self, tag, traffic, line, w, cols, feat, sems):
        self.tag, self.t, self.at, self.line = tag, traffic, traffic.at, line
        self.w, self.cols, self.feat = w, cols, feat
        self.col_s, self.col_r, self.one_s, self.one_r, self.two_s, self.two_r, self.sib_s, self.sib_r = sems

    def piece(self, row, c, core):
        half = self.feat // 2
        rows = pl.ds(pl.multiple_of(c * self.feat + core * half, half), half)
        return self.w.at[row, rows, self.cols]

    def move(self, key, row, c, send_sem, recv_sem, device, cond=None):
        here = functools.partial(self.piece, row, c, self.at.dp)
        self.t.send(
            (self.tag,) + key, here, here,
            lambda: at_index(*send_sem), lambda: at_index(*recv_sem), device, cond,
        )

    def own(self):
        at, line = self.at, self.line
        c = line.c
        for i in range(2):
            self.move(
                ("own", i), at.row, c, (self.col_s, i), (self.col_r, c),
                at.col_dev(line.near[1 + i]), line.mid if i else None,
            )
        self.rows(0)

    def rows(self, j):
        at, c = self.at, self.line.near[j]
        self.move(("one", j), at.row, c, (self.one_s, j), (self.one_r, j), at.first_dev)
        self.move(("two", j), at.row, c, (self.two_s, 0, j), (self.two_r, 0, j), at.second_dev)
        if j:
            self.move(("sib", j), at.row, c, (self.sib_s, 0, j), (self.sib_r, 0, j), at.sibling)

    def arrive(self, j):
        at, c = self.at, self.line.near[j]
        self.t.landed(self.piece(at.row, c, at.dp), self.col_r.at[c])
        self.move(
            ("pass", j), at.row, c, (self.col_s, 1 + j), (self.col_r, c),
            at.col_dev(self.line.pass_to[j]), self.line.mid,
        )
        self.rows(j)

    def first(self, j):
        at, c = self.at, self.line.near[j]
        self.t.landed(self.piece(at.first, c, at.dp), self.one_r.at[j])
        self.move(("far", j), at.first, c, (self.two_s, 1, j), (self.two_r, 1, j), at.second_dev)
        self.move(("sib1", j), at.first, c, (self.sib_s, 1, j), (self.sib_r, 1, j), at.sibling)

    def second(self, j):
        at, c = self.at, self.line.near[j]
        for i, row in ((0, at.second), (1, at.both)):
            self.t.landed(self.piece(row, c, at.dp), self.two_r.at[i, j])
            self.move(
                ("sib2", i, j), row, c, (self.sib_s, 2 + i, j), (self.sib_r, 2 + i, j), at.sibling
            )

    def finish(self):
        at = self.at
        for j in range(4):
            c, core = self.line.near[j], 1 - at.dp
            if j:
                self.t.landed(self.piece(at.row, c, core), self.sib_r.at[0, j])
            self.t.landed(self.piece(at.second, c, core), self.sib_r.at[1, j])
            self.t.landed(self.piece(at.first, c, core), self.sib_r.at[2, j])
            self.t.landed(self.piece(at.both, c, core), self.sib_r.at[3, j])


def row_order(row, n):
    return (row % 2 + (3 - n) // 2) % 2 + 2 * ((row // 2 + n + 1) % 2)


class LineSum:
    def __init__(self, tag, traffic, line, out, landing, sems):
        self.tag, self.t, self.line = tag, traffic, line
        self.out, self.landing = out, landing
        self.send_s, self.recv_s = sems

    def move(self, i, cond):
        line = self.line
        self.t.send(
            (self.tag, "col", i, cond is line.mid),
            lambda: self.out.at[i], lambda: self.landing.at[line.slot[i]],
            lambda: self.send_s.at[i], lambda: self.recv_s.at[line.slot[i]],
            self.t.at.col_dev(line.sum_to[i]), cond,
        )

    def put(self, i, value):
        self.out[i] = value.astype(BF16)
        self.move(i, self.line.end)

    def relay(self, i):
        s = self.line.far[i]

        @pl.when(self.line.mid)
        def _():
            self.t.landed(self.landing.at[s], self.recv_s.at[s])
            self.out[i] = self.out[i] + self.landing[s]

        self.move(i, self.line.mid)

    def receive(self, add):
        for slot, cond in ((self.line.c, self.line.c > 0), (4, self.line.c < 3)):

            @pl.when(cond)
            def _(slot=slot):
                self.t.landed(self.landing.at[slot], self.recv_s.at[slot])
                add(self.landing[slot].astype(F32))


class WeightScatter:
    def __init__(self, tag, traffic, line, gw, cols, sib, two, one, zs, zb, out, sems):
        self.tag, self.t, self.at, self.line = tag, traffic, traffic.at, line
        self.gw, self.cols = gw, cols
        self.sib, self.two, self.one, self.out = sib, two, one, out
        self.sib_s, self.sib_r, self.two_s, self.two_r, self.one_s, self.one_r = sems[:6]
        self.fin_s, self.fin_r = sems[8:]
        self.zs, self.zb, self.col_s, self.col_r = zs, zb, sems[6], sems[7]
        self.half = out.shape[0] // 2

    def begin(self, n):
        self.t.send(
            (self.tag, "sib", n),
            lambda: self.gw.at[row_order(self.at.row, n), :, 1 - self.at.dp, :, self.cols],
            lambda: self.sib.at[row_order(self.at.row, n)],
            lambda: self.sib_s.at[n], lambda: self.sib_r.at[n], self.at.sibling,
        )

    def across(self, n, row):
        self.t.send(
            (self.tag, "two", n),
            lambda: self.sib.at[row], lambda: self.two.at[n],
            lambda: self.two_s.at[n], lambda: self.two_r.at[n], self.at.second_dev,
        )

    def merge(self, n):
        r = row_order(self.at.row, n)
        self.t.landed(self.sib.at[r], self.sib_r.at[n])
        for c in range(4):
            here = self.gw[r, c, self.at.dp, :, self.cols]
            self.sib[r, c] = here + self.sib[r, c]
        if n == 0:
            self.across(1, self.at.both)
        if n == 2:
            self.across(0, self.at.second)

    def step2(self):
        self.t.landed(self.two.at[1], self.two_r.at[1])
        for c in range(4):
            self.two[1, c] = self.sib[self.at.first, c] + self.two[1, c]
        self.t.send(
            (self.tag, "one"),
            lambda: self.two.at[1], lambda: self.one,
            lambda: self.one_s, lambda: self.one_r, self.at.first_dev,
        )

    def total(self, c):
        near = self.sib[self.at.row, c].astype(F32) + self.two[0, c].astype(F32)
        return near + self.one[c].astype(F32)

    def step3(self):
        self.t.landed(self.two.at[0], self.two_r.at[0])
        self.t.landed(self.one, self.one_r)
        c = self.line.c
        for i in range(3):
            to = self.line.far[i]
            self.zs[i] = self.total(to).astype(BF16)
            self.t.send(
                (self.tag, "col", i),
                lambda i=i: self.zs.at[i], lambda: self.zb.at[c],
                lambda i=i: self.col_s.at[i], lambda: self.col_r.at[c], self.at.col_dev(to),
            )

    def step4(self):
        mine = pl.ds(pl.multiple_of(self.at.dp * self.half, self.half), self.half)
        total = self.total(self.line.c)
        for s in self.line.near[1:]:
            self.t.landed(self.zb.at[s], self.col_r.at[s])
            total = total + self.zb[s].astype(F32)
        self.out[mine] = total
        self.t.send(
            (self.tag, "fin"),
            lambda: self.out.at[mine], lambda: self.out.at[mine],
            lambda: self.fin_s, lambda: self.fin_r, self.at.sibling,
        )

    def finish(self):
        other = pl.ds(pl.multiple_of((1 - self.at.dp) * self.half, self.half), self.half)
        self.t.landed(self.out.at[other], self.fin_r)


def step_kernel(
    parts, lens_ref, len_table, x_ref, y_hbm, tx_hbm, ty_hbm, wq_ref, wo_ref, wu_ref, wd_ref,
    va_ref, vb_ref, vc_ref, vd_ref,
    xbo, gco, gx_ref, out1, out2, gv_ref,
    y_ref, tx_ref, ty_ref, w, gw, xp, xc, xo, xt, kv, kvt, qt, att, lse, delta, d_att, s_scr, pf_scr, p_scr, ds_scr,
    dsa, hid, acc, ba, dx, tdp, tdo, xb, vrow, gpb, gxz, gcb, sm, smb, smz,
    sib1, two1, one1, zs1, zb1, sib2, two2, one2, zs2, zb2,
    xs, xr, cs, cr, ts, tr, vs, vr, bs, br, gs, gr, ks, kr, ss, sr, zs, zr, ls, *wsems,
):
    ncol = 4
    at = Places(ncol)
    t = Traffic(at)
    c = at.col
    line = Line(c)
    feat = x_ref.shape[0]
    own = xo.shape[1]
    cont = xc.shape[1]
    near, rest = slice(0, 4 * BLOCK), slice(4 * BLOCK, w.shape[2])

    def rows_of(s):
        return pl.ds(pl.multiple_of(s * feat, feat), feat)

    def own_cols(s):
        return pl.ds(pl.multiple_of(s * own, own), own)

    def cont_cols(s, first=0):
        return pl.ds(pl.multiple_of(first + s * cont, cont), cont)

    mine = rows_of(c)
    staged = [
        pltpu.make_async_copy(src, dst, ls.at[i])
        for i, (src, dst) in enumerate(((y_hbm, y_ref), (tx_hbm, tx_ref), (ty_hbm, ty_ref)))
    ]
    for copy in staged:
        copy.start()
    at.meet()
    gather1 = WeightGather("w1", t, line, w, near, feat, wsems[0:8])
    gather2 = WeightGather("w2", t, line, w, rest, feat, wsems[8:16])

    for i in range(3):
        w[at.row, mine, i * BLOCK : (i + 1) * BLOCK] = wq_ref[:, i, :]
    w[at.row, mine, 3 * BLOCK : 4 * BLOCK] = wo_ref[...].T
    gather1.own()
    ff = wu_ref.shape[1]
    w[at.row, mine, 4 * BLOCK : 4 * BLOCK + ff] = wu_ref[...]
    w[at.row, mine, 4 * BLOCK + ff :] = wd_ref[...].T
    gather2.own()
    for i in range(2):
        t.send(
            ("x", i),
            lambda: x_ref.at[:, :PROMPT], lambda: xp.at[mine],
            lambda i=i: xs.at[i], lambda: xr.at[c],
            at.col_dev(line.near[1 + i]), line.mid if i else None,
        )
    local = [
        lambda: pltpu.make_async_copy(x_ref.at[:, :PROMPT], xp.at[mine], ls.at[3]),
        lambda: pltpu.make_async_copy(x_ref.at[:, cont_cols(c, PROMPT)], xc.at[mine], ls.at[4]),
    ]
    for make in local:
        make().start()
    rows = [ref[...].astype(F32).reshape(1, feat) for ref in (va_ref, vb_ref, vc_ref, vd_ref)]
    vrow[c] = jnp.concatenate(rows + rows, axis=0)
    for k in range(1, ncol):
        to = at.ahead(k)
        t.send(
            ("v", k),
            lambda: vrow.at[c], lambda: vrow.at[c],
            lambda k=k: vs.at[k], lambda k=k: vr.at[k], at.col_dev(to),
        )
    pieces = order_pieces(parts)
    for copy in staged:
        copy.wait()
    for to, frm, width in pieces:
        tdp[0, :, to : to + width] = tx_ref[:, frm : frm + width]
        y_here = y_ref[:, frm : frm + width].astype(F32)
        tdp[1, :, to : to + width] = (y_here - ty_ref[:, frm : frm + width].astype(F32)).astype(BF16)

    def x_arrive(j):
        s = line.near[j]
        t.landed(xp.at[rows_of(s)], xr.at[s])
        t.send(
            ("xpass", j),
            lambda: xp.at[rows_of(s)], lambda: xp.at[rows_of(s)],
            lambda: xs.at[1 + j], lambda: xr.at[s],
            at.col_dev(line.pass_to[j]), line.mid,
        )

    gather1.arrive(1)
    gather1.arrive(2)
    gather1.first(0)
    gather2.arrive(1)
    gather2.arrive(2)
    gather2.first(0)
    gather1.arrive(3)
    gather1.first(1)
    gather1.first(2)
    gather2.arrive(3)
    x_arrive(1)
    x_arrive(2)
    for k, to in enumerate(line.near[1:]):
        t.send(
            ("xc", k),
            lambda to=to: x_ref.at[:, cont_cols(to, PROMPT)], lambda: xc.at[mine],
            lambda k=k: cs.at[k], lambda: cr.at[c], at.col_dev(to),
        )
    gather2.first(1)
    gather1.first(3)
    gather2.first(2)
    gather1.second(0)
    gather1.second(1)
    gather1.second(2)
    gather1.second(3)
    x_arrive(3)
    for s in line.near[1:]:
        t.landed(xc.at[rows_of(s)], cr.at[s])
    for make in local:
        make().wait()
    gather1.finish()

    group = at.dp * lax.axis_size("row") + at.row
    lens = [lens_ref[group, 0]] + [lens_ref[group, 1 + 2 * c + n] for n in range(2)]
    count = jnp.sum(len_table[...].astype(F32))
    total_tokens = lens_ref.shape[0] * GROUP
    layer = Layer(c, parts, lens, total_tokens, count, functools.partial(row_order, at.row))
    for k, to in enumerate(line.near[1:]):
        t.send(
            ("td", k),
            lambda to=to: tdp.at[:, :, own_cols(to)], lambda: tdo.at[:, mine],
            lambda k=k: ts.at[k], lambda: tr.at[c], at.col_dev(to),
        )
    tdo[:, mine] = tdp[:, :, own_cols(c)]
    layer.project(xp, xc, w, xo, xt, kv, kvt, qt)


    def forward_steps(r):
        @pl.when(r == 0)
        def _():
            gather2.first(3)

        @pl.when(r == 1)
        def _():
            gather2.second(0)
            gather2.second(1)

        @pl.when(r == 2)
        def _():
            gather2.second(2)

        @pl.when(r == 3)
        def _():
            gather2.second(3)

    layer.attend(kv, kvt, qt, att, lse, s_scr, pf_scr, forward_steps)
    for k in range(1, ncol):
        t.landed(vrow.at[at.behind(k)], vr.at[k])
    gather2.finish()
    vec = jnp.concatenate([vrow[s].T for s in range(ncol)], axis=0)

    def tokens_ready():
        for s in line.near[1:]:
            t.landed(tdo.at[:, rows_of(s)], tr.at[s])

    def outputs_ready():
        for k, to in enumerate(line.near[1:]):
            t.send(
                ("xb", k),
                lambda to=to: xb.at[:, rows_of(to)], lambda: xbo.at[:, :, own_cols(c)],
                lambda k=k: bs.at[k], lambda: br.at[c], at.col_dev(to),
            )
        pltpu.make_async_copy(xb.at[:, mine], xbo.at[:, :, own_cols(c)], ls.at[5]).start()

    scatter1 = WeightScatter(
        "g1", t, line, gw, near, sib1, two1, one1, zs1, zb1, out1, wsems[16:26]
    )
    scatter2 = WeightScatter(
        "g2", t, line, gw, rest, sib2, two2, one2, zs2, zb2, out2, wsems[26:36]
    )
    x_sum = LineSum("gx", t, line, gpb, gxz, (gs, gr))

    def begin_after(scatter, n):
        for i in range(4):
            pl.when(n == i)(lambda i=i: scatter.begin(i))

    def back_done():
        scatter2.merge(0)
        scatter2.merge(1)

    layer.middle(
        xo, tdo, w, vec, att, xb, gw, sm, d_att, delta, dsa, hid, acc, ba,
        tokens_ready, outputs_ready, lambda n: begin_after(scatter2, n), back_done,
    )

    def small_send(i, src, device):
        t.send(
            ("sm", i), src, lambda: smb.at[i], lambda: ss.at[i], lambda: sr.at[i], device
        )

    small_send(0, lambda: sm, at.sibling)
    scatter2.merge(2)
    scatter2.merge(3)

    def back_steps(n):
        begin_after(scatter1, n)

        @pl.when(n == 0)
        def _():
            t.landed(smb.at[0], sr.at[0])
            smb[3] = sm[...] + smb[0]
            small_send(1, lambda: smb.at[3], at.second_dev)

        @pl.when(n == 1)
        def _():
            t.landed(smb.at[1], sr.at[1])
            smb[4] = smb[3] + smb[1]
            small_send(2, lambda: smb.at[4], at.first_dev)
            scatter2.step2()
            scatter1.merge(0)

        @pl.when(n == 2)
        def _():
            t.landed(smb.at[2], sr.at[2])
            smb[5] = smb[4] + smb[2]
            for k in range(1, ncol):
                to = at.ahead(k)
                t.send(
                    ("smz", k),
                    lambda to=to: smb.at[5, to], lambda k=k: smz.at[k],
                    lambda k=k: zs.at[k], lambda k=k: zr.at[k], at.col_dev(to),
                )
            scatter1.merge(1)

        @pl.when(n == 3)
        def _():
            scatter1.merge(2)
            scatter1.step2()

    dx[...] = jnp.zeros_like(dx)
    acc[...] = dsa[...]
    layer.attend_back(
        kv, kvt, qt, lse, delta, d_att, kvt, qt, p_scr, ds_scr, back_steps, (xp, xc, xo, gw),
        (w, dx, acc),
    )

    low, high = layer.own_columns()
    dx[:, low] += acc[:, :BLOCK]
    dx[:, high] += acc[:, BLOCK:PAIR]
    dx[:, PROMPT:] += acc[:, PAIR:]

    def grad_send(i):
        s = line.far[i]
        x_sum.put(i, dx[rows_of(s), :PROMPT])
        gcb[i] = dx[rows_of(s), PROMPT:].astype(BF16)
        t.send(
            ("gc", i),
            lambda: gcb.at[i], lambda: gco.at[c],
            lambda: ks.at[i], lambda: kr.at[c], at.col_dev(s),
        )

    grad_send(0)
    scatter1.merge(3)
    scatter2.step3()
    grad_send(1)
    grad_send(2)
    gx_ref[...] = dx[mine, :PROMPT]
    gcb[3] = dx[mine, PROMPT:].astype(BF16)
    own_copies = [
        pltpu.make_async_copy(xb.at[:, mine], xbo.at[:, :, own_cols(c)], ls.at[5]),
        pltpu.make_async_copy(gcb.at[3], gco.at[c], ls.at[6]),
    ]
    own_copies[1].start()
    x_sum.relay(0)
    scatter1.step3()
    x_sum.relay(1)
    x_sum.relay(2)

    for s in line.near[1:]:
        t.landed(xbo.at[:, :, own_cols(s)], br.at[s])
    scatter2.step4()
    scatter1.step4()
    small = smb[5, c]
    for k in range(1, ncol):
        t.landed(smz.at[k], zr.at[k])
        small = small + smz[k]
    gv_ref[...] = small
    for k in range(1, ncol):
        s = at.behind(k)
        t.landed(gco.at[s], kr.at[s])

    def add_grad(value):
        gx_ref[...] += value

    x_sum.receive(add_grad)
    scatter2.finish()
    scatter1.finish()
    for copy in own_copies:
        copy.wait()
    t.drain()


def order_pieces(parts):
    own, cont = GROUP // parts, NCONT * CONT // parts
    pieces = []
    for p in range(parts):
        pieces.append((p * own, p * BLOCK, BLOCK))
        pieces.append((p * own + BLOCK, (2 * parts - 1 - p) * BLOCK, BLOCK))
        pieces.append((p * own + PAIR, PROMPT + p * cont, cont))
    return pieces


def finish_kernel(
    parts, full, lens_ref, len_table, y_ref, ty_ref, xbo, gco, gp_ref, out1, out2, sums,
    xout_ref, yout_ref, gx_ref, gy_ref, gq_ref, go_ref, gu_ref, gd_ref,
    ga_ref, gb_ref, gc_ref, gd2_ref, loss_ref,
):
    group = lax.axis_index("dp") * lax.axis_size("row") + lax.axis_index("row")
    count = jnp.sum(len_table[...].astype(F32))
    slot = iota((1, CONT), 1)
    live = [(iota((1, PROMPT), 1) < lens_ref[group, 0]).astype(F32)]
    live += [(slot < lens_ref[group, 1 + n]).astype(F32) for n in range(NCONT)]
    weight = jnp.concatenate(live, axis=1) * (lens_ref.shape[0] * GROUP / count)
    for frm, to, width in order_pieces(parts):
        cols = slice(to, to + width)
        xout_ref[:, cols] = xbo[0, :, frm : frm + width]
        branch = xbo[1, :, frm : frm + width].astype(F32)
        y_here = y_ref[:, cols].astype(F32)
        yout_ref[:, cols] = (y_here + branch).astype(BF16)
        gy_ref[:, cols] = (y_here - ty_ref[:, cols].astype(F32) + branch) * weight[:, cols]
    gx_ref[:, :PROMPT] = gp_ref[...]
    cont = gco.shape[2]
    for p in range(parts):
        gx_ref[:, PROMPT + p * cont : PROMPT + (p + 1) * cont] = gco[p].astype(F32)
    ff = gu_ref.shape[1]
    for i in range(3):
        gq_ref[:, i, :] = out1[:, i * BLOCK : (i + 1) * BLOCK]
    go_ref[...] = out1[:, 3 * BLOCK :].T
    gu_ref[...] = out2[:, :ff]
    gd_ref[...] = out2[:, ff:].T
    for i, ref in enumerate((ga_ref, gb_ref, gc_ref, gd2_ref)):
        ref[...] = sums[i : i + 1].reshape(ref.shape)
    loss_ref[...] = sums[4:5, :1] / (2.0 * count * full)


def run_step(lengths, x, y, tx, ty, wq, wo, wu, wd, vecs):
    feat, tokens = x.shape
    full = 4 * feat
    ff = wu.shape[1]
    width = 4 * BLOCK + 2 * ff
    rest = 2 * ff
    half = feat // 2
    own, cont = tokens // 4, NCONT * CONT // 4
    keys = PROMPT + cont
    heads = full // HD
    vmem = pl.BlockSpec(memory_space=pltpu.VMEM)
    dma = pltpu.SemaphoreType.DMA

    def bf(*shape):
        return pltpu.VMEM(shape, BF16)

    def f32(*shape):
        return pltpu.VMEM(shape, F32)

    def reduce_buffers(cols):
        return [
            bf(4, 4, half, cols), bf(2, 4, half, cols), bf(4, half, cols), bf(3, half, cols),
            bf(4, half, cols),
        ]

    gather_sems = [
        dma((5,)), dma((4,)), dma((4,)), dma((4,)), dma((2, 4)), dma((2, 4)), dma((4, 4)), dma((4, 4)),
    ]
    scatter_sems = [
        dma((4,)), dma((4,)), dma((2,)), dma((2,)), dma(()), dma(()), dma((3,)), dma((4,)),
        dma(()), dma(()),
    ]
    sums = (4, 8, feat)
    smem, anywhere = pl.BlockSpec(memory_space=pltpu.SMEM), pl.BlockSpec(memory_space=pl.ANY)

    def shape(*dims, dtype=F32):
        return jax.ShapeDtypeStruct(dims, dtype)

    raw = pl.pallas_call(
        functools.partial(step_kernel, 4),
        out_shape=(
            shape(2, feat, tokens, dtype=BF16), shape(4, feat, cont, dtype=BF16), shape(feat, PROMPT),
            shape(feat, 4 * BLOCK), shape(feat, rest), shape(8, feat),
        ),
        in_specs=[smem, vmem] + [anywhere] * 4 + [vmem] * 8,
        out_specs=[anywhere] * 2 + [vmem] * 4,
        scratch_shapes=[
            bf(feat, tokens), bf(feat, tokens), bf(feat, tokens),
            bf(4, full, width), bf(4, 4, 2, half, width), bf(full, PROMPT), bf(full, cont), bf(full, own),
            bf(keys, full), bf(keys, 4 * PAIR), bf(4, PAIR, keys), bf(full, own), bf(full, own),
            f32(heads, own), f32(heads, own), bf(full, own), f32(2, PROMPT, PAIR), bf(2, PROMPT, PAIR),
            bf(2, PROMPT, own), bf(2, PROMPT, own), f32(full, own), bf(4, own, ff), f32(full, own),
            f32(full, own), f32(full, keys), bf(2, feat, tokens), bf(2, full, own),
            bf(2, full, own), f32(4, 8, feat), bf(3, feat, PROMPT),
            bf(5, feat, PROMPT), bf(4, feat, cont),
            f32(*sums), f32(6, *sums), f32(*sums),
        ]
        + reduce_buffers(4 * BLOCK)
        + reduce_buffers(rest)
        + [
            dma((5,)), dma((4,)), dma((4,)), dma((4,)), dma((4,)), dma((4,)), dma((4,)), dma((4,)),
            dma((4,)), dma((4,)), dma((3,)), dma((5,)), dma((3,)), dma((5,)), dma((3,)), dma((3,)),
            dma((4,)), dma((4,)), dma((7,)),
        ]
        + gather_sems * 2
        + scatter_sems * 2,
        compiler_params=pltpu.CompilerParams(
            collective_id=2, has_side_effects=True, vmem_limit_bytes=61 << 20
        ),
        name="layer_step",
    )(lengths, lengths, x, y, tx, ty, wq, wo, wu, wd, *vecs)
    return pl.pallas_call(
        functools.partial(finish_kernel, 4, full),
        out_shape=(
            shape(feat, tokens, dtype=BF16), shape(feat, tokens, dtype=BF16), shape(feat, tokens),
            shape(feat, tokens), shape(*wq.shape), shape(*wo.shape), shape(*wu.shape),
            shape(*wd.shape), shape(feat), shape(feat), shape(feat), shape(feat), shape(1, 1),
        ),
        in_specs=[smem] + [vmem] * 9,
        out_specs=[vmem] * 13,
        compiler_params=pltpu.CompilerParams(vmem_limit_bytes=61 << 20),
        name="layer_results",
    )(lengths, lengths, y, ty, *raw)


def body(
    x_stream, y_stream, w_qkv, w_out, gain_attn, bias_attn, w_up, w_down, gain_ffn, bias_ffn,
    teach_x, teach_y, lengths,
):
    ncol, nrow = lax.axis_size("col"), lax.axis_size("row")
    feat, tokens = x_stream.shape
    full = feat * ncol
    groups_here = tokens // GROUP
    parts = ncol // groups_here
    assert parts * 2 * BLOCK == PROMPT and nrow == 4
    block = w_qkv.shape[2]
    ff_block = w_up.shape[1]

    if ncol == parts:
        (
            x_out, y_out, grad_x, grad_y, g_q, g_o, g_u, g_d, g_ga, g_ba, g_gf, g_bf, loss,
        ) = run_step(
            lengths, x_stream, y_stream, teach_x, teach_y, w_qkv, w_out, w_up, w_down,
            (gain_attn, bias_attn, gain_ffn, bias_ffn),
        )
        return (
            x_out, y_out, grad_x, grad_y, g_q, g_o, g_ga, g_ba, g_u, g_d, g_gf, g_bf,
            loss.reshape(()),
        )

    y_f32 = y_stream.astype(F32)
    dy = y_f32 - teach_y.astype(F32)
    teach_dy = to_parts(jnp.stack([teach_x, dy.astype(BF16)]), parts)
    packed = jnp.concatenate([w_qkv.reshape(feat, 3 * block), w_out.T, w_up, w_down.T], axis=1)
    small_vecs = jnp.stack([gain_attn, bias_attn, gain_ffn, bias_ffn])
    vecs = lax.all_gather(small_vecs, "col", axis=1, tiled=True)

    x_prompt, x_cont, tdo, weights = gather_all(x_stream, teach_dy, packed, ncol, nrow, parts)

    first = (lax.axis_index("dp") * nrow + lax.axis_index("row")) * groups_here
    count_all = jnp.sum(lengths).astype(F32)
    total_tokens = lengths.shape[0] * GROUP
    vec = jnp.pad(vecs.T, ((0, 0), (0, 124)))
    xb, gp, gc, gw, small = run_layer(lengths, x_prompt, x_cont, tdo, weights, vec, parts)
    lanes = max(feat, 128)
    small = small[0].reshape(8, ncol, feat).transpose(1, 0, 2)
    small = jnp.pad(small, ((0, 0), (0, 0), (0, lanes - feat)))
    xb, gp, gc, gw, sums = scatter_all(xb, gp, gc, gw, small, ncol, parts)

    xb = from_parts(xb, parts)
    branch = xb[1].astype(F32)
    live_all = live_slots(
        lax.dynamic_slice_in_dim(lengths, first, groups_here, 0)
    ).reshape(1, tokens)
    y_out = (y_f32 + branch).astype(BF16)
    grad_y_out = (dy + branch) * (live_all * (total_tokens / count_all))
    gp = jnp.sum(gp.astype(F32), axis=0).reshape(feat, groups_here, PROMPT)
    gc = gc.astype(F32).reshape(feat, groups_here, NCONT * CONT)
    grad_x = jnp.concatenate([gp, gc], axis=2).reshape(feat, tokens)
    loss = sums[4, 0] / (2.0 * count_all * full)
    first_up = 4 * block
    return (
        xb[0],
        y_out,
        grad_x,
        grad_y_out,
        gw[:, : 3 * block].reshape(feat, 3, block),
        gw[:, 3 * block : 4 * block].T,
        sums[0, :feat],
        sums[1, :feat],
        gw[:, first_up : first_up + ff_block],
        gw[:, first_up + ff_block :].T,
        sums[2, :feat],
        sums[3, :feat],
        loss,
    )


def live_slots(lens):
    prompt = jnp.arange(PROMPT, dtype=jnp.int32)[None, :] < lens[:, 0:1]
    cont = jnp.arange(CONT, dtype=jnp.int32)[None, None, :] < lens[:, 1:, None]
    cont = cont.reshape(lens.shape[0], NCONT * CONT)
    return jnp.concatenate([prompt, cont], axis=1).astype(F32)


def solution(mesh):
    stream = P("col", ("dp", "row"))
    up, down = P("col", "row"), P("row", "col")
    qkv, vec = P("col", None, "row"), P("col")
    return jax.shard_map(
        body,
        mesh=mesh,
        in_specs=(
            stream, stream, qkv, down, vec, vec, up, down, vec, vec, stream, stream, P(),
        ),
        out_specs=(
            stream, stream, stream, stream, qkv, down, vec, vec, up, down, vec, vec, P(),
        ),
        check_vma=False,
    )
```
